32 devices in a mesh: tm: 4 (over y, core), agent: 8 (over z, x).
Axes of the slice: x: 2, y: 2, z: 4, core: 2. Of those that a mesh axis runs over, the one named last changes fastest.
Arguments:
- features: bfloat16 [16, 512, 512], P('agent', 'tm'), may hold values from -6 to 6
- norm_gain: float32 [512], replicated, may hold values from 0.1 to 1.9
- w_query: bfloat16 [512, 512], P('agent'), may hold values from -8 to 8
- w_key: bfloat16 [512, 512], P('agent'), may hold values from -8 to 8
- w_value: bfloat16 [512, 512], P('agent'), may hold values from -1 to 1
- w_out: bfloat16 [512, 512], P('agent'), may hold values from -0.5 to 0.5
- tracks: int32 [16, 2], P('agent'), may hold values from 0 to 512, as said below
Outputs:
- mixed_out: bfloat16 [16, 512, 512], P('agent', 'tm')
The draws below stay inside these ranges and needn't reach their ends.
Inputs may be any that keep to these rules, and one draw needn't show every extreme that they name: tracks[a, 0] < 256, tracks[a, 1] - tracks[a, 0] >= 128 unless tracks[a, 1] = 512; some agent spans all 512 steps.
All inputs are finite; a program needn't handle non-finite values.
Results may differ from the reference program's by a relative error of at most 0.0082.
Values may be sent and summed in bfloat16 or wider, within the bound.
No kernel may reach another device: no remote copies, remote signals or barrier semaphores. Data moves between devices by JAX's collectives and lax.ppermute only.
A program may use at most 64 MiB of HBM per device.

```python
import math
import jax
import jax.numpy as jnp
from jax import lax

D = 512
HEADS = 8
AGENTS = 16
STEPS = 512


def shared_base(key):
    return jax.random.normal(jax.random.fold_in(key, 101), (D, D), jnp.float32)


def draw_w_key(key, part):
    return (shared_base(key) / math.sqrt(D)).astype(jnp.bfloat16)


def draw_w_query(key, part):
    independent = jax.random.normal(jax.random.fold_in(key, 303), (D, D), jnp.float32) / math.sqrt(D)
    matrix = independent
    return jnp.clip(matrix, -8.0, 8.0).astype(jnp.bfloat16)


def draw_tracks(key, part):
    first_key = jax.random.fold_in(key, 11)
    span_key = jax.random.fold_in(key, 12)
    full_key = jax.random.fold_in(key, 13)
    starts = jax.random.randint(first_key, (AGENTS,), 0, STEPS // 2, jnp.int32)
    spans = jax.random.randint(span_key, (AGENTS,), max(STEPS // 4, 1), STEPS + 1, jnp.int32)
    ends = jnp.minimum(starts + spans, STEPS)
    chosen = jax.random.randint(full_key, (), 0, AGENTS, jnp.int32)
    index = jnp.arange(AGENTS, dtype=jnp.int32)
    starts = jnp.where(index == chosen, 0, starts)
    ends = jnp.where(index == chosen, STEPS, ends)
    return jnp.stack([starts, ends], axis=1).astype(jnp.int32)


def block_levels(rng, extent, shards, smallest, high):
    level = 1.0
    for dim, shards_of in shards:
        heights = jax.random.uniform(jax.random.fold_in(jax.random.fold_in(rng, 6), dim), (shards_of,), jnp.float32, smallest / len(shards), high / len(shards))
        level = level * jnp.repeat(jnp.exp(heights), extent[dim] // shards_of).reshape((-1,) + (1,) * (len(extent) - 1 - dim))
    return level


def centred(rng, extent, deviation, most, pieces=(), held_as=jnp.bfloat16):
    drawn = deviation * jax.random.normal(rng, extent, jnp.float32)
    if pieces:
        drawn = drawn * block_levels(rng, extent, pieces, -0.22, 0.18)
    return jnp.clip(drawn, -most, most).astype(held_as)


def setup_inputs(seed: int = 0) -> dict:
    key_list = jax.random.split(jax.random.key(seed), 8)
    return {
        "features": centred(key_list[0], (AGENTS, STEPS, D), 1.0, 6.0, ((0, 8), (1, 4))),
        "norm_gain": jnp.clip(1.0 + 0.18 * jax.random.normal(key_list[1], (D,), jnp.float32), 0.1, 1.9),
        "w_query": draw_w_query(jax.random.fold_in(key_list[7], 71), 0),
        "w_key": draw_w_key(jax.random.fold_in(key_list[7], 71), 0),
        "w_value": centred(key_list[4], (D, D), (D // 16) ** -0.5, 1.0, ((0, 8),)),
        "w_out": centred(key_list[5], (D, D), (D // 4) ** -0.5, 0.5, ((0, 8),)),
        "tracks": draw_tracks(jax.random.fold_in(key_list[7], 71), 0),
    }


EPSILON = 1e-05
NEGATIVE = -1e+30

def normalize(inputs, gain):
    values = inputs.astype(jnp.float32)
    meansq = lax.optimization_barrier(jnp.mean(values * values, axis=-1, keepdims=True))
    return (values * lax.rsqrt(meansq + EPSILON) * gain.astype(jnp.float32)).astype(jnp.bfloat16)

def project(normed, weight):
    return jnp.einsum('asd,de->ase', normed.astype(jnp.float32), weight.astype(jnp.float32)).astype(jnp.bfloat16)

def reference(features, norm_gain, w_query, w_key, w_value, w_out, tracks):
    normed = normalize(features, norm_gain)
    queries = project(normed, w_query)
    keys = project(normed, w_key)
    values = project(normed, w_value)
    head_dim = D // HEADS
    scale = 1.0 / math.sqrt(head_dim)
    block = 512 if STEPS % 512 == 0 else STEPS
    positions = jnp.arange(STEPS, dtype=jnp.int32)

    def one_agent(packed):
        query_rows, key_rows, value_rows, track = packed
        query_heads = query_rows.reshape(STEPS, HEADS, head_dim).astype(jnp.float32)
        key_heads = key_rows.reshape(STEPS, HEADS, head_dim).astype(jnp.float32)
        value_heads = value_rows.reshape(STEPS, HEADS, head_dim).astype(jnp.float32)

        def one_block(index):
            query_block = lax.dynamic_slice_in_dim(query_heads, (index * block).astype(jnp.int32), block, 0)
            query_pos = index * block + jnp.arange(block, dtype=jnp.int32)
            scores = jnp.einsum('thd,shd->hts', query_block, key_heads) * scale
            row_live = (query_pos >= track[0]) & (query_pos < track[1])
            allowed = (positions[None, :] >= track[0]) & (positions[None, :] <= query_pos[:, None]) & row_live[:, None]
            masked = jnp.where(allowed[None], scores, NEGATIVE)
            highest = lax.optimization_barrier(jnp.max(masked, axis=-1, keepdims=True))
            weights = jnp.where(allowed[None], jnp.exp(scores - highest), 0.0)
            total = lax.optimization_barrier(jnp.sum(weights, axis=-1))
            rounded = lax.optimization_barrier(weights.astype(jnp.bfloat16)).astype(jnp.float32)
            summed = jnp.einsum('hts,shd->thd', rounded, value_heads)
            denom = jnp.where(row_live[None, :], total, 1.0)
            result = summed / jnp.transpose(denom)[:, :, None] * row_live[:, None, None].astype(jnp.float32)
            return result.reshape(block, D)
        blocks = lax.map(one_block, jnp.arange(STEPS // block, dtype=jnp.int32))
        return blocks.reshape(STEPS, D).astype(jnp.bfloat16)
    attended = lax.map(one_agent, (queries, keys, values, tracks))
    return jnp.einsum('asd,de->aes', attended.astype(jnp.float32), w_out.astype(jnp.float32)).astype(jnp.bfloat16)
```

```python
import functools
import math

import jax
import jax.numpy as jnp
from jax import lax
from jax.experimental import pallas as pl
from jax.experimental.pallas import tpu as pltpu
from jax.sharding import PartitionSpec as P

HEADS = 8


EPSILON = 1e-05
NEGATIVE = -1e30
LANES = 128


def normalize(inputs, gain):
    values = inputs.astype(jnp.float32)
    meansq = jnp.mean(values * values, axis=-1, keepdims=True)
    return (values * lax.rsqrt(meansq + EPSILON) * gain).astype(jnp.bfloat16)


def project(normed, weight):
    return jnp.einsum("asd,de->ase", normed, weight, preferred_element_type=jnp.float32).astype(
        jnp.bfloat16
    )


def body(features, norm_gain, w_query, w_key, w_value, w_out, tracks):
    full_query, full_key, full_value, full_out = (
        lax.all_gather(w_query, "agent", axis=0, tiled=True),
        lax.all_gather(w_key, "agent", axis=0, tiled=True),
        lax.all_gather(w_value, "agent", axis=0, tiled=True),
        lax.all_gather(w_out, "agent", axis=0, tiled=True),
    )
    agents_here, rows_here, width = features.shape
    head_dim = width // HEADS
    scale = 1.0 / math.sqrt(head_dim)
    normed = normalize(features, norm_gain)
    starts = tracks[:, 0]
    ends = tracks[:, 1]
    queries = project(normed, full_query).reshape(agents_here, rows_here, HEADS, head_dim)
    first_row = lax.axis_index("tm") * rows_here
    query_pos = first_row + jnp.arange(rows_here, dtype=jnp.int32)
    row_live = (query_pos[None, :] >= starts[:, None]) & (query_pos[None, :] < ends[:, None])
    initial = (
        jnp.full((agents_here, HEADS, rows_here), NEGATIVE, jnp.float32),
        jnp.zeros((agents_here, HEADS, rows_here), jnp.float32),
        jnp.zeros((agents_here, HEADS, rows_here, head_dim), jnp.float32),
    )

    def attend(carry, key_block, value_block, key_start):
        highest, total, summed = carry
        count = key_block.shape[1]
        key_pos = key_start + jnp.arange(count, dtype=jnp.int32)
        scores = (
            jnp.einsum("athd,ashd->ahts", queries, key_block, preferred_element_type=jnp.float32)
            * scale
        )
        allowed = (
            (key_pos[None, None, :] >= starts[:, None, None])
            & (key_pos[None, None, :] <= query_pos[None, :, None])
            & row_live[:, :, None]
        )
        allowed = allowed[:, None]
        masked = jnp.where(allowed, scores, NEGATIVE)
        new_high = jnp.maximum(highest, jnp.max(masked, axis=-1))
        weights = jnp.where(allowed, jnp.exp(scores - new_high[..., None]), 0.0)
        factor = jnp.exp(highest - new_high)
        total = factor * total + jnp.sum(weights, axis=-1)
        summed = factor[..., None] * summed + jnp.einsum(
            "ahts,ashd->ahtd",
            weights.astype(jnp.bfloat16),
            value_block,
            preferred_element_type=jnp.float32,
        )
        return (new_high, total, summed)

    def sweep(carry, key_rows, value_rows, key_start):
        count = key_rows.shape[1]
        span = 512
        if span == count:
            return attend(carry, key_rows, value_rows, key_start)

        def advance(index, state):
            offset = (index * span).astype(jnp.int32)
            key_block = lax.dynamic_slice_in_dim(key_rows, offset, span, 1)
            value_block = lax.dynamic_slice_in_dim(value_rows, offset, span, 1)
            return attend(state, key_block, value_block, key_start + offset)

        return lax.fori_loop(0, count // span, advance, carry)

    piece = lax.all_gather(normed, "tm", axis=1, tiled=True)
    count = piece.shape[1]
    key_rows = project(piece, full_key).reshape(agents_here, count, HEADS, head_dim)
    value_rows = project(piece, full_value).reshape(agents_here, count, HEADS, head_dim)
    final = sweep(initial, key_rows, value_rows, jnp.int32(0))
    highest, total, summed = final
    denom = jnp.where(row_live[:, None, :], total, 1.0)
    attended = summed / denom[..., None] * row_live[:, None, :, None].astype(jnp.float32)
    attended = (
        jnp.transpose(attended, (0, 2, 1, 3))
        .reshape(agents_here, rows_here, width)
        .astype(jnp.bfloat16)
    )
    projected = jnp.einsum(
        "asd,de->aes", attended, full_out, preferred_element_type=jnp.float32
    ).astype(jnp.bfloat16)
    return lax.all_to_all(projected, "tm", split_axis=1, concat_axis=2, tiled=True)


def attention_kernel(n_tm, n_agent, head_dim, *refs):
    tracks_ref, gain_ref = refs[:2]
    feature_refs = refs[2 : 2 + n_tm]
    weight_refs = refs[2 + n_tm : 2 + n_tm + n_agent]
    out_ref, weights, normed, queries, keys, values = refs[2 + n_tm + n_agent :]
    agents_here, rows_here, width = feature_refs[0].shape
    depth = weight_refs[0].shape[0]
    steps = n_tm * rows_here
    span = out_ref.shape[1]
    block = LANES
    tm = lax.axis_index("tm")
    agent = lax.axis_index("agent")
    for k in range(n_agent):
        weights[pl.ds(pl.multiple_of((agent ^ k) * depth, depth), depth), :] = weight_refs[k][...]
    gain = gain_ref[...]
    for a in range(agents_here):
        for k in range(n_tm):
            rows = pl.ds(pl.multiple_of((tm ^ k) * rows_here, rows_here), rows_here)
            normed[rows, :] = normalize(feature_refs[k][a], gain)
        projected = jnp.dot(normed[...], weights[...], preferred_element_type=jnp.float32)
        scale = 1.0 / math.sqrt(head_dim)
        queries[...] = projected[:, :span].astype(jnp.bfloat16)
        keys[...] = projected[:, span : 2 * span].astype(jnp.bfloat16)
        values[...] = projected[:, 2 * span :].T.astype(jnp.bfloat16)
        start, end = tracks_ref[a, 0], tracks_ref[a, 1]
        lane = lax.broadcasted_iota(jnp.int32, (block, span), 1)
        for j in range(steps // block):
            reach = (j + 1) * block
            key_pos = lax.broadcasted_iota(jnp.int32, (reach, block), 0)
            query_pos = j * block + lax.broadcasted_iota(jnp.int32, (reach, block), 1)
            allowed = (key_pos >= start) & (key_pos <= query_pos)
            column = j * block + lax.broadcasted_iota(jnp.int32, (1, block), 1)
            live = (column >= start) & (column < end)
            query_block = queries[pl.ds(j * block, block), :]
            for h in range(span // head_dim):
                mine = (lane >= h * head_dim) & (lane < (h + 1) * head_dim)
                one = jnp.where(mine, query_block, jnp.zeros_like(query_block))
                scores = lax.dot_general(
                    keys[pl.ds(0, reach), :],
                    one,
                    (((1,), (1,)), ((), ())),
                    preferred_element_type=jnp.float32,
                )
                scores = jnp.where(allowed, scores * scale, NEGATIVE)
                highest = jnp.max(scores, axis=0, keepdims=True)
                weight = jnp.exp(scores - highest)
                total = jnp.sum(weight, axis=0, keepdims=True)
                summed = jnp.dot(
                    values[pl.ds(h * head_dim, head_dim), pl.ds(0, reach)],
                    weight.astype(jnp.bfloat16),
                    preferred_element_type=jnp.float32,
                )
                result = jnp.where(live, summed / total, 0.0)
                out_ref[a, pl.ds(h * head_dim, head_dim), pl.ds(j * block, block)] = result.astype(
                    jnp.bfloat16
                )


def output_kernel(n_tm, n_agent, *refs):
    attended_refs = refs[:n_tm]
    weight_refs = refs[n_tm : n_tm + n_agent]
    out_ref, weights = refs[n_tm + n_agent :]
    depth = weight_refs[0].shape[0]
    agents_here, span, steps = attended_refs[0].shape
    tm = lax.axis_index("tm")
    agent = lax.axis_index("agent")
    for k in range(n_agent):
        weights[pl.ds(pl.multiple_of((agent ^ k) * depth, depth), depth), :] = weight_refs[k][...]
    for a in range(agents_here):
        total = None
        for k in range(n_tm):
            rows = pl.ds(pl.multiple_of((tm ^ k) * span, span), span)
            term = lax.dot_general(
                weights[rows, :],
                attended_refs[k][a],
                (((0,), (0,)), ((), ())),
                preferred_element_type=jnp.float32,
            )
            total = term if total is None else total + term
        out_ref[a] = total.astype(jnp.bfloat16)


def fits(n_tm, n_agent, features):
    agents_here, rows_here, width = features.shape
    head_dim = width // HEADS
    powers = all(n & (n - 1) == 0 for n in (n_tm, n_agent))
    return (
        powers
        and HEADS % n_tm == 0
        and (width // n_tm) % LANES == 0
        and rows_here % LANES == 0
        and width % (16 * n_agent) == 0
        and n_tm * rows_here * width * 2 <= 2**21
    )


def exchange(value, axis, size):
    blocks = [value]
    step = 1
    while step < size:
        pairs = [(i, i ^ step) for i in range(size)]
        blocks += [lax.ppermute(b, axis, pairs) for b in blocks]
        step *= 2
    return blocks


def split_heads(n_tm, n_agent, features, norm_gain, w_query, w_key, w_value, w_out, tracks):
    agents_here, rows_here, width = features.shape
    head_dim = width // HEADS
    span = width // n_tm
    steps = n_tm * rows_here
    tm = lax.axis_index("tm")
    mine = [
        lax.dynamic_slice_in_dim(w, tm * span, span, 1) for w in (w_query, w_key, w_value, w_out)
    ]
    packed = jnp.concatenate(mine[:3], axis=1)
    feature_blocks = exchange(features, "tm", n_tm)
    weight_blocks = [packed] + [
        lax.ppermute(packed, "agent", [(i, i ^ k) for i in range(n_agent)])
        for k in range(1, n_agent)
    ]
    out_blocks = [mine[3]] + [
        lax.ppermute(mine[3], "agent", [(i, i ^ k) for i in range(n_agent)])
        for k in range(1, n_agent)
    ]
    vmem = pl.BlockSpec(memory_space=pltpu.VMEM)
    smem = pl.BlockSpec(memory_space=pltpu.SMEM)
    attended = pl.pallas_call(
        functools.partial(attention_kernel, n_tm, n_agent, head_dim),
        out_shape=jax.ShapeDtypeStruct((agents_here, span, steps), jnp.bfloat16),
        in_specs=[smem] + [vmem] * (1 + n_tm + n_agent),
        out_specs=vmem,
        scratch_shapes=[
            pltpu.VMEM((width, 3 * span), jnp.bfloat16),
            pltpu.VMEM((steps, width), jnp.bfloat16),
            pltpu.VMEM((steps, span), jnp.bfloat16),
            pltpu.VMEM((steps, span), jnp.bfloat16),
            pltpu.VMEM((span, steps), jnp.bfloat16),
        ],
        cost_estimate=pl.CostEstimate(
            flops=agents_here * steps * (6 * width * span + 4 * steps * span),
            bytes_accessed=4 * agents_here * steps * width,
            transcendentals=agents_here * steps * steps,
        ),
        name="attention",
    )(tracks, norm_gain.reshape(1, width), *feature_blocks, *weight_blocks)
    attended_blocks = exchange(attended, "tm", n_tm)
    return pl.pallas_call(
        functools.partial(output_kernel, n_tm, n_agent),
        out_shape=jax.ShapeDtypeStruct((agents_here, span, steps), jnp.bfloat16),
        in_specs=[vmem] * (n_tm + n_agent),
        out_specs=vmem,
        scratch_shapes=[pltpu.VMEM((width, span), jnp.bfloat16)],
        cost_estimate=pl.CostEstimate(
            flops=2 * agents_here * steps * width * span,
            bytes_accessed=4 * agents_here * steps * width,
            transcendentals=0,
        ),
        name="output",
    )(*attended_blocks, *out_blocks)


def solution(mesh):
    in_specs = (
        P("agent", "tm", None),
        P(),
        P("agent", None),
        P("agent", None),
        P("agent", None),
        P("agent", None),
        P("agent", None),
    )
    out_specs = P("agent", "tm", None)
    n_tm, n_agent = mesh.shape["tm"], mesh.shape["agent"]

    def local(features, *rest):
        if fits(n_tm, n_agent, features):
            return split_heads(n_tm, n_agent, features, *rest)
        return body(features, *rest)

    return jax.shard_map(local, mesh=mesh, in_specs=in_specs, out_specs=out_specs, check_vma=False)
```

```python
import functools
import math

import jax
import jax.numpy as jnp
from jax import lax
from jax.experimental import pallas as pl
from jax.experimental.pallas import tpu as pltpu
from jax.sharding import PartitionSpec as P

HEADS = 8


EPSILON = 1e-05
NEGATIVE = -1e30
LANES = 128


def normalize(inputs, gain):
    values = inputs.astype(jnp.float32)
    meansq = jnp.mean(values * values, axis=-1, keepdims=True)
    return (values * lax.rsqrt(meansq + EPSILON) * gain).astype(jnp.bfloat16)


def project(normed, weight):
    return jnp.einsum("asd,de->ase", normed, weight, preferred_element_type=jnp.float32).astype(
        jnp.bfloat16
    )


def body(features, norm_gain, w_query, w_key, w_value, w_out, tracks):
    full_query, full_key, full_value, full_out = (
        lax.all_gather(w_query, "agent", axis=0, tiled=True),
        lax.all_gather(w_key, "agent", axis=0, tiled=True),
        lax.all_gather(w_value, "agent", axis=0, tiled=True),
        lax.all_gather(w_out, "agent", axis=0, tiled=True),
    )
    agents_here, rows_here, width = features.shape
    head_dim = width // HEADS
    scale = 1.0 / math.sqrt(head_dim)
    normed = normalize(features, norm_gain)
    starts = tracks[:, 0]
    ends = tracks[:, 1]
    queries = project(normed, full_query).reshape(agents_here, rows_here, HEADS, head_dim)
    first_row = lax.axis_index("tm") * rows_here
    query_pos = first_row + jnp.arange(rows_here, dtype=jnp.int32)
    row_live = (query_pos[None, :] >= starts[:, None]) & (query_pos[None, :] < ends[:, None])
    initial = (
        jnp.full((agents_here, HEADS, rows_here), NEGATIVE, jnp.float32),
        jnp.zeros((agents_here, HEADS, rows_here), jnp.float32),
        jnp.zeros((agents_here, HEADS, rows_here, head_dim), jnp.float32),
    )

    def attend(carry, key_block, value_block, key_start):
        highest, total, summed = carry
        count = key_block.shape[1]
        key_pos = key_start + jnp.arange(count, dtype=jnp.int32)
        scores = (
            jnp.einsum("athd,ashd->ahts", queries, key_block, preferred_element_type=jnp.float32)
            * scale
        )
        allowed = (
            (key_pos[None, None, :] >= starts[:, None, None])
            & (key_pos[None, None, :] <= query_pos[None, :, None])
            & row_live[:, :, None]
        )
        allowed = allowed[:, None]
        masked = jnp.where(allowed, scores, NEGATIVE)
        new_high = jnp.maximum(highest, jnp.max(masked, axis=-1))
        weights = jnp.where(allowed, jnp.exp(scores - new_high[..., None]), 0.0)
        factor = jnp.exp(highest - new_high)
        total = factor * total + jnp.sum(weights, axis=-1)
        summed = factor[..., None] * summed + jnp.einsum(
            "ahts,ashd->ahtd",
            weights.astype(jnp.bfloat16),
            value_block,
            preferred_element_type=jnp.float32,
        )
        return (new_high, total, summed)

    def sweep(carry, key_rows, value_rows, key_start):
        count = key_rows.shape[1]
        span = 512
        if span == count:
            return attend(carry, key_rows, value_rows, key_start)

        def advance(index, state):
            offset = (index * span).astype(jnp.int32)
            key_block = lax.dynamic_slice_in_dim(key_rows, offset, span, 1)
            value_block = lax.dynamic_slice_in_dim(value_rows, offset, span, 1)
            return attend(state, key_block, value_block, key_start + offset)

        return lax.fori_loop(0, count // span, advance, carry)

    piece = lax.all_gather(normed, "tm", axis=1, tiled=True)
    count = piece.shape[1]
    key_rows = project(piece, full_key).reshape(agents_here, count, HEADS, head_dim)
    value_rows = project(piece, full_value).reshape(agents_here, count, HEADS, head_dim)
    final = sweep(initial, key_rows, value_rows, jnp.int32(0))
    highest, total, summed = final
    denom = jnp.where(row_live[:, None, :], total, 1.0)
    attended = summed / denom[..., None] * row_live[:, None, :, None].astype(jnp.float32)
    attended = (
        jnp.transpose(attended, (0, 2, 1, 3))
        .reshape(agents_here, rows_here, width)
        .astype(jnp.bfloat16)
    )
    projected = jnp.einsum(
        "asd,de->aes", attended, full_out, preferred_element_type=jnp.float32
    ).astype(jnp.bfloat16)
    return lax.all_to_all(projected, "tm", split_axis=1, concat_axis=2, tiled=True)


def attention_kernel(sources, head_dim, *refs):
    tracks_ref, gain_ref = refs[:2]
    feature_refs = refs[2:6]
    weight_refs = refs[6 : 7 + 2 * len(sources)]
    out_ref, out_weights, weights, normed, queries, keys, values = refs[7 + 2 * len(sources) :]
    rows_here, width = feature_refs[0].shape
    depth = weight_refs[0].shape[0]
    span, steps = out_ref.shape
    block = LANES
    tm = lax.axis_index("tm")
    core = tm % 2
    agent = lax.axis_index("agent")

    def place(ref, index):
        rows = pl.ds(pl.multiple_of(index * depth, depth), depth)
        weights[rows, :] = ref[:, : 3 * span]
        out_weights[rows, :] = ref[:, 3 * span :]

    place(weight_refs[0], agent)
    for n, (first, second) in enumerate(sources):
        fetched, swapped = weight_refs[1 + 2 * n], weight_refs[2 + 2 * n]
        for here in (0, 1):
            kept, given = (first, second) if here == 0 else (second, first)

            @pl.when(core == here)
            def _():
                if kept is not None:
                    place(fetched, agent ^ kept)
                if given is not None:
                    place(swapped, agent ^ given)

    gain = gain_ref[...]
    for k in range(4):
        rows = pl.ds(pl.multiple_of((tm ^ k) * rows_here, rows_here), rows_here)
        normed[rows, :] = normalize(feature_refs[k][...], gain)
    scale = 1.0 / math.sqrt(head_dim)
    for n, held in enumerate((queries, keys)):
        held[...] = jnp.dot(
            normed[...], weights[:, n * span : (n + 1) * span], preferred_element_type=jnp.float32
        ).astype(jnp.bfloat16)
    projected = jnp.dot(normed[...], weights[:, 2 * span :], preferred_element_type=jnp.float32)
    values[...] = projected.T.astype(jnp.bfloat16)
    start, end = tracks_ref[core, 0], tracks_ref[core, 1]
    lane = lax.broadcasted_iota(jnp.int32, (block, LANES), 1)
    for j in range(steps // block):
        reach = (j + 1) * block
        key_pos = lax.broadcasted_iota(jnp.int32, (reach, block), 0)
        query_pos = j * block + lax.broadcasted_iota(jnp.int32, (reach, block), 1)
        allowed = (key_pos >= start) & (key_pos <= query_pos)
        column = j * block + lax.broadcasted_iota(jnp.int32, (1, block), 1)
        live = (column >= start) & (column < end)
        for h in range(span // head_dim):
            low = h * head_dim // LANES * LANES
            mine = (lane >= h * head_dim - low) & (lane < (h + 1) * head_dim - low)
            query_block = queries[pl.ds(j * block, block), pl.ds(low, LANES)]
            one = jnp.where(mine, query_block, jnp.zeros_like(query_block))
            scores = lax.dot_general(
                keys[pl.ds(0, reach), pl.ds(low, LANES)],
                one,
                (((1,), (1,)), ((), ())),
                preferred_element_type=jnp.float32,
            )
            scores = jnp.where(allowed, scores * scale, NEGATIVE)
            highest = jnp.max(scores, axis=0, keepdims=True)
            weight = jnp.exp(scores - highest)
            total = jnp.sum(weight, axis=0, keepdims=True)
            summed = jnp.dot(
                values[pl.ds(h * head_dim, head_dim), pl.ds(0, reach)],
                weight.astype(jnp.bfloat16),
                preferred_element_type=jnp.float32,
            )
            result = jnp.where(live, summed / total, 0.0)
            out_ref[pl.ds(h * head_dim, head_dim), pl.ds(j * block, block)] = result.astype(
                jnp.bfloat16
            )


def output_kernel(mine_ref, other_ref, weights_ref, out_ref):
    span, steps = mine_ref.shape
    y = lax.axis_index("tm") // 2
    total = None
    for k, ref in enumerate((mine_ref, other_ref)):
        rows = pl.ds(pl.multiple_of((y ^ k) * span, span), span)
        term = lax.dot_general(
            weights_ref[rows, :],
            ref[...],
            (((0,), (0,)), ((), ())),
            preferred_element_type=jnp.float32,
        )
        total = term if total is None else total + term
    out_ref[...] = total.astype(jnp.bfloat16).reshape(out_ref.shape)


def fits(n_tm, n_agent, features):
    agents_here, rows_here, width = features.shape
    return (
        n_tm == 4
        and n_agent & (n_agent - 1) == 0
        and agents_here == 2
        and width // 2 % LANES == 0
        and HEADS % 2 == 0
        and LANES % (width // HEADS) == 0
        and rows_here % LANES == 0
        and width % (16 * n_agent) == 0
        and n_tm * rows_here * width <= 2**20
    )


def split_heads(n_tm, n_agent, features, norm_gain, w_query, w_key, w_value, w_out, tracks):
    agents_here, rows_here, width = features.shape
    head_dim = width // HEADS
    span = width // 2
    steps = n_tm * rows_here
    tm = lax.axis_index("tm")
    core, y = tm % 2, tm // 2

    def across(value):
        return lax.ppermute(value, "tm", [(i, i ^ 2) for i in range(n_tm)])

    def swap(value):
        return lax.ppermute(value, "tm", [(i, i ^ 1) for i in range(n_tm)])

    def fetch(value, offsets):
        pairs = [
            (t * n_agent + (a ^ offsets[t % 2]), t * n_agent + a)
            for t in range(n_tm)
            for a in range(n_agent)
            if offsets[t % 2] is not None
        ]
        return lax.ppermute(value, ("tm", "agent"), pairs)

    other_rows = across(features)
    packed = jnp.concatenate(
        [lax.dynamic_slice_in_dim(w, y * span, span, 1) for w in (w_query, w_key, w_value, w_out)],
        axis=1,
    )
    far = list(range(n_agent - 1, 0, -1))
    firsts, seconds = [k for k in far if k % 2 == 0], [k for k in far if k % 2 == 1]
    sources = [
        (firsts[n] if n < len(firsts) else None, seconds[n]) for n in range(len(seconds))
    ]
    fetched = [fetch(packed, pair) for pair in sources]
    own, given = features[core], features[1 - core]
    beside = swap(given)
    swapped = [swap(f) for f in fetched]
    diagonal = swap(other_rows[1 - core])
    feature_blocks = [own, beside, other_rows[core], diagonal]
    weight_blocks = [packed] + [b for pair in zip(fetched, swapped) for b in pair]
    vmem = pl.BlockSpec(memory_space=pltpu.VMEM)
    smem = pl.BlockSpec(memory_space=pltpu.SMEM)
    attended, out_weights = pl.pallas_call(
        functools.partial(attention_kernel, sources, head_dim),
        out_shape=(
            jax.ShapeDtypeStruct((span, steps), jnp.bfloat16),
            jax.ShapeDtypeStruct((width, span), jnp.bfloat16),
        ),
        in_specs=[smem] + [vmem] * (1 + len(feature_blocks) + len(weight_blocks)),
        out_specs=(vmem, vmem),
        scratch_shapes=[
            pltpu.VMEM((width, 3 * span), jnp.bfloat16),
            pltpu.VMEM((steps, width), jnp.bfloat16),
            pltpu.VMEM((steps, span), jnp.bfloat16),
            pltpu.VMEM((steps, span), jnp.bfloat16),
            pltpu.VMEM((span, steps), jnp.bfloat16),
        ],
        compiler_params=pltpu.CompilerParams(vmem_limit_bytes=24 * 2**20),
        cost_estimate=pl.CostEstimate(
            flops=steps * (6 * width * span + 4 * steps * span),
            bytes_accessed=4 * steps * width,
            transcendentals=steps * steps * (span // head_dim),
        ),
        name="attention",
    )(tracks, norm_gain.reshape(1, width), *feature_blocks, *weight_blocks)
    channels = pl.pallas_call(
        output_kernel,
        out_shape=jax.ShapeDtypeStruct((2, span // 2, steps), jnp.bfloat16),
        in_specs=[vmem] * 3,
        out_specs=vmem,
        compiler_params=pltpu.CompilerParams(vmem_limit_bytes=24 * 2**20),
        cost_estimate=pl.CostEstimate(
            flops=2 * steps * width * span,
            bytes_accessed=6 * steps * width,
            transcendentals=0,
        ),
        name="output",
    )(attended, across(attended), out_weights)
    kept, received = channels[core], swap(channels[1 - core])
    return jnp.where(core == 0, jnp.stack([kept, received]), jnp.stack([received, kept]))


def solution(mesh):
    in_specs = (
        P("agent", "tm", None),
        P(),
        P("agent", None),
        P("agent", None),
        P("agent", None),
        P("agent", None),
        P("agent", None),
    )
    out_specs = P("agent", "tm", None)
    n_tm, n_agent = mesh.shape["tm"], mesh.shape["agent"]

    def local(features, *rest):
        if fits(n_tm, n_agent, features):
            return split_heads(n_tm, n_agent, features, *rest)
        return body(features, *rest)

    return jax.shard_map(local, mesh=mesh, in_specs=in_specs, out_specs=out_specs, check_vma=False)
```

```python
import functools
import math

import jax
import jax.numpy as jnp
from jax import lax
from jax.experimental import pallas as pl
from jax.experimental.pallas import tpu as pltpu
from jax.sharding import PartitionSpec as P


HEADS = 8


EPSILON = 1e-05
NEGATIVE = -1e30
LANES = 128


def normalize(inputs, gain):
    values = inputs.astype(jnp.float32)
    meansq = jnp.mean(values * values, axis=-1, keepdims=True)
    return (values * lax.rsqrt(meansq + EPSILON) * gain).astype(jnp.bfloat16)


def project(normed, weight):
    return jnp.einsum("asd,de->ase", normed, weight, preferred_element_type=jnp.float32).astype(
        jnp.bfloat16
    )


def body(features, norm_gain, w_query, w_key, w_value, w_out, tracks):
    full_query, full_key, full_value, full_out = (
        lax.all_gather(w_query, "agent", axis=0, tiled=True),
        lax.all_gather(w_key, "agent", axis=0, tiled=True),
        lax.all_gather(w_value, "agent", axis=0, tiled=True),
        lax.all_gather(w_out, "agent", axis=0, tiled=True),
    )
    agents_here, rows_here, width = features.shape
    head_dim = width // HEADS
    scale = 1.0 / math.sqrt(head_dim)
    normed = normalize(features, norm_gain)
    starts = tracks[:, 0]
    ends = tracks[:, 1]
    queries = project(normed, full_query).reshape(agents_here, rows_here, HEADS, head_dim)
    first_row = lax.axis_index("tm") * rows_here
    query_pos = first_row + jnp.arange(rows_here, dtype=jnp.int32)
    row_live = (query_pos[None, :] >= starts[:, None]) & (query_pos[None, :] < ends[:, None])
    initial = (
        jnp.full((agents_here, HEADS, rows_here), NEGATIVE, jnp.float32),
        jnp.zeros((agents_here, HEADS, rows_here), jnp.float32),
        jnp.zeros((agents_here, HEADS, rows_here, head_dim), jnp.float32),
    )

    def attend(carry, key_block, value_block, key_start):
        highest, total, summed = carry
        count = key_block.shape[1]
        key_pos = key_start + jnp.arange(count, dtype=jnp.int32)
        scores = (
            jnp.einsum("athd,ashd->ahts", queries, key_block, preferred_element_type=jnp.float32)
            * scale
        )
        allowed = (
            (key_pos[None, None, :] >= starts[:, None, None])
            & (key_pos[None, None, :] <= query_pos[None, :, None])
            & row_live[:, :, None]
        )
        allowed = allowed[:, None]
        masked = jnp.where(allowed, scores, NEGATIVE)
        new_high = jnp.maximum(highest, jnp.max(masked, axis=-1))
        weights = jnp.where(allowed, jnp.exp(scores - new_high[..., None]), 0.0)
        factor = jnp.exp(highest - new_high)
        total = factor * total + jnp.sum(weights, axis=-1)
        summed = factor[..., None] * summed + jnp.einsum(
            "ahts,ashd->ahtd",
            weights.astype(jnp.bfloat16),
            value_block,
            preferred_element_type=jnp.float32,
        )
        return (new_high, total, summed)

    def sweep(carry, key_rows, value_rows, key_start):
        count = key_rows.shape[1]
        span = 512
        if span == count:
            return attend(carry, key_rows, value_rows, key_start)

        def advance(index, state):
            offset = (index * span).astype(jnp.int32)
            key_block = lax.dynamic_slice_in_dim(key_rows, offset, span, 1)
            value_block = lax.dynamic_slice_in_dim(value_rows, offset, span, 1)
            return attend(state, key_block, value_block, key_start + offset)

        return lax.fori_loop(0, count // span, advance, carry)

    piece = lax.all_gather(normed, "tm", axis=1, tiled=True)
    count = piece.shape[1]
    key_rows = project(piece, full_key).reshape(agents_here, count, HEADS, head_dim)
    value_rows = project(piece, full_value).reshape(agents_here, count, HEADS, head_dim)
    final = sweep(initial, key_rows, value_rows, jnp.int32(0))
    _, total, summed = final
    denom = jnp.where(row_live[:, None, :], total, 1.0)
    attended = summed / denom[..., None] * row_live[:, None, :, None].astype(jnp.float32)
    attended = (
        jnp.transpose(attended, (0, 2, 1, 3))
        .reshape(agents_here, rows_here, width)
        .astype(jnp.bfloat16)
    )
    projected = jnp.einsum(
        "asd,de->aes", attended, full_out, preferred_element_type=jnp.float32
    ).astype(jnp.bfloat16)
    return lax.all_to_all(projected, "tm", split_axis=1, concat_axis=2, tiled=True)


def params():
    return pltpu.CompilerParams(vmem_limit_bytes=24 * 2**20)


def cost(flops, transcendentals=0, bytes_accessed=2**20):
    return pl.CostEstimate(
        flops=flops, transcendentals=transcendentals, bytes_accessed=bytes_accessed
    )


def norm_kernel(tracks_ref, gain_ref, mine_ref, beside_ref, other_ref, diagonal_ref, *outs):
    normed_ref, bounds_ref = outs
    rows_here = mine_ref.shape[1]
    tm = lax.axis_index("tm")
    core = tm % 2
    gain = gain_ref[...]
    for k, ref in enumerate((mine_ref, beside_ref, other_ref, diagonal_ref)):
        rows = pl.ds(pl.multiple_of((tm ^ k) * rows_here, rows_here), rows_here)
        normed_ref[rows, :] = normalize(ref[core], gain)
    for n in range(2):
        bounds_ref[n] = jnp.full(bounds_ref.shape[1:], tracks_ref[core, n], jnp.int32)


def attend(bounds_ref, queries, keys, values, out_ref, head_dim):
    span, steps = out_ref.shape
    block = LANES
    scale = 1.0 / math.sqrt(head_dim)
    start, end = bounds_ref[0, :1, :block], bounds_ref[1, :1, :block]
    lane = lax.broadcasted_iota(jnp.int32, (block, span), 1)
    for j in range(steps // block):
        reach = (j + 1) * block
        key_pos = lax.broadcasted_iota(jnp.int32, (reach, block), 0)
        query_pos = j * block + lax.broadcasted_iota(jnp.int32, (reach, block), 1)
        allowed = (key_pos >= start) & (key_pos <= query_pos)
        column = j * block + lax.broadcasted_iota(jnp.int32, (1, block), 1)
        live = (column >= start) & (column < end)
        query_block = queries[pl.ds(j * block, block), :]
        for h in range(span // head_dim):
            mine = (lane >= h * head_dim) & (lane < (h + 1) * head_dim)
            one = jnp.where(mine, query_block, jnp.zeros_like(query_block))
            scores = lax.dot_general(
                keys[pl.ds(0, reach), :],
                one,
                (((1,), (1,)), ((), ())),
                preferred_element_type=jnp.float32,
            )
            scores = jnp.where(allowed, scores * scale, NEGATIVE)
            highest = jnp.max(scores, axis=0, keepdims=True)
            weight = jnp.exp(scores - highest)
            total = jnp.sum(weight, axis=0, keepdims=True)
            summed = jnp.dot(
                values[pl.ds(h * head_dim, head_dim), pl.ds(0, reach)],
                weight.astype(jnp.bfloat16),
                preferred_element_type=jnp.float32,
            )
            result = jnp.where(live, summed / total, 0.0)
            out_ref[pl.ds(h * head_dim, head_dim), pl.ds(j * block, block)] = result.astype(
                jnp.bfloat16
            )


def place(sources, refs, target, begin, columns):
    depth = refs[0].shape[0]
    agent = lax.axis_index("agent")
    core = lax.axis_index("tm") % 2

    def put(ref, index):
        rows = pl.ds(pl.multiple_of(index * depth, depth), depth)
        low = min(begin, ref.shape[1] - columns)
        target[rows, :] = ref[:, low : low + columns]

    put(refs[0], agent)
    for n, pair in enumerate(sources):
        for here in (0, 1):
            for ref, offset in zip(refs[1 + 2 * n : 3 + 2 * n], (pair[here], pair[1 - here])):
                if offset is not None:
                    pl.when(core == here)(functools.partial(put, ref, agent ^ offset))


def first_kernel(sources, head_dim, bounds_ref, normed_ref, *refs):
    shards, refs = refs[: 1 + 2 * len(sources)], refs[1 + 2 * len(sources) :]
    out_ref, late, weights, held = refs[0], refs[1:4], refs[4], refs[5:]
    _, columns = weights.shape
    span = columns // 3
    place(sources, shards, weights, 0, columns)
    for n in range(3):
        full = jnp.dot(
            normed_ref[...], weights[:, n * span : (n + 1) * span], preferred_element_type=jnp.float32
        )
        for m, target in enumerate((held[n], late[n])):
            part = full[:, m * LANES : (m + 1) * LANES]
            target[...] = (part.T if n == 2 else part).astype(jnp.bfloat16)
    attend(bounds_ref, *held, out_ref, head_dim)


def second_kernel(head_dim, bounds_ref, queries, keys, values, out_ref):
    attend(bounds_ref, queries, keys, values, out_ref, head_dim)


def transposed_dot(weight, value):
    return lax.dot_general(
        weight, value, (((0,), (0,)), ((), ())), preferred_element_type=jnp.float32
    )


def partial_kernel(sources, *refs):
    shards, refs = refs[: 1 + 2 * len(sources)], refs[1 + 2 * len(sources) :]
    here, kept_ref, given_ref, kept_weights, given_weights, weights = (
        refs[:3],
        *refs[3:7],
        refs[7],
    )
    _, columns = weights.shape
    half = columns // 2
    core, y = lax.axis_index("tm") % 2, lax.axis_index("tm") // 2
    place(sources, shards, weights, 3 * columns, columns)
    for n, (ref, last) in enumerate(((kept_ref, kept_weights), (given_ref, given_weights))):
        lanes = pl.ds(pl.multiple_of((core ^ n) * half, half), half)
        total = None
        for m, value in enumerate(here):
            first = ((y ^ (m // 2)) * 2 + m % 2) * LANES
            rows = pl.ds(pl.multiple_of(first, LANES), LANES)
            term = transposed_dot(weights[rows, lanes], value[...])
            total = term if total is None else total + term
        ref[...] = total
        last[...] = weights[pl.ds(pl.multiple_of(((y ^ 1) * 2 + 1) * LANES, LANES), LANES), lanes]


def given_kernel(partial_ref, weights_ref, value_ref, out_ref):
    out_ref[...] = (partial_ref[...] + transposed_dot(weights_ref[...], value_ref[...])).astype(
        jnp.bfloat16
    )


def final_kernel(partial_ref, weights_ref, value_ref, received_ref, out_ref):
    core = lax.axis_index("tm") % 2
    out_ref[1 - core] = received_ref[...]
    out_ref[core] = (partial_ref[...] + transposed_dot(weights_ref[...], value_ref[...])).astype(
        jnp.bfloat16
    )


def fits(n_tm, n_agent, features):
    agents_here, rows_here, width = features.shape
    return (
        n_tm == 4
        and n_agent >= 4
        and n_agent & (n_agent - 1) == 0
        and agents_here == 2
        and width == 4 * LANES
        and LANES % (width // HEADS) == 0
        and rows_here % LANES == 0
        and width % (16 * n_agent) == 0
        and n_tm * rows_here * width <= 2**20
    )


def split_heads(n_tm, n_agent, features, norm_gain, w_query, w_key, w_value, w_out, tracks):
    _, rows_here, width = features.shape
    head_dim = width // HEADS
    span = width // 2
    steps = n_tm * rows_here
    y = lax.axis_index("tm") // 2

    def across(value):
        return lax.ppermute(value, "tm", [(i, i ^ 2) for i in range(n_tm)])

    def swap(value):
        return lax.ppermute(value, "tm", [(i, i ^ 1) for i in range(n_tm)])

    def fetch(value, offsets):
        pairs = [
            (t * n_agent + (a ^ offsets[t % 2]), t * n_agent + a)
            for t in range(n_tm)
            for a in range(n_agent)
            if offsets[t % 2] is not None
        ]
        return lax.ppermute(value, ("tm", "agent"), pairs)

    def kernel(body, outs, args, scratch=(), smem=0, **estimate):
        vmem = pl.BlockSpec(memory_space=pltpu.VMEM)
        out = pl.pallas_call(
            body,
            out_shape=[jax.ShapeDtypeStruct(shape, dtype) for shape, dtype in outs],
            in_specs=[pl.BlockSpec(memory_space=pltpu.SMEM)] * smem + [vmem] * (len(args) - smem),
            out_specs=[vmem] * len(outs),
            scratch_shapes=[pltpu.VMEM(shape, dtype) for shape, dtype in scratch],
            compiler_params=params(),
            cost_estimate=cost(**estimate),
        )(*args)
        return out

    half, full = jnp.bfloat16, jnp.float32
    pieces = [
        lax.dynamic_slice_in_dim(w, y * span, span, 1) for w in (w_query, w_key, w_value, w_out)
    ]
    packed, projections, outward = jnp.concatenate(pieces, 1), jnp.concatenate(pieces[:3], 1), pieces[3]
    evens = list(range(n_agent - 2, 0, -2))
    odds = list(range(n_agent - 1, 0, -2))
    sources = list(zip(evens + [None], odds))
    near = len(sources) - 2
    fetched = [fetch(projections if n < near else packed, pair) for n, pair in enumerate(sources)]
    fetched_out = [fetch(outward, pair) for pair in sources[:near]]
    other_rows = across(features)
    beside = swap(features)
    diagonal = swap(other_rows)
    swapped = [swap(value) for value in fetched]
    swapped_out = [swap(value) for value in fetched_out]
    normed, bounds = kernel(
        norm_kernel,
        [((steps, width), half), ((2, 8, LANES), jnp.int32)],
        (tracks, norm_gain.reshape(1, width), features, beside, other_rows, diagonal),
        smem=1,
        flops=8 * steps * width,
    )
    shards = [packed] + [v for pair in zip(fetched, swapped) for v in pair]
    head_flops = 4 * steps * steps * LANES
    heads = [((steps, LANES), half)] * 2 + [((LANES, steps), half)]
    exponentials = steps * steps * LANES // head_dim
    attended_first, *late = kernel(
        functools.partial(first_kernel, sources, head_dim),
        [((LANES, steps), half)] + heads,
        (bounds, normed, *shards),
        scratch=[((width, 3 * span), half)] + heads,
        flops=6 * steps * width * span + head_flops,
        transcendentals=exponentials,
    )
    other_first = across(attended_first)
    (attended_second,) = kernel(
        functools.partial(second_kernel, head_dim),
        [((LANES, steps), half)],
        (bounds, *late),
        flops=head_flops,
        transcendentals=exponentials,
    )
    other_second = across(attended_second)
    out_shards = [packed] + [
        v
        for pair in zip(fetched_out + fetched[near:], swapped_out + swapped[near:])
        for v in pair
    ]
    kept, given, kept_weights, given_weights = kernel(
        functools.partial(partial_kernel, sources),
        [((span // 2, steps), full)] * 2 + [((LANES, span // 2), half)] * 2,
        (*out_shards, attended_first, attended_second, other_first),
        scratch=[((width, span), half)],
        flops=2 * steps * width * span,
    )
    (given,) = kernel(
        given_kernel,
        [((span // 2, steps), half)],
        (given, given_weights, other_second),
        flops=steps * LANES * span,
    )
    received = swap(given)
    (out,) = kernel(
        final_kernel,
        [((2, span // 2, steps), half)],
        (kept, kept_weights, other_second, received),
        flops=steps * LANES * span,
    )
    return out


def solution(mesh):
    in_specs = (
        P("agent", "tm", None),
        P(),
        P("agent", None),
        P("agent", None),
        P("agent", None),
        P("agent", None),
        P("agent", None),
    )
    out_specs = P("agent", "tm", None)
    n_tm, n_agent = mesh.shape["tm"], mesh.shape["agent"]

    def local(features, *rest):
        if fits(n_tm, n_agent, features):
            return split_heads(n_tm, n_agent, features, *rest)
        return body(features, *rest)

    return jax.shard_map(local, mesh=mesh, in_specs=in_specs, out_specs=out_specs, check_vma=False)
```

```python
import functools
import math

import jax
import jax.numpy as jnp
from jax import lax
from jax.experimental import pallas as pl
from jax.experimental.pallas import tpu as pltpu
from jax.sharding import PartitionSpec as P


HEADS = 8


EPSILON = 1e-05
NEGATIVE = -1e30
LANES = 128


def normalize(inputs, gain):
    values = inputs.astype(jnp.float32)
    meansq = jnp.mean(values * values, axis=-1, keepdims=True)
    return (values * lax.rsqrt(meansq + EPSILON) * gain).astype(jnp.bfloat16)


def project(normed, weight):
    return jnp.einsum("asd,de->ase", normed, weight, preferred_element_type=jnp.float32).astype(
        jnp.bfloat16
    )


def body(features, norm_gain, w_query, w_key, w_value, w_out, tracks):
    full_query, full_key, full_value, full_out = (
        lax.all_gather(w_query, "agent", axis=0, tiled=True),
        lax.all_gather(w_key, "agent", axis=0, tiled=True),
        lax.all_gather(w_value, "agent", axis=0, tiled=True),
        lax.all_gather(w_out, "agent", axis=0, tiled=True),
    )
    agents_here, rows_here, width = features.shape
    head_dim = width // HEADS
    scale = 1.0 / math.sqrt(head_dim)
    normed = normalize(features, norm_gain)
    starts = tracks[:, 0]
    ends = tracks[:, 1]
    queries = project(normed, full_query).reshape(agents_here, rows_here, HEADS, head_dim)
    first_row = lax.axis_index("tm") * rows_here
    query_pos = first_row + jnp.arange(rows_here, dtype=jnp.int32)
    row_live = (query_pos[None, :] >= starts[:, None]) & (query_pos[None, :] < ends[:, None])
    initial = (
        jnp.full((agents_here, HEADS, rows_here), NEGATIVE, jnp.float32),
        jnp.zeros((agents_here, HEADS, rows_here), jnp.float32),
        jnp.zeros((agents_here, HEADS, rows_here, head_dim), jnp.float32),
    )

    def attend(carry, key_block, value_block, key_start):
        highest, total, summed = carry
        count = key_block.shape[1]
        key_pos = key_start + jnp.arange(count, dtype=jnp.int32)
        scores = (
            jnp.einsum("athd,ashd->ahts", queries, key_block, preferred_element_type=jnp.float32)
            * scale
        )
        allowed = (
            (key_pos[None, None, :] >= starts[:, None, None])
            & (key_pos[None, None, :] <= query_pos[None, :, None])
            & row_live[:, :, None]
        )
        allowed = allowed[:, None]
        masked = jnp.where(allowed, scores, NEGATIVE)
        new_high = jnp.maximum(highest, jnp.max(masked, axis=-1))
        weights = jnp.where(allowed, jnp.exp(scores - new_high[..., None]), 0.0)
        factor = jnp.exp(highest - new_high)
        total = factor * total + jnp.sum(weights, axis=-1)
        summed = factor[..., None] * summed + jnp.einsum(
            "ahts,ashd->ahtd",
            weights.astype(jnp.bfloat16),
            value_block,
            preferred_element_type=jnp.float32,
        )
        return (new_high, total, summed)

    def sweep(carry, key_rows, value_rows, key_start):
        count = key_rows.shape[1]
        span = 512
        if span == count:
            return attend(carry, key_rows, value_rows, key_start)

        def advance(index, state):
            offset = (index * span).astype(jnp.int32)
            key_block = lax.dynamic_slice_in_dim(key_rows, offset, span, 1)
            value_block = lax.dynamic_slice_in_dim(value_rows, offset, span, 1)
            return attend(state, key_block, value_block, key_start + offset)

        return lax.fori_loop(0, count // span, advance, carry)

    piece = lax.all_gather(normed, "tm", axis=1, tiled=True)
    count = piece.shape[1]
    key_rows = project(piece, full_key).reshape(agents_here, count, HEADS, head_dim)
    value_rows = project(piece, full_value).reshape(agents_here, count, HEADS, head_dim)
    final = sweep(initial, key_rows, value_rows, jnp.int32(0))
    _, total, summed = final
    denom = jnp.where(row_live[:, None, :], total, 1.0)
    attended = summed / denom[..., None] * row_live[:, None, :, None].astype(jnp.float32)
    attended = (
        jnp.transpose(attended, (0, 2, 1, 3))
        .reshape(agents_here, rows_here, width)
        .astype(jnp.bfloat16)
    )
    projected = jnp.einsum(
        "asd,de->aes", attended, full_out, preferred_element_type=jnp.float32
    ).astype(jnp.bfloat16)
    return lax.all_to_all(projected, "tm", split_axis=1, concat_axis=2, tiled=True)


def params():
    return pltpu.CompilerParams(vmem_limit_bytes=24 * 2**20)


def cost(flops, transcendentals=0, bytes_accessed=2**20):
    return pl.CostEstimate(
        flops=flops, transcendentals=transcendentals, bytes_accessed=bytes_accessed
    )


def norm_kernel(tracks_ref, gain_ref, mine_ref, beside_ref, other_ref, diagonal_ref, *outs):
    normed_ref, bounds_ref = outs
    rows_here = mine_ref.shape[1]
    tm = lax.axis_index("tm")
    core = tm % 2
    gain = gain_ref[...]
    for k, ref in enumerate((mine_ref, beside_ref, other_ref, diagonal_ref)):
        rows = pl.ds(pl.multiple_of((tm ^ k) * rows_here, rows_here), rows_here)
        normed_ref[rows, :] = normalize(ref[core], gain)
    for n in range(2):
        bounds_ref[n] = jnp.full(bounds_ref.shape[1:], tracks_ref[core, n], jnp.int32)


def attend(bounds_ref, queries, keys, values, out_ref, head_dim):
    span, steps = out_ref.shape
    block = LANES
    scale = 1.0 / math.sqrt(head_dim)
    start, end = bounds_ref[0, :1, :block], bounds_ref[1, :1, :block]
    lane = lax.broadcasted_iota(jnp.int32, (block, span), 1)
    for j in range(steps // block):
        reach = (j + 1) * block
        key_pos = lax.broadcasted_iota(jnp.int32, (reach, block), 0)
        query_pos = j * block + lax.broadcasted_iota(jnp.int32, (reach, block), 1)
        allowed = (key_pos >= start) & (key_pos <= query_pos)
        allowed = jnp.concatenate([allowed] * (span // head_dim), axis=1)
        column = j * block + lax.broadcasted_iota(jnp.int32, (1, block), 1)
        live = (column >= start) & (column < end)
        query_block = queries[pl.ds(j * block, block), :]
        one = [
            jnp.where((lane >= low) & (lane < low + head_dim), query_block, jnp.zeros_like(query_block))
            for low in range(0, span, head_dim)
        ]
        scores = lax.dot_general(
            keys[pl.ds(0, reach), :],
            jnp.concatenate(one, axis=0),
            (((1,), (1,)), ((), ())),
            preferred_element_type=jnp.float32,
        )
        scores = jnp.where(allowed, scores * scale, NEGATIVE)
        highest = jnp.max(scores, axis=0, keepdims=True)
        weight = jnp.exp(scores - highest)
        total = jnp.sum(weight, axis=0, keepdims=True)
        summed = jnp.dot(
            values[:, pl.ds(0, reach)], weight.astype(jnp.bfloat16), preferred_element_type=jnp.float32
        )
        for h in range(span // head_dim):
            rows, lanes = slice(h * head_dim, (h + 1) * head_dim), slice(h * block, (h + 1) * block)
            result = jnp.where(live, summed[rows, lanes] / total[:, lanes], 0.0)
            out_ref[rows, pl.ds(j * block, block)] = result.astype(jnp.bfloat16)


def place(sources, refs, target, begin, columns):
    depth = refs[0].shape[0]
    agent = lax.axis_index("agent")
    core = lax.axis_index("tm") % 2

    def put(ref, index):
        rows = pl.ds(pl.multiple_of(index * depth, depth), depth)
        low = min(begin, ref.shape[1] - columns)
        target[rows, :] = ref[:, low : low + columns]

    put(refs[0], agent)
    for n, pair in enumerate(sources):
        for here in (0, 1):
            for ref, offset in zip(refs[1 + 2 * n : 3 + 2 * n], (pair[here], pair[1 - here])):
                if offset is not None:
                    pl.when(core == here)(functools.partial(put, ref, agent ^ offset))


def first_kernel(sources, head_dim, bounds_ref, normed_ref, *refs):
    shards, refs = refs[: 1 + 2 * len(sources)], refs[1 + 2 * len(sources) :]
    out_ref, late, weights, held = refs[0], refs[1:4], refs[4], refs[5:]
    _, columns = weights.shape
    span = columns // 3
    place(sources, shards, weights, 0, columns)
    for n in range(3):
        full = jnp.dot(
            normed_ref[...], weights[:, n * span : (n + 1) * span], preferred_element_type=jnp.float32
        )
        for m, target in enumerate((held[n], late[n])):
            part = full[:, m * LANES : (m + 1) * LANES]
            target[...] = (part.T if n == 2 else part).astype(jnp.bfloat16)
    attend(bounds_ref, *held, out_ref, head_dim)


def second_kernel(head_dim, bounds_ref, queries, keys, values, out_ref):
    attend(bounds_ref, queries, keys, values, out_ref, head_dim)


def transposed_dot(weight, value):
    return lax.dot_general(
        weight, value, (((0,), (0,)), ((), ())), preferred_element_type=jnp.float32
    )


def partial_kernel(sources, *refs):
    shards, refs = refs[: 1 + 2 * len(sources)], refs[1 + 2 * len(sources) :]
    here, kept_ref, given_ref, kept_weights, given_weights, weights = (
        refs[:3],
        *refs[3:7],
        refs[7],
    )
    _, columns = weights.shape
    half = columns // 2
    core, y = lax.axis_index("tm") % 2, lax.axis_index("tm") // 2
    place(sources, shards, weights, 3 * columns, columns)
    for n, (ref, last) in enumerate(((kept_ref, kept_weights), (given_ref, given_weights))):
        lanes = pl.ds(pl.multiple_of((core ^ n) * half, half), half)
        total = None
        for m, value in enumerate(here):
            first = ((y ^ (m // 2)) * 2 + m % 2) * LANES
            rows = pl.ds(pl.multiple_of(first, LANES), LANES)
            term = transposed_dot(weights[rows, lanes], value[...])
            total = term if total is None else total + term
        ref[...] = total
        last[...] = weights[pl.ds(pl.multiple_of(((y ^ 1) * 2 + 1) * LANES, LANES), LANES), lanes]


def given_kernel(partial_ref, weights_ref, value_ref, out_ref):
    out_ref[...] = (partial_ref[...] + transposed_dot(weights_ref[...], value_ref[...])).astype(
        jnp.bfloat16
    )


def final_kernel(partial_ref, weights_ref, value_ref, received_ref, out_ref):
    core = lax.axis_index("tm") % 2
    out_ref[1 - core] = received_ref[...]
    out_ref[core] = (partial_ref[...] + transposed_dot(weights_ref[...], value_ref[...])).astype(
        jnp.bfloat16
    )


def fits(n_tm, n_agent, features):
    agents_here, rows_here, width = features.shape
    return (
        n_tm == 4
        and n_agent >= 4
        and n_agent & (n_agent - 1) == 0
        and agents_here == 2
        and width == 4 * LANES
        and LANES % (width // HEADS) == 0
        and rows_here % LANES == 0
        and width % (16 * n_agent) == 0
        and n_tm * rows_here * width <= 2**20
    )


def split_heads(n_tm, n_agent, features, norm_gain, w_query, w_key, w_value, w_out, tracks):
    _, rows_here, width = features.shape
    head_dim = width // HEADS
    span = width // 2
    steps = n_tm * rows_here
    y = lax.axis_index("tm") // 2

    def across(value):
        return lax.ppermute(value, "tm", [(i, i ^ 2) for i in range(n_tm)])

    def swap(value):
        return lax.ppermute(value, "tm", [(i, i ^ 1) for i in range(n_tm)])

    def fetch(value, offsets):
        pairs = [
            (t * n_agent + (a ^ offsets[t % 2]), t * n_agent + a)
            for t in range(n_tm)
            for a in range(n_agent)
            if offsets[t % 2] is not None
        ]
        return lax.ppermute(value, ("tm", "agent"), pairs)

    def kernel(body, outs, args, scratch=(), smem=0, **estimate):
        vmem = pl.BlockSpec(memory_space=pltpu.VMEM)
        out = pl.pallas_call(
            body,
            out_shape=[jax.ShapeDtypeStruct(shape, dtype) for shape, dtype in outs],
            in_specs=[pl.BlockSpec(memory_space=pltpu.SMEM)] * smem + [vmem] * (len(args) - smem),
            out_specs=[vmem] * len(outs),
            scratch_shapes=[pltpu.VMEM(shape, dtype) for shape, dtype in scratch],
            compiler_params=params(),
            cost_estimate=cost(**estimate),
        )(*args)
        return out

    half, full = jnp.bfloat16, jnp.float32
    pieces = [
        lax.dynamic_slice_in_dim(w, y * span, span, 1) for w in (w_query, w_key, w_value, w_out)
    ]
    packed, projections, outward = jnp.concatenate(pieces, 1), jnp.concatenate(pieces[:3], 1), pieces[3]
    evens = list(range(n_agent - 2, 0, -2))
    odds = list(range(n_agent - 1, 0, -2))
    sources = list(zip(evens + [None], odds))
    near = len(sources) - 2
    fetched = [fetch(projections if n < near else packed, pair) for n, pair in enumerate(sources)]
    fetched_out = [fetch(outward, pair) for pair in sources[:near]]
    other_rows = across(features)
    beside = swap(features)
    diagonal = swap(other_rows)
    swapped = [swap(value) for value in fetched]
    swapped_out = [swap(value) for value in fetched_out]
    normed, bounds = kernel(
        norm_kernel,
        [((steps, width), half), ((2, 8, LANES), jnp.int32)],
        (tracks, norm_gain.reshape(1, width), features, beside, other_rows, diagonal),
        smem=1,
        flops=8 * steps * width,
    )
    shards = [packed] + [v for pair in zip(fetched, swapped) for v in pair]
    head_flops = 4 * steps * steps * LANES
    heads = [((steps, LANES), half)] * 2 + [((LANES, steps), half)]
    exponentials = steps * steps * LANES // head_dim
    attended_first, *late = kernel(
        functools.partial(first_kernel, sources, head_dim),
        [((LANES, steps), half)] + heads,
        (bounds, normed, *shards),
        scratch=[((width, 3 * span), half)] + heads,
        flops=6 * steps * width * span + head_flops,
        transcendentals=exponentials,
    )
    other_first = across(attended_first)
    (attended_second,) = kernel(
        functools.partial(second_kernel, head_dim),
        [((LANES, steps), half)],
        (bounds, *late),
        flops=head_flops,
        transcendentals=exponentials,
    )
    other_second = across(attended_second)
    out_shards = [packed] + [
        v
        for pair in zip(fetched_out + fetched[near:], swapped_out + swapped[near:])
        for v in pair
    ]
    kept, given, kept_weights, given_weights = kernel(
        functools.partial(partial_kernel, sources),
        [((span // 2, steps), full)] * 2 + [((LANES, span // 2), half)] * 2,
        (*out_shards, attended_first, attended_second, other_first),
        scratch=[((width, span), half)],
        flops=2 * steps * width * span,
    )
    (given,) = kernel(
        given_kernel,
        [((span // 2, steps), half)],
        (given, given_weights, other_second),
        flops=steps * LANES * span,
    )
    received = swap(given)
    (out,) = kernel(
        final_kernel,
        [((2, span // 2, steps), half)],
        (kept, kept_weights, other_second, received),
        flops=steps * LANES * span,
    )
    return out


def solution(mesh):
    in_specs = (
        P("agent", "tm", None),
        P(),
        P("agent", None),
        P("agent", None),
        P("agent", None),
        P("agent", None),
        P("agent", None),
    )
    out_specs = P("agent", "tm", None)
    n_tm, n_agent = mesh.shape["tm"], mesh.shape["agent"]

    def local(features, *rest):
        if fits(n_tm, n_agent, features):
            return split_heads(n_tm, n_agent, features, *rest)
        return body(features, *rest)

    return jax.shard_map(local, mesh=mesh, in_specs=in_specs, out_specs=out_specs, check_vma=False)
```

```python
import functools
import math

import jax
import jax.numpy as jnp
from jax import lax
from jax.experimental import pallas as pl
from jax.experimental.pallas import tpu as pltpu
from jax.sharding import PartitionSpec as P


HEADS = 8


EPSILON = 1e-05
NEGATIVE = -1e30
LANES = 128


def normalize(inputs, gain):
    values = inputs.astype(jnp.float32)
    meansq = jnp.mean(values * values, axis=-1, keepdims=True)
    return (values * lax.rsqrt(meansq + EPSILON) * gain).astype(jnp.bfloat16)


def project(normed, weight):
    return jnp.einsum("asd,de->ase", normed, weight, preferred_element_type=jnp.float32).astype(
        jnp.bfloat16
    )


def body(features, norm_gain, w_query, w_key, w_value, w_out, tracks):
    full_query, full_key, full_value, full_out = (
        lax.all_gather(w_query, "agent", axis=0, tiled=True),
        lax.all_gather(w_key, "agent", axis=0, tiled=True),
        lax.all_gather(w_value, "agent", axis=0, tiled=True),
        lax.all_gather(w_out, "agent", axis=0, tiled=True),
    )
    agents_here, rows_here, width = features.shape
    head_dim = width // HEADS
    scale = 1.0 / math.sqrt(head_dim)
    normed = normalize(features, norm_gain)
    starts = tracks[:, 0]
    ends = tracks[:, 1]
    queries = project(normed, full_query).reshape(agents_here, rows_here, HEADS, head_dim)
    first_row = lax.axis_index("tm") * rows_here
    query_pos = first_row + jnp.arange(rows_here, dtype=jnp.int32)
    row_live = (query_pos[None, :] >= starts[:, None]) & (query_pos[None, :] < ends[:, None])
    initial = (
        jnp.full((agents_here, HEADS, rows_here), NEGATIVE, jnp.float32),
        jnp.zeros((agents_here, HEADS, rows_here), jnp.float32),
        jnp.zeros((agents_here, HEADS, rows_here, head_dim), jnp.float32),
    )

    def attend(carry, key_block, value_block, key_start):
        highest, total, summed = carry
        count = key_block.shape[1]
        key_pos = key_start + jnp.arange(count, dtype=jnp.int32)
        scores = (
            jnp.einsum("athd,ashd->ahts", queries, key_block, preferred_element_type=jnp.float32)
            * scale
        )
        allowed = (
            (key_pos[None, None, :] >= starts[:, None, None])
            & (key_pos[None, None, :] <= query_pos[None, :, None])
            & row_live[:, :, None]
        )
        allowed = allowed[:, None]
        masked = jnp.where(allowed, scores, NEGATIVE)
        new_high = jnp.maximum(highest, jnp.max(masked, axis=-1))
        weights = jnp.where(allowed, jnp.exp(scores - new_high[..., None]), 0.0)
        factor = jnp.exp(highest - new_high)
        total = factor * total + jnp.sum(weights, axis=-1)
        summed = factor[..., None] * summed + jnp.einsum(
            "ahts,ashd->ahtd",
            weights.astype(jnp.bfloat16),
            value_block,
            preferred_element_type=jnp.float32,
        )
        return (new_high, total, summed)

    def sweep(carry, key_rows, value_rows, key_start):
        count = key_rows.shape[1]
        span = 512
        if span == count:
            return attend(carry, key_rows, value_rows, key_start)

        def advance(index, state):
            offset = (index * span).astype(jnp.int32)
            key_block = lax.dynamic_slice_in_dim(key_rows, offset, span, 1)
            value_block = lax.dynamic_slice_in_dim(value_rows, offset, span, 1)
            return attend(state, key_block, value_block, key_start + offset)

        return lax.fori_loop(0, count // span, advance, carry)

    piece = lax.all_gather(normed, "tm", axis=1, tiled=True)
    count = piece.shape[1]
    key_rows = project(piece, full_key).reshape(agents_here, count, HEADS, head_dim)
    value_rows = project(piece, full_value).reshape(agents_here, count, HEADS, head_dim)
    final = sweep(initial, key_rows, value_rows, jnp.int32(0))
    _, total, summed = final
    denom = jnp.where(row_live[:, None, :], total, 1.0)
    attended = summed / denom[..., None] * row_live[:, None, :, None].astype(jnp.float32)
    attended = (
        jnp.transpose(attended, (0, 2, 1, 3))
        .reshape(agents_here, rows_here, width)
        .astype(jnp.bfloat16)
    )
    projected = jnp.einsum(
        "asd,de->aes", attended, full_out, preferred_element_type=jnp.float32
    ).astype(jnp.bfloat16)
    return lax.all_to_all(projected, "tm", split_axis=1, concat_axis=2, tiled=True)


def params():
    return pltpu.CompilerParams(vmem_limit_bytes=24 * 2**20)


def cost(flops, transcendentals=0, bytes_accessed=2**20):
    return pl.CostEstimate(
        flops=flops, transcendentals=transcendentals, bytes_accessed=bytes_accessed
    )


def norm_kernel(tracks_ref, gain_ref, mine_ref, beside_ref, other_ref, diagonal_ref, *outs):
    normed_ref, below_ref, within_ref, live_ref = outs
    rows_here = mine_ref.shape[1]
    tm = lax.axis_index("tm")
    core = tm % 2
    gain = gain_ref[...]
    for k, ref in enumerate((mine_ref, beside_ref, other_ref, diagonal_ref)):
        rows = pl.ds(pl.multiple_of((tm ^ k) * rows_here, rows_here), rows_here)
        normed_ref[rows, :] = normalize(ref[core], gain)
    start, end = tracks_ref[core, 0], tracks_ref[core, 1]
    steps, block = below_ref.shape
    key_pos = lax.broadcasted_iota(jnp.int32, (steps, block), 0)
    column = lax.broadcasted_iota(jnp.int32, (steps, block), 1)
    early = key_pos < start
    barred = early | (lax.rem(key_pos, block) > column)
    below_ref[...] = jnp.where(early, NEGATIVE, 0.0).astype(below_ref.dtype)
    within_ref[...] = jnp.where(barred, NEGATIVE, 0.0).astype(within_ref.dtype)
    position = lax.broadcasted_iota(jnp.int32, live_ref.shape, 1)
    live_ref[...] = ((position >= start) & (position < end)).astype(jnp.float32)


def attend(below_ref, within_ref, live_ref, queries, keys, values, out_ref, first, head_dim):
    steps = out_ref.shape[1]
    block = span = LANES
    group = pl.ds(first, span)
    ratio = math.log2(math.e) / math.sqrt(head_dim)
    lane = lax.broadcasted_iota(jnp.int32, (block, span), 1)
    diagonal = lane == lax.broadcasted_iota(jnp.int32, (block, span), 0)
    diagonal = diagonal.astype(jnp.float32).astype(jnp.bfloat16)
    for j in range(steps // block):
        here = pl.ds(j * block, block)
        query_block = queries[here, group]
        one = [
            jnp.where((lane >= low) & (lane < low + head_dim), query_block, jnp.zeros_like(query_block))
            for low in range(0, span, head_dim)
        ]
        one = jnp.concatenate([jnp.concatenate([o, diagonal], axis=1) for o in one], axis=0)
        scores = []
        for begin, count, mask in ((0, j * block, below_ref), (j * block, block, within_ref)):
            if count:
                rows = pl.ds(begin, count)
                scores.append(
                    lax.dot_general(
                        jnp.concatenate([keys[rows, group], mask[rows, :]], axis=1),
                        one,
                        (((1,), (1,)), ((), ())),
                        preferred_element_type=jnp.float32,
                    )
                )
        highest = functools.reduce(
            jnp.maximum, [jnp.max(score, axis=0, keepdims=True) for score in scores]
        )
        weight = [jnp.exp2((score - highest) * ratio) for score in scores]
        total = sum(jnp.sum(w, axis=0, keepdims=True) for w in weight)
        weight = jnp.concatenate([w.astype(jnp.bfloat16) for w in weight], axis=0)
        summed = jnp.dot(
            values[group, pl.ds(0, (j + 1) * block)], weight, preferred_element_type=jnp.float32
        )
        live = live_ref[:1, here] > 0.0
        for h in range(span // head_dim):
            rows, lanes = slice(h * head_dim, (h + 1) * head_dim), slice(h * block, (h + 1) * block)
            result = jnp.where(live, summed[rows, lanes] / total[:, lanes], 0.0)
            out_ref[pl.ds(first + h * head_dim, head_dim), here] = result.astype(jnp.bfloat16)


def place(sources, refs, target, begin, columns):
    depth = refs[0].shape[0]
    agent = lax.axis_index("agent")
    core = lax.axis_index("tm") % 2

    def put(ref, index):
        rows = pl.ds(pl.multiple_of(index * depth, depth), depth)
        low = min(begin, ref.shape[1] - columns)
        target[rows, :] = ref[:, low : low + columns]

    put(refs[0], agent)
    for n, pair in enumerate(sources):
        for here in (0, 1):
            for ref, offset in zip(refs[1 + 2 * n : 3 + 2 * n], (pair[here], pair[1 - here])):
                if offset is not None:
                    pl.when(core == here)(functools.partial(put, ref, agent ^ offset))


def attention_kernel(sources, head_dim, normed_ref, below_ref, within_ref, live_ref, *refs):
    shards = refs[: 1 + 2 * len(sources)]
    out_ref, weights, queries, keys, values = refs[1 + 2 * len(sources) :]
    _, columns = weights.shape
    span = columns // 3
    place(sources, shards, weights, 0, columns)
    for n, target in enumerate((queries, keys, values)):
        full = jnp.dot(
            normed_ref[...], weights[:, n * span : (n + 1) * span], preferred_element_type=jnp.float32
        )
        target[...] = (full.T if n == 2 else full).astype(jnp.bfloat16)
    for first in range(0, span, LANES):
        attend(below_ref, within_ref, live_ref, queries, keys, values, out_ref, first, head_dim)


def transposed_dot(weight, value):
    return lax.dot_general(
        weight, value, (((0,), (0,)), ((), ())), preferred_element_type=jnp.float32
    )


def partial_kernel(sources, *refs):
    shards, refs = refs[: 1 + 2 * len(sources)], refs[1 + 2 * len(sources) :]
    value_ref, kept_ref, given_ref, kept_weights, given_weights, weights = refs
    _, columns = weights.shape
    half = columns // 2
    core, y = lax.axis_index("tm") % 2, lax.axis_index("tm") // 2
    place(sources, shards, weights, 3 * columns, columns)
    mine = pl.ds(pl.multiple_of(y * columns, columns), columns)
    other = pl.ds(pl.multiple_of((y ^ 1) * columns, columns), columns)
    for n, (ref, last) in enumerate(((kept_ref, kept_weights), (given_ref, given_weights))):
        lanes = pl.ds(pl.multiple_of((core ^ n) * half, half), half)
        ref[...] = transposed_dot(weights[mine, lanes], value_ref[...])
        last[...] = weights[other, lanes]


def given_kernel(partial_ref, weights_ref, value_ref, out_ref):
    out_ref[...] = (partial_ref[...] + transposed_dot(weights_ref[...], value_ref[...])).astype(
        jnp.bfloat16
    )


def kept_kernel(partial_ref, weights_ref, value_ref, out_ref, held):
    given_kernel(partial_ref, weights_ref, value_ref, held)
    pltpu.sync_copy(held, out_ref.at[lax.axis_index("tm") % 2])


def final_kernel(received_ref, started_ref, out_ref):
    pltpu.sync_copy(received_ref, out_ref.at[1 - lax.axis_index("tm") % 2])


def fits(n_tm, n_agent, features):
    agents_here, rows_here, width = features.shape
    return (
        n_tm == 4
        and n_agent >= 4
        and n_agent & (n_agent - 1) == 0
        and agents_here == 2
        and width == 4 * LANES
        and LANES % (width // HEADS) == 0
        and rows_here % LANES == 0
        and width % (16 * n_agent) == 0
        and n_tm * rows_here * width <= 2**20
    )


def split_heads(n_tm, n_agent, features, norm_gain, w_query, w_key, w_value, w_out, tracks):
    _, rows_here, width = features.shape
    head_dim = width // HEADS
    span = width // 2
    steps = n_tm * rows_here
    y = lax.axis_index("tm") // 2

    def across(value):
        return lax.ppermute(value, "tm", [(i, i ^ 2) for i in range(n_tm)])

    def swap(value):
        return lax.ppermute(value, "tm", [(i, i ^ 1) for i in range(n_tm)])

    def fetch(value, offsets):
        pairs = [
            (t * n_agent + (a ^ offsets[t % 2]), t * n_agent + a)
            for t in range(n_tm)
            for a in range(n_agent)
            if offsets[t % 2] is not None
        ]
        return lax.ppermute(value, ("tm", "agent"), pairs)

    vmem = pl.BlockSpec(memory_space=pltpu.VMEM)
    smem = pl.BlockSpec(memory_space=pltpu.SMEM)
    anywhere = pl.BlockSpec(memory_space=pl.ANY)

    def kernel(body, outs, args, scratch=(), specs=None, out_spec=vmem, aliases={}, **estimate):
        return pl.pallas_call(
            body,
            out_shape=[jax.ShapeDtypeStruct(shape, dtype) for shape, dtype in outs],
            in_specs=specs or [vmem] * len(args),
            out_specs=[out_spec] * len(outs),
            scratch_shapes=[pltpu.VMEM(shape, dtype) for shape, dtype in scratch],
            input_output_aliases=aliases,
            compiler_params=params(),
            cost_estimate=cost(**estimate),
        )(*args)

    half, full = jnp.bfloat16, jnp.float32
    pieces = [
        lax.dynamic_slice_in_dim(w, y * span, span, 1) for w in (w_query, w_key, w_value, w_out)
    ]
    packed, projections, outward = jnp.concatenate(pieces, 1), jnp.concatenate(pieces[:3], 1), pieces[3]
    evens = list(range(n_agent - 2, 0, -2))
    odds = list(range(n_agent - 1, 0, -2))
    sources = list(zip(evens + [None], odds))
    near = len(sources) - 2
    fetched = [fetch(projections if n < near else packed, pair) for n, pair in enumerate(sources)]
    fetched_out = [fetch(outward, pair) for pair in sources[:near]]
    other_rows = across(features)
    beside = swap(features)
    diagonal = swap(other_rows)
    swapped = [swap(value) for value in fetched]
    swapped_out = [swap(value) for value in fetched_out]
    masks = kernel(
        norm_kernel,
        [((steps, width), half)] + [((steps, LANES), half)] * 2 + [((8, steps), full)],
        (tracks, norm_gain.reshape(1, width), features, beside, other_rows, diagonal),
        specs=[smem] + [vmem] * 5,
        flops=8 * steps * width,
    )
    shards = [packed] + [v for pair in zip(fetched, swapped) for v in pair]
    (attended,) = kernel(
        functools.partial(attention_kernel, sources, head_dim),
        [((span, steps), half)],
        (*masks, *shards),
        scratch=[((width, 3 * span), half)] + [((steps, span), half)] * 2 + [((span, steps), half)],
        flops=6 * steps * width * span + 4 * steps * steps * span,
        transcendentals=steps * steps * span // head_dim,
    )
    other = across(attended)
    out_shards = [packed] + [
        v
        for pair in zip(fetched_out + fetched[near:], swapped_out + swapped[near:])
        for v in pair
    ]
    kept, given, kept_weights, given_weights = kernel(
        functools.partial(partial_kernel, sources),
        [((span // 2, steps), full)] * 2 + [((span, span // 2), half)] * 2,
        (*out_shards, attended),
        scratch=[((width, span), half)],
        flops=2 * steps * span * span,
    )
    (given,) = kernel(
        given_kernel,
        [((span // 2, steps), half)],
        (given, given_weights, other),
        flops=steps * span * span,
    )
    received = swap(given)
    (started,) = kernel(
        kept_kernel,
        [((2, span // 2, steps), half)],
        (kept, kept_weights, other),
        scratch=[((span // 2, steps), half)],
        out_spec=anywhere,
        flops=steps * span * span,
    )
    (out,) = kernel(
        final_kernel,
        [((2, span // 2, steps), half)],
        (received, started),
        specs=[vmem, anywhere],
        out_spec=anywhere,
        aliases={1: 0},
        flops=0,
    )
    return out


def solution(mesh):
    in_specs = (
        P("agent", "tm", None),
        P(),
        P("agent", None),
        P("agent", None),
        P("agent", None),
        P("agent", None),
        P("agent", None),
    )
    out_specs = P("agent", "tm", None)
    n_tm, n_agent = mesh.shape["tm"], mesh.shape["agent"]

    def local(features, *rest):
        if fits(n_tm, n_agent, features):
            return split_heads(n_tm, n_agent, features, *rest)
        return body(features, *rest)

    return jax.shard_map(local, mesh=mesh, in_specs=in_specs, out_specs=out_specs, check_vma=False)
```

```python
import functools
import math

import jax
import jax.numpy as jnp
from jax import lax
from jax.experimental import pallas as pl
from jax.experimental.pallas import tpu as pltpu
from jax.sharding import PartitionSpec as P


HEADS = 8


EPSILON = 1e-05
NEGATIVE = -1e30
LANES = 128


def normalize(inputs, gain):
    values = inputs.astype(jnp.float32)
    meansq = jnp.mean(values * values, axis=-1, keepdims=True)
    return (values * lax.rsqrt(meansq + EPSILON) * gain).astype(jnp.bfloat16)


def project(normed, weight):
    return jnp.einsum("asd,de->ase", normed, weight, preferred_element_type=jnp.float32).astype(
        jnp.bfloat16
    )


def body(features, norm_gain, w_query, w_key, w_value, w_out, tracks):
    full_query, full_key, full_value, full_out = (
        lax.all_gather(w_query, "agent", axis=0, tiled=True),
        lax.all_gather(w_key, "agent", axis=0, tiled=True),
        lax.all_gather(w_value, "agent", axis=0, tiled=True),
        lax.all_gather(w_out, "agent", axis=0, tiled=True),
    )
    agents_here, rows_here, width = features.shape
    head_dim = width // HEADS
    scale = 1.0 / math.sqrt(head_dim)
    normed = normalize(features, norm_gain)
    starts = tracks[:, 0]
    ends = tracks[:, 1]
    queries = project(normed, full_query).reshape(agents_here, rows_here, HEADS, head_dim)
    first_row = lax.axis_index("tm") * rows_here
    query_pos = first_row + jnp.arange(rows_here, dtype=jnp.int32)
    row_live = (query_pos[None, :] >= starts[:, None]) & (query_pos[None, :] < ends[:, None])
    initial = (
        jnp.full((agents_here, HEADS, rows_here), NEGATIVE, jnp.float32),
        jnp.zeros((agents_here, HEADS, rows_here), jnp.float32),
        jnp.zeros((agents_here, HEADS, rows_here, head_dim), jnp.float32),
    )

    def attend(carry, key_block, value_block, key_start):
        highest, total, summed = carry
        count = key_block.shape[1]
        key_pos = key_start + jnp.arange(count, dtype=jnp.int32)
        scores = (
            jnp.einsum("athd,ashd->ahts", queries, key_block, preferred_element_type=jnp.float32)
            * scale
        )
        allowed = (
            (key_pos[None, None, :] >= starts[:, None, None])
            & (key_pos[None, None, :] <= query_pos[None, :, None])
            & row_live[:, :, None]
        )
        allowed = allowed[:, None]
        masked = jnp.where(allowed, scores, NEGATIVE)
        new_high = jnp.maximum(highest, jnp.max(masked, axis=-1))
        weights = jnp.where(allowed, jnp.exp(scores - new_high[..., None]), 0.0)
        factor = jnp.exp(highest - new_high)
        total = factor * total + jnp.sum(weights, axis=-1)
        summed = factor[..., None] * summed + jnp.einsum(
            "ahts,ashd->ahtd",
            weights.astype(jnp.bfloat16),
            value_block,
            preferred_element_type=jnp.float32,
        )
        return (new_high, total, summed)

    def sweep(carry, key_rows, value_rows, key_start):
        count = key_rows.shape[1]
        span = 512
        if span == count:
            return attend(carry, key_rows, value_rows, key_start)

        def advance(index, state):
            offset = (index * span).astype(jnp.int32)
            key_block = lax.dynamic_slice_in_dim(key_rows, offset, span, 1)
            value_block = lax.dynamic_slice_in_dim(value_rows, offset, span, 1)
            return attend(state, key_block, value_block, key_start + offset)

        return lax.fori_loop(0, count // span, advance, carry)

    piece = lax.all_gather(normed, "tm", axis=1, tiled=True)
    count = piece.shape[1]
    key_rows = project(piece, full_key).reshape(agents_here, count, HEADS, head_dim)
    value_rows = project(piece, full_value).reshape(agents_here, count, HEADS, head_dim)
    final = sweep(initial, key_rows, value_rows, jnp.int32(0))
    _, total, summed = final
    denom = jnp.where(row_live[:, None, :], total, 1.0)
    attended = summed / denom[..., None] * row_live[:, None, :, None].astype(jnp.float32)
    attended = (
        jnp.transpose(attended, (0, 2, 1, 3))
        .reshape(agents_here, rows_here, width)
        .astype(jnp.bfloat16)
    )
    projected = jnp.einsum(
        "asd,de->aes", attended, full_out, preferred_element_type=jnp.float32
    ).astype(jnp.bfloat16)
    return lax.all_to_all(projected, "tm", split_axis=1, concat_axis=2, tiled=True)


def params():
    return pltpu.CompilerParams(vmem_limit_bytes=24 * 2**20)


def cost(flops, transcendentals=0, bytes_accessed=2**20):
    return pl.CostEstimate(
        flops=flops, transcendentals=transcendentals, bytes_accessed=bytes_accessed
    )


def norm_kernel(tracks_ref, gain_ref, mine_ref, beside_ref, other_ref, diagonal_ref, *outs):
    normed_ref, below_ref, within_ref, live_ref = outs
    rows_here = mine_ref.shape[1]
    tm = lax.axis_index("tm")
    core = tm % 2
    gain = gain_ref[...]
    for k, ref in enumerate((mine_ref, beside_ref, other_ref, diagonal_ref)):
        rows = pl.ds(pl.multiple_of((tm ^ k) * rows_here, rows_here), rows_here)
        normed_ref[rows, :] = normalize(ref[core], gain)
    start, end = tracks_ref[core, 0], tracks_ref[core, 1]
    steps, block = below_ref.shape
    key_pos = lax.broadcasted_iota(jnp.int32, (steps, block), 0)
    column = lax.broadcasted_iota(jnp.int32, (steps, block), 1)
    early = key_pos < start
    barred = early | (lax.rem(key_pos, block) > column)
    below_ref[...] = jnp.where(early, NEGATIVE, 0.0).astype(below_ref.dtype)
    within_ref[...] = jnp.where(barred, NEGATIVE, 0.0).astype(within_ref.dtype)
    position = lax.broadcasted_iota(jnp.int32, live_ref.shape, 1)
    live_ref[...] = ((position >= start) & (position < end)).astype(jnp.float32)


def attend(below_ref, within_ref, live_ref, queries, keys, values, out_ref, head_dim):
    steps = out_ref.shape[1]
    block = span = LANES
    ratio = math.log2(math.e) / math.sqrt(head_dim)
    lane = lax.broadcasted_iota(jnp.int32, (block, span), 1)
    diagonal = lane == lax.broadcasted_iota(jnp.int32, (block, span), 0)
    diagonal = diagonal.astype(jnp.float32).astype(jnp.bfloat16)
    for j in range(steps // block):
        here = pl.ds(j * block, block)
        query_block = queries[here, :]
        one = [
            jnp.where((lane >= low) & (lane < low + head_dim), query_block, jnp.zeros_like(query_block))
            for low in range(0, span, head_dim)
        ]
        one = jnp.concatenate([jnp.concatenate([o, diagonal], axis=1) for o in one], axis=0)
        scores = []
        for begin, count, mask in ((0, j * block, below_ref), (j * block, block, within_ref)):
            if count:
                rows = pl.ds(begin, count)
                scores.append(
                    lax.dot_general(
                        jnp.concatenate([keys[rows, :], mask[rows, :]], axis=1),
                        one,
                        (((1,), (1,)), ((), ())),
                        preferred_element_type=jnp.float32,
                    )
                )
        highest = functools.reduce(
            jnp.maximum, [jnp.max(score, axis=0, keepdims=True) for score in scores]
        )
        weight = [jnp.exp2((score - highest) * ratio) for score in scores]
        total = sum(jnp.sum(w, axis=0, keepdims=True) for w in weight)
        weight = jnp.concatenate([w.astype(jnp.bfloat16) for w in weight], axis=0)
        summed = jnp.dot(
            values[:, pl.ds(0, (j + 1) * block)], weight, preferred_element_type=jnp.float32
        )
        live = live_ref[:1, here] > 0.0
        for h in range(span // head_dim):
            rows, lanes = slice(h * head_dim, (h + 1) * head_dim), slice(h * block, (h + 1) * block)
            result = jnp.where(live, summed[rows, lanes] / total[:, lanes], 0.0)
            out_ref[pl.ds(h * head_dim, head_dim), here] = result.astype(jnp.bfloat16)


def pack_kernel(*refs):
    sources, out_ref, sems = refs[:-2], refs[-2], refs[-1]
    span = out_ref.shape[1] // len(sources)
    first = pl.multiple_of(lax.axis_index("tm") // 2 * span, span)
    copies = [
        pltpu.make_async_copy(
            ref.at[:, pl.ds(first, span)], out_ref.at[:, pl.ds(n * span, span)], sems.at[n]
        )
        for n, ref in enumerate(sources)
    ]
    for copy in copies:
        copy.start()
    for copy in copies:
        copy.wait()


def place(sources, refs, target, begin):
    depth, columns = refs[0].shape[0], target.shape[1]
    agent = lax.axis_index("agent")
    core = lax.axis_index("tm") % 2

    def put(ref, index):
        rows = pl.ds(pl.multiple_of(index * depth, depth), depth)
        target[rows, :] = ref[:, begin : begin + columns]

    put(refs[0], agent)
    for n, pair in enumerate(sources):
        for here in (0, 1):
            for ref, offset in zip(refs[1 + 2 * n : 3 + 2 * n], (pair[here], pair[1 - here])):
                if offset is not None:
                    pl.when(core == here)(functools.partial(put, ref, agent ^ offset))


def first_kernel(sources, head_dim, normed_ref, below_ref, within_ref, live_ref, *refs):
    shards, refs = refs[: 1 + 2 * len(sources)], refs[1 + 2 * len(sources) :]
    out_ref, late, weights, held = refs[0], refs[1:4], refs[4], refs[5:]
    _, columns = weights.shape
    span = columns // 3
    place(sources, shards, weights, 0)
    for n in range(3):
        full = jnp.dot(
            normed_ref[...], weights[:, n * span : (n + 1) * span], preferred_element_type=jnp.float32
        )
        for m, target in enumerate((held[n], late[n])):
            part = full[:, m * LANES : (m + 1) * LANES]
            target[...] = (part.T if n == 2 else part).astype(jnp.bfloat16)
    attend(below_ref, within_ref, live_ref, *held, out_ref, head_dim)


def second_kernel(head_dim, below_ref, within_ref, live_ref, queries, keys, values, out_ref):
    attend(below_ref, within_ref, live_ref, queries, keys, values, out_ref, head_dim)


def transposed_dot(weight, value):
    return lax.dot_general(
        weight, value, (((0,), (0,)), ((), ())), preferred_element_type=jnp.float32
    )


def partial_kernel(sources, *refs):
    shards, refs = refs[: 1 + 2 * len(sources)], refs[1 + 2 * len(sources) :]
    here, kept_ref, given_ref, kept_weights, given_weights, weights = (
        refs[:3],
        *refs[3:7],
        refs[7],
    )
    _, columns = weights.shape
    half = columns // 2
    core, y = lax.axis_index("tm") % 2, lax.axis_index("tm") // 2
    place(sources, shards, weights, 3 * columns)
    for n, (ref, last) in enumerate(((kept_ref, kept_weights), (given_ref, given_weights))):
        lanes = pl.ds(pl.multiple_of((core ^ n) * half, half), half)
        total = None
        for m, value in enumerate(here):
            group = ((y ^ (m // 2)) * 2 + m % 2) * LANES
            rows = pl.ds(pl.multiple_of(group, LANES), LANES)
            term = transposed_dot(weights[rows, lanes], value[...])
            total = term if total is None else total + term
        ref[...] = total
        last[...] = weights[pl.ds(pl.multiple_of(((y ^ 1) * 2 + 1) * LANES, LANES), LANES), lanes]


def given_kernel(partial_ref, weights_ref, value_ref, out_ref):
    out_ref[...] = (partial_ref[...] + transposed_dot(weights_ref[...], value_ref[...])).astype(
        jnp.bfloat16
    )


def kept_kernel(partial_ref, weights_ref, value_ref, out_ref, held):
    given_kernel(partial_ref, weights_ref, value_ref, held)
    pltpu.sync_copy(held, out_ref.at[lax.axis_index("tm") % 2])


def final_kernel(received_ref, started_ref, out_ref):
    pltpu.sync_copy(received_ref, out_ref.at[1 - lax.axis_index("tm") % 2])


def fits(n_tm, n_agent, features):
    agents_here, rows_here, width = features.shape
    return (
        n_tm == 4
        and n_agent == 8
        and agents_here == 2
        and width == 4 * LANES
        and LANES % (width // HEADS) == 0
        and rows_here % LANES == 0
        and width % (16 * n_agent) == 0
        and n_tm * rows_here * width <= 2**20
    )


def split_heads(n_tm, n_agent, features, norm_gain, w_query, w_key, w_value, w_out, tracks):
    _, rows_here, width = features.shape
    head_dim = width // HEADS
    span = width // 2
    steps = n_tm * rows_here

    def across(value):
        return lax.ppermute(value, "tm", [(i, i ^ 2) for i in range(n_tm)])

    def swap(value):
        return lax.ppermute(value, "tm", [(i, i ^ 1) for i in range(n_tm)])

    def fetch(value, offsets):
        pairs = [
            (t * n_agent + (a ^ offsets[t % 2]), t * n_agent + a)
            for t in range(n_tm)
            for a in range(n_agent)
            if offsets[t % 2] is not None
        ]
        return lax.ppermute(value, ("tm", "agent"), pairs)

    vmem = pl.BlockSpec(memory_space=pltpu.VMEM)
    smem = pl.BlockSpec(memory_space=pltpu.SMEM)
    anywhere = pl.BlockSpec(memory_space=pl.ANY)

    def kernel(body, outs, args, scratch=(), specs=None, out_spec=vmem, aliases={}, **estimate):
        return pl.pallas_call(
            body,
            out_shape=[jax.ShapeDtypeStruct(shape, dtype) for shape, dtype in outs],
            in_specs=specs or [vmem] * len(args),
            out_specs=[out_spec] * len(outs),
            scratch_shapes=[pltpu.VMEM(*s) if isinstance(s, tuple) else s for s in scratch],
            input_output_aliases=aliases,
            compiler_params=params(),
            cost_estimate=cost(**estimate),
        )(*args)

    half, full = jnp.bfloat16, jnp.float32
    (packed,) = kernel(
        pack_kernel,
        [((width // n_agent, 4 * span), half)],
        tuple(
            pltpu.with_memory_space_constraint(w, pltpu.HBM)
            for w in (w_query, w_key, w_value, w_out)
        ),
        specs=[pl.BlockSpec(memory_space=pltpu.HBM)] * 4,
        scratch=[pltpu.SemaphoreType.DMA((4,))],
        flops=0,
    )
    sources = [(6, 4), (2, 3), (None, 1), (7, 5)]
    fetched = [fetch(packed, pair) for pair in sources[:3]]
    fetched.append(fetch(fetched[0], (1, 1)))
    other_rows = across(features)
    beside = swap(features)
    diagonal = swap(other_rows)
    swapped = [swap(value) for value in fetched]
    masks = kernel(
        norm_kernel,
        [((steps, width), half)] + [((steps, LANES), half)] * 2 + [((8, steps), full)],
        (tracks, norm_gain.reshape(1, width), features, beside, other_rows, diagonal),
        specs=[smem] + [vmem] * 5,
        flops=8 * steps * width,
    )
    shards = [packed] + [v for pair in zip(fetched, swapped) for v in pair]
    head_flops = 4 * steps * steps * LANES
    heads = [((steps, LANES), half)] * 2 + [((LANES, steps), half)]
    exponentials = steps * steps * LANES // head_dim
    attended_first, *late = kernel(
        functools.partial(first_kernel, sources, head_dim),
        [((LANES, steps), half)] + heads,
        (*masks, *shards),
        scratch=[((width, 3 * span), half)] + heads,
        flops=6 * steps * width * span + head_flops,
        transcendentals=exponentials,
    )
    other_first = across(attended_first)
    (attended_second,) = kernel(
        functools.partial(second_kernel, head_dim),
        [((LANES, steps), half)],
        (*masks[1:], *late),
        flops=head_flops,
        transcendentals=exponentials,
    )
    other = across(attended_second)
    kept, given, kept_weights, given_weights = kernel(
        functools.partial(partial_kernel, sources),
        [((span // 2, steps), full)] * 2 + [((LANES, span // 2), half)] * 2,
        (*shards, attended_first, attended_second, other_first),
        scratch=[((width, span), half)],
        flops=2 * steps * width * span,
    )
    (given,) = kernel(
        given_kernel,
        [((span // 2, steps), half)],
        (given, given_weights, other),
        flops=steps * span * span,
    )
    received = swap(given)
    (started,) = kernel(
        kept_kernel,
        [((2, span // 2, steps), half)],
        (kept, kept_weights, other),
        scratch=[((span // 2, steps), half)],
        out_spec=anywhere,
        flops=steps * span * span,
    )
    (out,) = kernel(
        final_kernel,
        [((2, span // 2, steps), half)],
        (received, started),
        specs=[vmem, anywhere],
        out_spec=anywhere,
        aliases={1: 0},
        flops=0,
    )
    return out


def solution(mesh):
    in_specs = (
        P("agent", "tm", None),
        P(),
        P("agent", None),
        P("agent", None),
        P("agent", None),
        P("agent", None),
        P("agent", None),
    )
    out_specs = P("agent", "tm", None)
    n_tm, n_agent = mesh.shape["tm"], mesh.shape["agent"]

    def local(features, *rest):
        if fits(n_tm, n_agent, features):
            return split_heads(n_tm, n_agent, features, *rest)
        return body(features, *rest)

    return jax.shard_map(local, mesh=mesh, in_specs=in_specs, out_specs=out_specs, check_vma=False)
```

```python
import functools
import math

import jax
import jax.numpy as jnp
from jax import lax
from jax.experimental import pallas as pl
from jax.experimental.pallas import tpu as pltpu
from jax.sharding import PartitionSpec as P


HEADS = 8


EPSILON = 1e-05
NEGATIVE = -1e30
LANES = 128


def normalize(inputs, gain):
    values = inputs.astype(jnp.float32)
    meansq = jnp.mean(values * values, axis=-1, keepdims=True)
    return (values * lax.rsqrt(meansq + EPSILON) * gain).astype(jnp.bfloat16)


def project(normed, weight):
    return jnp.einsum("asd,de->ase", normed, weight, preferred_element_type=jnp.float32).astype(
        jnp.bfloat16
    )


def body(features, norm_gain, w_query, w_key, w_value, w_out, tracks):
    full_query, full_key, full_value, full_out = (
        lax.all_gather(w_query, "agent", axis=0, tiled=True),
        lax.all_gather(w_key, "agent", axis=0, tiled=True),
        lax.all_gather(w_value, "agent", axis=0, tiled=True),
        lax.all_gather(w_out, "agent", axis=0, tiled=True),
    )
    agents_here, rows_here, width = features.shape
    head_dim = width // HEADS
    scale = 1.0 / math.sqrt(head_dim)
    normed = normalize(features, norm_gain)
    starts = tracks[:, 0]
    ends = tracks[:, 1]
    queries = project(normed, full_query).reshape(agents_here, rows_here, HEADS, head_dim)
    first_row = lax.axis_index("tm") * rows_here
    query_pos = first_row + jnp.arange(rows_here, dtype=jnp.int32)
    row_live = (query_pos[None, :] >= starts[:, None]) & (query_pos[None, :] < ends[:, None])
    initial = (
        jnp.full((agents_here, HEADS, rows_here), NEGATIVE, jnp.float32),
        jnp.zeros((agents_here, HEADS, rows_here), jnp.float32),
        jnp.zeros((agents_here, HEADS, rows_here, head_dim), jnp.float32),
    )

    def attend(carry, key_block, value_block, key_start):
        highest, total, summed = carry
        count = key_block.shape[1]
        key_pos = key_start + jnp.arange(count, dtype=jnp.int32)
        scores = (
            jnp.einsum("athd,ashd->ahts", queries, key_block, preferred_element_type=jnp.float32)
            * scale
        )
        allowed = (
            (key_pos[None, None, :] >= starts[:, None, None])
            & (key_pos[None, None, :] <= query_pos[None, :, None])
            & row_live[:, :, None]
        )
        allowed = allowed[:, None]
        masked = jnp.where(allowed, scores, NEGATIVE)
        new_high = jnp.maximum(highest, jnp.max(masked, axis=-1))
        weights = jnp.where(allowed, jnp.exp(scores - new_high[..., None]), 0.0)
        factor = jnp.exp(highest - new_high)
        total = factor * total + jnp.sum(weights, axis=-1)
        summed = factor[..., None] * summed + jnp.einsum(
            "ahts,ashd->ahtd",
            weights.astype(jnp.bfloat16),
            value_block,
            preferred_element_type=jnp.float32,
        )
        return (new_high, total, summed)

    def sweep(carry, key_rows, value_rows, key_start):
        count = key_rows.shape[1]
        span = 512
        if span == count:
            return attend(carry, key_rows, value_rows, key_start)

        def advance(index, state):
            offset = (index * span).astype(jnp.int32)
            key_block = lax.dynamic_slice_in_dim(key_rows, offset, span, 1)
            value_block = lax.dynamic_slice_in_dim(value_rows, offset, span, 1)
            return attend(state, key_block, value_block, key_start + offset)

        return lax.fori_loop(0, count // span, advance, carry)

    piece = lax.all_gather(normed, "tm", axis=1, tiled=True)
    count = piece.shape[1]
    key_rows = project(piece, full_key).reshape(agents_here, count, HEADS, head_dim)
    value_rows = project(piece, full_value).reshape(agents_here, count, HEADS, head_dim)
    final = sweep(initial, key_rows, value_rows, jnp.int32(0))
    _, total, summed = final
    denom = jnp.where(row_live[:, None, :], total, 1.0)
    attended = summed / denom[..., None] * row_live[:, None, :, None].astype(jnp.float32)
    attended = (
        jnp.transpose(attended, (0, 2, 1, 3))
        .reshape(agents_here, rows_here, width)
        .astype(jnp.bfloat16)
    )
    projected = jnp.einsum(
        "asd,de->aes", attended, full_out, preferred_element_type=jnp.float32
    ).astype(jnp.bfloat16)
    return lax.all_to_all(projected, "tm", split_axis=1, concat_axis=2, tiled=True)


def params():
    return pltpu.CompilerParams(vmem_limit_bytes=24 * 2**20)


def cost(flops, transcendentals=0, bytes_accessed=2**20):
    return pl.CostEstimate(
        flops=flops, transcendentals=transcendentals, bytes_accessed=bytes_accessed
    )


def norm_kernel(tracks_ref, gain_ref, mine_ref, beside_ref, other_ref, diagonal_ref, *outs):
    normed_ref, bounds_ref = outs
    rows_here = mine_ref.shape[1]
    tm = lax.axis_index("tm")
    core = tm % 2
    gain = gain_ref[...]
    for k, ref in enumerate((mine_ref, beside_ref, other_ref, diagonal_ref)):
        rows = pl.ds(pl.multiple_of((tm ^ k) * rows_here, rows_here), rows_here)
        normed_ref[rows, :] = normalize(ref[core], gain)
    for n in range(2):
        bounds_ref[n] = jnp.full(bounds_ref.shape[1:], tracks_ref[core, n], jnp.int32)


def attend(bounds_ref, queries, keys, values, out_ref, head_dim):
    steps = out_ref.shape[1]
    block = span = LANES
    heads = span // head_dim
    ratio = math.log2(math.e) / math.sqrt(head_dim)
    start, end = bounds_ref[0, :1, :block], bounds_ref[1, :1, :block]
    lane = lax.broadcasted_iota(jnp.int32, (block, span), 1)

    def score(j):
        query_block = queries[pl.ds(j * block, block), :]
        one = [
            jnp.where((lane >= low) & (lane < low + head_dim), query_block, jnp.zeros_like(query_block))
            for low in range(0, span, head_dim)
        ]
        return lax.dot_general(
            keys[pl.ds(0, (j + 1) * block), :],
            jnp.concatenate(one, axis=0),
            (((1,), (1,)), ((), ())),
            preferred_element_type=jnp.float32,
        )

    def weigh(j, scores):
        reach = (j + 1) * block
        key_pos = lax.broadcasted_iota(jnp.int32, (reach, block), 0)
        query_pos = j * block + lax.broadcasted_iota(jnp.int32, (reach, block), 1)
        allowed = (key_pos >= start) & (key_pos <= query_pos)
        scores = jnp.where(jnp.concatenate([allowed] * heads, axis=1), scores, NEGATIVE)
        highest = jnp.max(scores, axis=0, keepdims=True)
        weight = jnp.exp2((scores - highest) * ratio)
        return weight.astype(jnp.bfloat16), jnp.sum(weight, axis=0, keepdims=True)

    def finish(j, weight, total):
        summed = jnp.dot(
            values[:, pl.ds(0, (j + 1) * block)], weight, preferred_element_type=jnp.float32
        )
        column = j * block + lax.broadcasted_iota(jnp.int32, (1, block), 1)
        live = (column >= start) & (column < end)
        for h in range(heads):
            rows, lanes = slice(h * head_dim, (h + 1) * head_dim), slice(h * block, (h + 1) * block)
            result = jnp.where(live, summed[rows, lanes] / total[:, lanes], 0.0)
            out_ref[rows, pl.ds(j * block, block)] = result.astype(jnp.bfloat16)

    blocks = steps // block
    scores, weights = {}, {}
    for j in range(blocks + 2):
        if j < blocks:
            scores[j] = score(j)
        if 0 <= j - 1 < blocks:
            weights[j - 1] = weigh(j - 1, scores.pop(j - 1))
        if j >= 2:
            finish(j - 2, *weights.pop(j - 2))


def pack_kernel(*refs):
    sources, outs, sems = refs[:4], refs[4:7], refs[7]
    span = outs[2].shape[1]
    first = pl.multiple_of(lax.axis_index("tm") // 2 * span, span)
    parts = [(n, 0, n) for n in range(4)] + [(n, 1, n) for n in range(3)] + [(3, 2, 0)]
    copies = [
        pltpu.make_async_copy(
            sources[n].at[:, pl.ds(first, span)], outs[o].at[:, pl.ds(m * span, span)], sems.at[k]
        )
        for k, (n, o, m) in enumerate(parts)
    ]
    for copy in copies:
        copy.start()
    for copy in copies:
        copy.wait()


def place(sources, refs, target, begin):
    depth, columns = refs[0].shape[0], target.shape[1]
    agent = lax.axis_index("agent")
    core = lax.axis_index("tm") % 2

    def put(ref, index):
        rows = pl.ds(pl.multiple_of(index * depth, depth), depth)
        low = min(begin, ref.shape[1] - columns)
        target[rows, :] = ref[:, low : low + columns]

    put(refs[0], agent)
    for n, pair in enumerate(sources):
        for here in (0, 1):
            for ref, offset in zip(refs[1 + 2 * n : 3 + 2 * n], (pair[here], pair[1 - here])):
                if offset is not None:
                    pl.when(core == here)(functools.partial(put, ref, agent ^ offset))


def first_kernel(sources, head_dim, bounds_ref, normed_ref, *refs):
    shards, refs = refs[: 1 + 2 * len(sources)], refs[1 + 2 * len(sources) :]
    out_ref, late, weights, held = refs[0], refs[1:4], refs[4], refs[5:]
    _, columns = weights.shape
    span = columns // 3
    place(sources, shards, weights, 0)
    for n in range(3):
        full = jnp.dot(
            normed_ref[...], weights[:, n * span : (n + 1) * span], preferred_element_type=jnp.float32
        )
        for m, target in enumerate((held[n], late[n])):
            part = full[:, m * LANES : (m + 1) * LANES]
            target[...] = (part.T if n == 2 else part).astype(jnp.bfloat16)
    attend(bounds_ref, *held, out_ref, head_dim)


def second_kernel(head_dim, bounds_ref, queries, keys, values, out_ref):
    attend(bounds_ref, queries, keys, values, out_ref, head_dim)


def transposed_dot(weight, value):
    return lax.dot_general(
        weight, value, (((0,), (0,)), ((), ())), preferred_element_type=jnp.float32
    )


def partial_kernel(sources, *refs):
    shards, refs = refs[: 1 + 2 * len(sources)], refs[1 + 2 * len(sources) :]
    here, kept_ref, given_ref, kept_weights, given_weights, weights = (
        refs[:3],
        *refs[3:7],
        refs[7],
    )
    _, columns = weights.shape
    half = columns // 2
    core, y = lax.axis_index("tm") % 2, lax.axis_index("tm") // 2
    place(sources, shards, weights, 3 * columns)
    for n, (ref, last) in enumerate(((kept_ref, kept_weights), (given_ref, given_weights))):
        lanes = pl.ds(pl.multiple_of((core ^ n) * half, half), half)
        total = None
        for m, value in enumerate(here):
            group = ((y ^ (m // 2)) * 2 + m % 2) * LANES
            rows = pl.ds(pl.multiple_of(group, LANES), LANES)
            term = transposed_dot(weights[rows, lanes], value[...])
            total = term if total is None else total + term
        ref[...] = total
        last[...] = weights[pl.ds(pl.multiple_of(((y ^ 1) * 2 + 1) * LANES, LANES), LANES), lanes]


def given_kernel(partial_ref, weights_ref, value_ref, out_ref):
    out_ref[...] = (partial_ref[...] + transposed_dot(weights_ref[...], value_ref[...])).astype(
        jnp.bfloat16
    )


def kept_kernel(partial_ref, weights_ref, value_ref, out_ref, held):
    given_kernel(partial_ref, weights_ref, value_ref, held)
    pltpu.sync_copy(held, out_ref.at[lax.axis_index("tm") % 2])


def final_kernel(received_ref, started_ref, out_ref):
    pltpu.sync_copy(received_ref, out_ref.at[1 - lax.axis_index("tm") % 2])


def fits(n_tm, n_agent, features):
    agents_here, rows_here, width = features.shape
    return (
        n_tm == 4
        and n_agent == 8
        and agents_here == 2
        and width == 4 * LANES
        and LANES % (width // HEADS) == 0
        and rows_here % LANES == 0
        and width % (16 * n_agent) == 0
        and n_tm * rows_here * width <= 2**20
    )


def split_heads(n_tm, n_agent, features, norm_gain, w_query, w_key, w_value, w_out, tracks):
    _, rows_here, width = features.shape
    head_dim = width // HEADS
    span = width // 2
    steps = n_tm * rows_here

    def across(value):
        return lax.ppermute(value, "tm", [(i, i ^ 2) for i in range(n_tm)])

    def swap(value):
        return lax.ppermute(value, "tm", [(i, i ^ 1) for i in range(n_tm)])

    def fetch(value, offsets):
        pairs = [
            (t * n_agent + (a ^ offsets[t % 2]), t * n_agent + a)
            for t in range(n_tm)
            for a in range(n_agent)
            if offsets[t % 2] is not None
        ]
        return lax.ppermute(value, ("tm", "agent"), pairs)

    vmem = pl.BlockSpec(memory_space=pltpu.VMEM)
    smem = pl.BlockSpec(memory_space=pltpu.SMEM)
    anywhere = pl.BlockSpec(memory_space=pl.ANY)

    def kernel(body, outs, args, scratch=(), specs=None, out_spec=vmem, aliases={}, **estimate):
        return pl.pallas_call(
            body,
            out_shape=[jax.ShapeDtypeStruct(shape, dtype) for shape, dtype in outs],
            in_specs=specs or [vmem] * len(args),
            out_specs=[out_spec] * len(outs),
            scratch_shapes=[pltpu.VMEM(*s) if isinstance(s, tuple) else s for s in scratch],
            input_output_aliases=aliases,
            compiler_params=params(),
            cost_estimate=cost(**estimate),
        )(*args)

    half, full = jnp.bfloat16, jnp.float32
    packed, projections, outward = kernel(
        pack_kernel,
        [((width // n_agent, n * span), half) for n in (4, 3, 1)],
        tuple(
            pltpu.with_memory_space_constraint(w, pltpu.HBM)
            for w in (w_query, w_key, w_value, w_out)
        ),
        specs=[pl.BlockSpec(memory_space=pltpu.HBM)] * 4,
        scratch=[pltpu.SemaphoreType.DMA((8,))],
        flops=0,
    )
    sources = [(6, 4), (2, 3), (None, 1), (7, 5)]
    fetched = [fetch(packed if n else projections, pair) for n, pair in enumerate(sources[:3])]
    fetched.append(fetch(fetched[0], (1, 1)))
    out_far = fetch(outward, sources[0])
    out_shards = [out_far, *fetched[1:3], fetch(out_far, (1, 1))]
    other_rows = across(features)
    beside = swap(features)
    diagonal = swap(other_rows)
    swapped = [swap(value) for value in fetched]
    swapped_out = [swap(out_shards[0]), *swapped[1:3], swap(out_shards[3])]
    normed, bounds = kernel(
        norm_kernel,
        [((steps, width), half), ((2, 8, LANES), jnp.int32)],
        (tracks, norm_gain.reshape(1, width), features, beside, other_rows, diagonal),
        specs=[smem] + [vmem] * 5,
        flops=8 * steps * width,
    )
    shards = [packed] + [v for pair in zip(fetched, swapped) for v in pair]
    head_flops = 4 * steps * steps * LANES
    heads = [((steps, LANES), half)] * 2 + [((LANES, steps), half)]
    exponentials = steps * steps * LANES // head_dim
    attended_first, *late = kernel(
        functools.partial(first_kernel, sources, head_dim),
        [((LANES, steps), half)] + heads,
        (bounds, normed, *shards),
        scratch=[((width, 3 * span), half)] + heads,
        flops=6 * steps * width * span + head_flops,
        transcendentals=exponentials,
    )
    other_first = across(attended_first)
    (attended_second,) = kernel(
        functools.partial(second_kernel, head_dim),
        [((LANES, steps), half)],
        (bounds, *late),
        flops=head_flops,
        transcendentals=exponentials,
    )
    other = across(attended_second)
    out_shards = [packed] + [v for pair in zip(out_shards, swapped_out) for v in pair]
    kept, given, kept_weights, given_weights = kernel(
        functools.partial(partial_kernel, sources),
        [((span // 2, steps), full)] * 2 + [((LANES, span // 2), half)] * 2,
        (*out_shards, attended_first, attended_second, other_first),
        scratch=[((width, span), half)],
        flops=2 * steps * width * span,
    )
    (given,) = kernel(
        given_kernel,
        [((span // 2, steps), half)],
        (given, given_weights, other),
        flops=steps * span * span,
    )
    received = swap(given)
    (started,) = kernel(
        kept_kernel,
        [((2, span // 2, steps), half)],
        (kept, kept_weights, other),
        scratch=[((span // 2, steps), half)],
        out_spec=anywhere,
        flops=steps * span * span,
    )
    (out,) = kernel(
        final_kernel,
        [((2, span // 2, steps), half)],
        (received, started),
        specs=[vmem, anywhere],
        out_spec=anywhere,
        aliases={1: 0},
        flops=0,
    )
    return out


def solution(mesh):
    in_specs = (
        P("agent", "tm", None),
        P(),
        P("agent", None),
        P("agent", None),
        P("agent", None),
        P("agent", None),
        P("agent", None),
    )
    out_specs = P("agent", "tm", None)
    n_tm, n_agent = mesh.shape["tm"], mesh.shape["agent"]

    def local(features, *rest):
        if fits(n_tm, n_agent, features):
            return split_heads(n_tm, n_agent, features, *rest)
        return body(features, *rest)

    return jax.shard_map(local, mesh=mesh, in_specs=in_specs, out_specs=out_specs, check_vma=False)
```

```python
import functools
import math

import jax
import jax.numpy as jnp
from jax import lax
from jax.experimental import pallas as pl
from jax.experimental.pallas import tpu as pltpu
from jax.sharding import PartitionSpec as P


HEADS = 8


EPSILON = 1e-05
NEGATIVE = -1e30
LANES = 128


def normalize(inputs, gain):
    values = inputs.astype(jnp.float32)
    meansq = jnp.mean(values * values, axis=-1, keepdims=True)
    return (values * lax.rsqrt(meansq + EPSILON) * gain).astype(jnp.bfloat16)


def project(normed, weight):
    return jnp.einsum("asd,de->ase", normed, weight, preferred_element_type=jnp.float32).astype(
        jnp.bfloat16
    )


def body(features, norm_gain, w_query, w_key, w_value, w_out, tracks):
    full_query, full_key, full_value, full_out = (
        lax.all_gather(w_query, "agent", axis=0, tiled=True),
        lax.all_gather(w_key, "agent", axis=0, tiled=True),
        lax.all_gather(w_value, "agent", axis=0, tiled=True),
        lax.all_gather(w_out, "agent", axis=0, tiled=True),
    )
    agents_here, rows_here, width = features.shape
    head_dim = width // HEADS
    scale = 1.0 / math.sqrt(head_dim)
    normed = normalize(features, norm_gain)
    starts = tracks[:, 0]
    ends = tracks[:, 1]
    queries = project(normed, full_query).reshape(agents_here, rows_here, HEADS, head_dim)
    first_row = lax.axis_index("tm") * rows_here
    query_pos = first_row + jnp.arange(rows_here, dtype=jnp.int32)
    row_live = (query_pos[None, :] >= starts[:, None]) & (query_pos[None, :] < ends[:, None])
    initial = (
        jnp.full((agents_here, HEADS, rows_here), NEGATIVE, jnp.float32),
        jnp.zeros((agents_here, HEADS, rows_here), jnp.float32),
        jnp.zeros((agents_here, HEADS, rows_here, head_dim), jnp.float32),
    )

    def attend(carry, key_block, value_block, key_start):
        highest, total, summed = carry
        count = key_block.shape[1]
        key_pos = key_start + jnp.arange(count, dtype=jnp.int32)
        scores = (
            jnp.einsum("athd,ashd->ahts", queries, key_block, preferred_element_type=jnp.float32)
            * scale
        )
        allowed = (
            (key_pos[None, None, :] >= starts[:, None, None])
            & (key_pos[None, None, :] <= query_pos[None, :, None])
            & row_live[:, :, None]
        )
        allowed = allowed[:, None]
        masked = jnp.where(allowed, scores, NEGATIVE)
        new_high = jnp.maximum(highest, jnp.max(masked, axis=-1))
        weights = jnp.where(allowed, jnp.exp(scores - new_high[..., None]), 0.0)
        factor = jnp.exp(highest - new_high)
        total = factor * total + jnp.sum(weights, axis=-1)
        summed = factor[..., None] * summed + jnp.einsum(
            "ahts,ashd->ahtd",
            weights.astype(jnp.bfloat16),
            value_block,
            preferred_element_type=jnp.float32,
        )
        return (new_high, total, summed)

    def sweep(carry, key_rows, value_rows, key_start):
        count = key_rows.shape[1]
        span = 512
        if span == count:
            return attend(carry, key_rows, value_rows, key_start)

        def advance(index, state):
            offset = (index * span).astype(jnp.int32)
            key_block = lax.dynamic_slice_in_dim(key_rows, offset, span, 1)
            value_block = lax.dynamic_slice_in_dim(value_rows, offset, span, 1)
            return attend(state, key_block, value_block, key_start + offset)

        return lax.fori_loop(0, count // span, advance, carry)

    piece = lax.all_gather(normed, "tm", axis=1, tiled=True)
    count = piece.shape[1]
    key_rows = project(piece, full_key).reshape(agents_here, count, HEADS, head_dim)
    value_rows = project(piece, full_value).reshape(agents_here, count, HEADS, head_dim)
    final = sweep(initial, key_rows, value_rows, jnp.int32(0))
    _, total, summed = final
    denom = jnp.where(row_live[:, None, :], total, 1.0)
    attended = summed / denom[..., None] * row_live[:, None, :, None].astype(jnp.float32)
    attended = (
        jnp.transpose(attended, (0, 2, 1, 3))
        .reshape(agents_here, rows_here, width)
        .astype(jnp.bfloat16)
    )
    projected = jnp.einsum(
        "asd,de->aes", attended, full_out, preferred_element_type=jnp.float32
    ).astype(jnp.bfloat16)
    return lax.all_to_all(projected, "tm", split_axis=1, concat_axis=2, tiled=True)


def params():
    return pltpu.CompilerParams(vmem_limit_bytes=24 * 2**20)


def cost(flops, transcendentals=0, bytes_accessed=2**20):
    return pl.CostEstimate(
        flops=flops, transcendentals=transcendentals, bytes_accessed=bytes_accessed
    )


def norm_kernel(tracks_ref, gain_ref, mine_ref, beside_ref, other_ref, diagonal_ref, *outs):
    normed_ref, bounds_ref = outs
    rows_here = mine_ref.shape[1]
    tm = lax.axis_index("tm")
    core = tm % 2
    gain = gain_ref[...]
    for k, ref in enumerate((mine_ref, beside_ref, other_ref, diagonal_ref)):
        rows = pl.ds(pl.multiple_of((tm ^ k) * rows_here, rows_here), rows_here)
        normed_ref[rows, :] = normalize(ref[core], gain)
    for n in range(2):
        bounds_ref[n] = jnp.full(bounds_ref.shape[1:], tracks_ref[core, n], jnp.int32)


def attend(bounds_ref, first, queries, keys, values, out_ref, head_dim):
    span, steps = out_ref.shape
    block = LANES
    heads = block // head_dim
    ratio = math.log2(math.e) / math.sqrt(head_dim)
    start, end = bounds_ref[0, :1, :block], bounds_ref[1, :1, :block]
    lane = lax.broadcasted_iota(jnp.int32, (block, block), 1)

    def score(t, group):
        query_block = queries[pl.ds(t, block), pl.ds(group, block)]
        one = [
            jnp.where((lane >= low) & (lane < low + head_dim), query_block, jnp.zeros_like(query_block))
            for low in range(0, block, head_dim)
        ]
        return lax.dot_general(
            keys[pl.ds(0, first + t + block), pl.ds(group, block)],
            jnp.concatenate(one, axis=0),
            (((1,), (1,)), ((), ())),
            preferred_element_type=jnp.float32,
        )

    def weigh(t, scores):
        reach = first + t + block
        key_pos = lax.broadcasted_iota(jnp.int32, (reach, block), 0)
        query_pos = first + t + lax.broadcasted_iota(jnp.int32, (reach, block), 1)
        allowed = (key_pos >= start) & (key_pos <= query_pos)
        scores = jnp.where(jnp.concatenate([allowed] * heads, axis=1), scores, NEGATIVE)
        highest = jnp.max(scores, axis=0, keepdims=True)
        weight = jnp.exp2((scores - highest) * ratio)
        return weight.astype(jnp.bfloat16), jnp.sum(weight, axis=0, keepdims=True)

    def finish(t, group, weight, total):
        summed = jnp.dot(
            values[pl.ds(group, block), pl.ds(0, first + t + block)],
            weight,
            preferred_element_type=jnp.float32,
        )
        column = first + t + lax.broadcasted_iota(jnp.int32, (1, block), 1)
        live = (column >= start) & (column < end)
        for h in range(heads):
            rows, lanes = slice(h * head_dim, (h + 1) * head_dim), slice(h * block, (h + 1) * block)
            result = jnp.where(live, summed[rows, lanes] / total[:, lanes], 0.0)
            out_ref[pl.ds(group + h * head_dim, head_dim), pl.ds(t, block)] = result.astype(
                jnp.bfloat16
            )

    tasks = [(t, group) for t in range(0, steps, block) for group in range(0, span, block)]
    scores, weights = {}, {}
    for n in range(len(tasks) + 2):
        if n < len(tasks):
            scores[n] = score(*tasks[n])
        if 0 <= n - 1 < len(tasks):
            weights[n - 1] = weigh(tasks[n - 1][0], scores.pop(n - 1))
        if n >= 2:
            finish(*tasks[n - 2], *weights.pop(n - 2))


def pack_kernel(*refs):
    sources, outs, sems = refs[:4], refs[4:7], refs[7]
    span = outs[2].shape[1]
    first = pl.multiple_of(lax.axis_index("tm") // 2 * span, span)
    parts = [(n, 0, n) for n in range(4)] + [(n, 1, n) for n in range(3)] + [(3, 2, 0)]
    copies = [
        pltpu.make_async_copy(
            sources[n].at[:, pl.ds(first, span)], outs[o].at[:, pl.ds(m * span, span)], sems.at[k]
        )
        for k, (n, o, m) in enumerate(parts)
    ]
    for copy in copies:
        copy.start()
    for copy in copies:
        copy.wait()


def place(sources, refs, target, begin):
    depth, columns = refs[0].shape[0], target.shape[1]
    agent = lax.axis_index("agent")
    core = lax.axis_index("tm") % 2

    def put(ref, index):
        rows = pl.ds(pl.multiple_of(index * depth, depth), depth)
        low = min(begin, ref.shape[1] - columns)
        target[rows, :] = ref[:, low : low + columns]

    put(refs[0], agent)
    for n, pair in enumerate(sources):
        for here in (0, 1):
            for ref, offset in zip(refs[1 + 2 * n : 3 + 2 * n], (pair[here], pair[1 - here])):
                if offset is not None:
                    pl.when(core == here)(functools.partial(put, ref, agent ^ offset))


def project_rows(normed, weights, queries, keys, values):
    span = queries.shape[1]
    for n, target in enumerate((queries, keys, values)):
        full = jnp.dot(
            normed, weights[:, n * span : (n + 1) * span], preferred_element_type=jnp.float32
        )
        target[...] = (full.T if n == 2 else full).astype(jnp.bfloat16)


def low_kernel(sources, head_dim, bounds_ref, normed_ref, *refs):
    shards, refs = refs[: 1 + 2 * len(sources)], refs[1 + 2 * len(sources) :]
    out_ref, weights, keys, values, queries = refs
    place(sources, shards, weights, 0)
    steps = out_ref.shape[1]
    project_rows(normed_ref[:steps, :], weights, queries, keys, values)
    attend(bounds_ref, 0, queries, keys, values, out_ref, head_dim)


def high_kernel(head_dim, bounds_ref, normed_ref, weights, low_keys, low_values, *refs):
    out_ref, queries, keys, values = refs
    first = low_keys.shape[0]
    keys[:first, :] = low_keys[...]
    values[:, :first] = low_values[...]
    later = pl.ds(first, keys.shape[0] - first)
    project_rows(
        normed_ref[first:, :], weights, queries, keys.at[later, :], values.at[:, later]
    )
    attend(bounds_ref, first, queries, keys, values, out_ref, head_dim)


def channel_terms(weights, ref, chip, core):
    span = ref.shape[0]
    half = weights.shape[1] // 2
    rows = pl.ds(pl.multiple_of(chip * span, span), span)
    lanes = pl.ds(pl.multiple_of(core * half, half), half)
    return lax.dot_general(
        weights[rows, lanes], ref[...], (((0,), (0,)), ((), ())), preferred_element_type=jnp.float32
    )


def low_output_kernel(sources, *refs):
    shards, refs = refs[: 1 + 2 * len(sources)], refs[1 + 2 * len(sources) :]
    mine_ref, other_ref, kept_ref, given_ref, weights = refs
    core, y = lax.axis_index("tm") % 2, lax.axis_index("tm") // 2
    place(sources, shards, weights, 3 * weights.shape[1])
    for n, ref in enumerate((kept_ref, given_ref)):
        total = channel_terms(weights, mine_ref, y, core ^ n)
        total = total + channel_terms(weights, other_ref, y ^ 1, core ^ n)
        ref[...] = total.astype(ref.dtype)


def partial_kernel(weights, mine_ref, kept_ref, given_ref):
    core, y = lax.axis_index("tm") % 2, lax.axis_index("tm") // 2
    for n, ref in enumerate((kept_ref, given_ref)):
        ref[...] = channel_terms(weights, mine_ref, y, core ^ n)


def given_kernel(weights, partial_ref, other_ref, out_ref):
    core, y = lax.axis_index("tm") % 2, lax.axis_index("tm") // 2
    total = partial_ref[...] + channel_terms(weights, other_ref, y ^ 1, core ^ 1)
    out_ref[...] = total.astype(out_ref.dtype)


def kept_kernel(weights, partial_ref, other_ref, low_ref, received_ref, out_ref, held, sems):
    core, y = lax.axis_index("tm") % 2, lax.axis_index("tm") // 2
    low, high = low_ref.shape[1], held.shape[1]
    copies = [
        pltpu.make_async_copy(low_ref, out_ref.at[core, :, pl.ds(0, low)], sems.at[0]),
        pltpu.make_async_copy(received_ref, out_ref.at[1 - core, :, pl.ds(0, low)], sems.at[1]),
        pltpu.make_async_copy(held, out_ref.at[core, :, pl.ds(low, high)], sems.at[2]),
    ]
    copies[0].start()
    copies[1].start()
    total = partial_ref[...] + channel_terms(weights, other_ref, y ^ 1, core)
    held[...] = total.astype(held.dtype)
    copies[2].start()
    for copy in copies:
        copy.wait()


def final_kernel(received_ref, begun_ref, out_ref):
    count = received_ref.shape[1]
    pltpu.sync_copy(
        received_ref,
        out_ref.at[1 - lax.axis_index("tm") % 2, :, pl.ds(out_ref.shape[2] - count, count)],
    )


def fits(n_tm, n_agent, features):
    agents_here, rows_here, width = features.shape
    return (
        n_tm == 4
        and n_agent == 8
        and agents_here == 2
        and width == 4 * LANES
        and LANES % (width // HEADS) == 0
        and rows_here % LANES == 0
        and width % (16 * n_agent) == 0
        and n_tm * rows_here * width <= 2**20
    )


def split_heads(n_tm, n_agent, features, norm_gain, w_query, w_key, w_value, w_out, tracks):
    _, rows_here, width = features.shape
    head_dim = width // HEADS
    span = width // 2
    steps = n_tm * rows_here

    def across(value):
        return lax.ppermute(value, "tm", [(i, i ^ 2) for i in range(n_tm)])

    def swap(value):
        return lax.ppermute(value, "tm", [(i, i ^ 1) for i in range(n_tm)])

    def fetch(value, offsets):
        pairs = [
            (t * n_agent + (a ^ offsets[t % 2]), t * n_agent + a)
            for t in range(n_tm)
            for a in range(n_agent)
            if offsets[t % 2] is not None
        ]
        return lax.ppermute(value, ("tm", "agent"), pairs)

    vmem = pl.BlockSpec(memory_space=pltpu.VMEM)
    smem = pl.BlockSpec(memory_space=pltpu.SMEM)
    anywhere = pl.BlockSpec(memory_space=pl.ANY)

    def kernel(body, outs, args, scratch=(), specs=None, out_spec=vmem, aliases={}, **estimate):
        return pl.pallas_call(
            body,
            out_shape=[jax.ShapeDtypeStruct(shape, dtype) for shape, dtype in outs],
            in_specs=specs or [vmem] * len(args),
            out_specs=[out_spec] * len(outs),
            scratch_shapes=[pltpu.VMEM(*s) if isinstance(s, tuple) else s for s in scratch],
            input_output_aliases=aliases,
            compiler_params=params(),
            cost_estimate=cost(**estimate),
        )(*args)

    half, full = jnp.bfloat16, jnp.float32
    packed, projections, outward = kernel(
        pack_kernel,
        [((width // n_agent, n * span), half) for n in (4, 3, 1)],
        tuple(
            pltpu.with_memory_space_constraint(w, pltpu.HBM)
            for w in (w_query, w_key, w_value, w_out)
        ),
        specs=[pl.BlockSpec(memory_space=pltpu.HBM)] * 4,
        scratch=[pltpu.SemaphoreType.DMA((8,))],
        flops=0,
    )
    sources = [(6, 4), (2, 3), (None, 1), (7, 5)]
    fetched = [fetch(packed if n else projections, pair) for n, pair in enumerate(sources[:3])]
    fetched.append(fetch(fetched[0], (1, 1)))
    out_far = fetch(outward, sources[0])
    out_shards = [out_far, *fetched[1:3], fetch(out_far, (1, 1))]
    other_rows = across(features)
    beside = swap(features)
    diagonal = swap(other_rows)
    swapped = [swap(value) for value in fetched]
    swapped_out = [swap(out_shards[0]), *swapped[1:3], swap(out_shards[3])]
    normed, bounds = kernel(
        norm_kernel,
        [((steps, width), half), ((2, 8, LANES), jnp.int32)],
        (tracks, norm_gain.reshape(1, width), features, beside, other_rows, diagonal),
        specs=[smem] + [vmem] * 5,
        flops=8 * steps * width,
    )
    shards = [packed] + [v for pair in zip(fetched, swapped) for v in pair]
    low = steps // 2
    high = steps - low
    exponentials = span // head_dim
    low_attended, weights, *low_held = kernel(
        functools.partial(low_kernel, sources, head_dim),
        [
            ((span, low), half),
            ((width, 3 * span), half),
            ((low, span), half),
            ((span, low), half),
        ],
        (bounds, normed, *shards),
        scratch=[((low, span), half)],
        flops=6 * low * width * span + 4 * low * low * span,
        transcendentals=low * low * exponentials,
    )
    low_other = across(low_attended)
    (high_attended,) = kernel(
        functools.partial(high_kernel, head_dim),
        [((span, high), half)],
        (bounds, normed, weights, *low_held),
        scratch=[((high, span), half), ((steps, span), half), ((span, steps), half)],
        flops=6 * high * width * span + 4 * high * steps * span,
        transcendentals=high * steps * exponentials,
    )
    high_other = across(high_attended)
    out_shards = [packed] + [v for pair in zip(out_shards, swapped_out) for v in pair]
    low_kept, low_given, out_weights = kernel(
        functools.partial(low_output_kernel, sources),
        [((span // 2, low), half)] * 2 + [((width, span), half)],
        (*out_shards, low_attended, low_other),
        flops=4 * low * span * span,
    )
    low_received = swap(low_given)
    kept, given = kernel(
        partial_kernel,
        [((span // 2, high), full)] * 2,
        (out_weights, high_attended),
        flops=2 * high * span * span,
    )
    (given,) = kernel(
        given_kernel,
        [((span // 2, high), half)],
        (out_weights, given, high_other),
        flops=high * span * span,
    )
    received = swap(given)
    (begun,) = kernel(
        kept_kernel,
        [((2, span // 2, steps), half)],
        (out_weights, kept, high_other, low_kept, low_received),
        scratch=[((span // 2, high), half), pltpu.SemaphoreType.DMA((3,))],
        out_spec=anywhere,
        flops=high * span * span,
    )
    (out,) = kernel(
        final_kernel,
        [((2, span // 2, steps), half)],
        (received, begun),
        specs=[vmem, anywhere],
        out_spec=anywhere,
        aliases={1: 0},
        flops=0,
    )
    return out


def solution(mesh):
    in_specs = (
        P("agent", "tm", None),
        P(),
        P("agent", None),
        P("agent", None),
        P("agent", None),
        P("agent", None),
        P("agent", None),
    )
    out_specs = P("agent", "tm", None)
    n_tm, n_agent = mesh.shape["tm"], mesh.shape["agent"]

    def local(features, *rest):
        if fits(n_tm, n_agent, features):
            return split_heads(n_tm, n_agent, features, *rest)
        return body(features, *rest)

    return jax.shard_map(local, mesh=mesh, in_specs=in_specs, out_specs=out_specs, check_vma=False)
```

```python
import functools
import math

import jax
import jax.numpy as jnp
from jax import lax
from jax.experimental import pallas as pl
from jax.experimental.pallas import tpu as pltpu
from jax.sharding import PartitionSpec as P


HEADS = 8


EPSILON = 1e-05
NEGATIVE = -1e30
LANES = 128


def normalize(inputs, gain):
    values = inputs.astype(jnp.float32)
    meansq = jnp.mean(values * values, axis=-1, keepdims=True)
    return (values * lax.rsqrt(meansq + EPSILON) * gain).astype(jnp.bfloat16)


def project(normed, weight):
    return jnp.einsum("asd,de->ase", normed, weight, preferred_element_type=jnp.float32).astype(
        jnp.bfloat16
    )


def body(features, norm_gain, w_query, w_key, w_value, w_out, tracks):
    full_query, full_key, full_value, full_out = (
        lax.all_gather(w_query, "agent", axis=0, tiled=True),
        lax.all_gather(w_key, "agent", axis=0, tiled=True),
        lax.all_gather(w_value, "agent", axis=0, tiled=True),
        lax.all_gather(w_out, "agent", axis=0, tiled=True),
    )
    agents_here, rows_here, width = features.shape
    head_dim = width // HEADS
    scale = 1.0 / math.sqrt(head_dim)
    normed = normalize(features, norm_gain)
    starts = tracks[:, 0]
    ends = tracks[:, 1]
    queries = project(normed, full_query).reshape(agents_here, rows_here, HEADS, head_dim)
    first_row = lax.axis_index("tm") * rows_here
    query_pos = first_row + jnp.arange(rows_here, dtype=jnp.int32)
    row_live = (query_pos[None, :] >= starts[:, None]) & (query_pos[None, :] < ends[:, None])
    initial = (
        jnp.full((agents_here, HEADS, rows_here), NEGATIVE, jnp.float32),
        jnp.zeros((agents_here, HEADS, rows_here), jnp.float32),
        jnp.zeros((agents_here, HEADS, rows_here, head_dim), jnp.float32),
    )

    def attend(carry, key_block, value_block, key_start):
        highest, total, summed = carry
        count = key_block.shape[1]
        key_pos = key_start + jnp.arange(count, dtype=jnp.int32)
        scores = (
            jnp.einsum("athd,ashd->ahts", queries, key_block, preferred_element_type=jnp.float32)
            * scale
        )
        allowed = (
            (key_pos[None, None, :] >= starts[:, None, None])
            & (key_pos[None, None, :] <= query_pos[None, :, None])
            & row_live[:, :, None]
        )
        allowed = allowed[:, None]
        masked = jnp.where(allowed, scores, NEGATIVE)
        new_high = jnp.maximum(highest, jnp.max(masked, axis=-1))
        weights = jnp.where(allowed, jnp.exp(scores - new_high[..., None]), 0.0)
        factor = jnp.exp(highest - new_high)
        total = factor * total + jnp.sum(weights, axis=-1)
        summed = factor[..., None] * summed + jnp.einsum(
            "ahts,ashd->ahtd",
            weights.astype(jnp.bfloat16),
            value_block,
            preferred_element_type=jnp.float32,
        )
        return (new_high, total, summed)

    def sweep(carry, key_rows, value_rows, key_start):
        count = key_rows.shape[1]
        span = 512
        if span == count:
            return attend(carry, key_rows, value_rows, key_start)

        def advance(index, state):
            offset = (index * span).astype(jnp.int32)
            key_block = lax.dynamic_slice_in_dim(key_rows, offset, span, 1)
            value_block = lax.dynamic_slice_in_dim(value_rows, offset, span, 1)
            return attend(state, key_block, value_block, key_start + offset)

        return lax.fori_loop(0, count // span, advance, carry)

    piece = lax.all_gather(normed, "tm", axis=1, tiled=True)
    count = piece.shape[1]
    key_rows = project(piece, full_key).reshape(agents_here, count, HEADS, head_dim)
    value_rows = project(piece, full_value).reshape(agents_here, count, HEADS, head_dim)
    final = sweep(initial, key_rows, value_rows, jnp.int32(0))
    _, total, summed = final
    denom = jnp.where(row_live[:, None, :], total, 1.0)
    attended = summed / denom[..., None] * row_live[:, None, :, None].astype(jnp.float32)
    attended = (
        jnp.transpose(attended, (0, 2, 1, 3))
        .reshape(agents_here, rows_here, width)
        .astype(jnp.bfloat16)
    )
    projected = jnp.einsum(
        "asd,de->aes", attended, full_out, preferred_element_type=jnp.float32
    ).astype(jnp.bfloat16)
    return lax.all_to_all(projected, "tm", split_axis=1, concat_axis=2, tiled=True)


def params():
    return pltpu.CompilerParams(vmem_limit_bytes=24 * 2**20)


def cost(flops, transcendentals=0, bytes_accessed=2**20):
    return pl.CostEstimate(
        flops=flops, transcendentals=transcendentals, bytes_accessed=bytes_accessed
    )


def norm_kernel(tracks_ref, gain_ref, mine_ref, beside_ref, other_ref, diagonal_ref, *outs):
    normed_ref, bounds_ref = outs
    rows_here = mine_ref.shape[1]
    tm = lax.axis_index("tm")
    core = tm % 2
    gain = gain_ref[...]
    for k, ref in enumerate((mine_ref, beside_ref, other_ref, diagonal_ref)):
        rows = pl.ds(pl.multiple_of((tm ^ k) * rows_here, rows_here), rows_here)
        normed_ref[rows, :] = normalize(ref[core], gain)
    for n in range(2):
        bounds_ref[n] = jnp.full(bounds_ref.shape[1:], tracks_ref[core, n], jnp.int32)


def attend(bounds_ref, first, queries, keys, values, out_ref, head_dim):
    span, steps = out_ref.shape
    block = LANES
    heads = block // head_dim
    ratio = math.log2(math.e) / math.sqrt(head_dim)
    start, end = bounds_ref[0, :1, :block], bounds_ref[1, :1, :block]
    lane = lax.broadcasted_iota(jnp.int32, (block, block), 1)

    def score(t, group):
        query_block = queries[pl.ds(t, block), pl.ds(group, block)]
        one = [
            jnp.where((lane >= low) & (lane < low + head_dim), query_block, jnp.zeros_like(query_block))
            for low in range(0, block, head_dim)
        ]
        return lax.dot_general(
            keys[pl.ds(0, first + t + block), pl.ds(group, block)],
            jnp.concatenate(one, axis=0),
            (((1,), (1,)), ((), ())),
            preferred_element_type=jnp.float32,
        )

    def weigh(t, scores):
        reach = first + t + block
        key_pos = lax.broadcasted_iota(jnp.int32, (reach, block), 0)
        query_pos = first + t + lax.broadcasted_iota(jnp.int32, (reach, block), 1)
        allowed = (key_pos >= start) & (key_pos <= query_pos)
        scores = jnp.where(jnp.concatenate([allowed] * heads, axis=1), scores, NEGATIVE)
        highest = jnp.max(scores, axis=0, keepdims=True)
        weight = jnp.exp2((scores - highest) * ratio)
        return weight.astype(jnp.bfloat16), jnp.sum(weight, axis=0, keepdims=True)

    def finish(t, group, weight, total):
        summed = jnp.dot(
            values[pl.ds(group, block), pl.ds(0, first + t + block)],
            weight,
            preferred_element_type=jnp.float32,
        )
        column = first + t + lax.broadcasted_iota(jnp.int32, (1, block), 1)
        live = (column >= start) & (column < end)
        for h in range(heads):
            rows, lanes = slice(h * head_dim, (h + 1) * head_dim), slice(h * block, (h + 1) * block)
            result = jnp.where(live, summed[rows, lanes] / total[:, lanes], 0.0)
            out_ref[pl.ds(group + h * head_dim, head_dim), pl.ds(t, block)] = result.astype(
                jnp.bfloat16
            )

    tasks = [(t, group) for t in range(0, steps, block) for group in range(0, span, block)]
    scores, weights = {}, {}
    for n in range(len(tasks) + 2):
        if n < len(tasks):
            scores[n] = score(*tasks[n])
        if 0 <= n - 1 < len(tasks):
            weights[n - 1] = weigh(tasks[n - 1][0], scores.pop(n - 1))
        if n >= 2:
            finish(*tasks[n - 2], *weights.pop(n - 2))


def pack_kernel(*refs):
    sources, out_ref, sems = refs[:-2], refs[-2], refs[-1]
    span = out_ref.shape[1] // len(sources)
    first = pl.multiple_of(lax.axis_index("tm") // 2 * span, span)
    copies = [
        pltpu.make_async_copy(
            ref.at[:, pl.ds(first, span)], out_ref.at[:, pl.ds(n * span, span)], sems.at[n]
        )
        for n, ref in enumerate(sources)
    ]
    for copy in copies:
        copy.start()
    for copy in copies:
        copy.wait()


def place(sources, refs, target, begin):
    depth, columns = refs[0].shape[0], target.shape[1]
    agent = lax.axis_index("agent")
    core = lax.axis_index("tm") % 2

    def put(ref, index):
        rows = pl.ds(pl.multiple_of(index * depth, depth), depth)
        low = min(begin, ref.shape[1] - columns)
        target[rows, :] = ref[:, low : low + columns]

    put(refs[0], agent)
    for n, pair in enumerate(sources):
        for here in (0, 1):
            for ref, offset in zip(refs[1 + 2 * n : 3 + 2 * n], (pair[here], pair[1 - here])):
                if offset is not None:
                    pl.when(core == here)(functools.partial(put, ref, agent ^ offset))


def project_rows(normed, weights, queries, keys, values):
    span = queries.shape[1]
    for n, target in enumerate((queries, keys, values)):
        full = jnp.dot(
            normed, weights[:, n * span : (n + 1) * span], preferred_element_type=jnp.float32
        )
        target[...] = (full.T if n == 2 else full).astype(jnp.bfloat16)


def low_kernel(sources, head_dim, bounds_ref, normed_ref, *refs):
    shards, refs = refs[: 1 + 2 * len(sources)], refs[1 + 2 * len(sources) :]
    out_ref, weights, keys, values, queries = refs
    place(sources, shards, weights, 0)
    steps = out_ref.shape[1]
    project_rows(normed_ref[:steps, :], weights, queries, keys, values)
    attend(bounds_ref, 0, queries, keys, values, out_ref, head_dim)


def high_kernel(head_dim, bounds_ref, normed_ref, weights, low_keys, low_values, *refs):
    out_ref, queries, keys, values = refs
    first = low_keys.shape[0]
    keys[:first, :] = low_keys[...]
    values[:, :first] = low_values[...]
    later = pl.ds(first, keys.shape[0] - first)
    project_rows(
        normed_ref[first:, :], weights, queries, keys.at[later, :], values.at[:, later]
    )
    attend(bounds_ref, first, queries, keys, values, out_ref, head_dim)


def channel_terms(weights, ref, chip, core):
    span = ref.shape[0]
    half = weights.shape[1] // 2
    rows = pl.ds(pl.multiple_of(chip * span, span), span)
    lanes = pl.ds(pl.multiple_of(core * half, half), half)
    return lax.dot_general(
        weights[rows, lanes], ref[...], (((0,), (0,)), ((), ())), preferred_element_type=jnp.float32
    )


def low_output_kernel(sources, *refs):
    shards, refs = refs[: 1 + 2 * len(sources)], refs[1 + 2 * len(sources) :]
    mine_ref, other_ref, kept_ref, given_ref, weights = refs
    core, y = lax.axis_index("tm") % 2, lax.axis_index("tm") // 2
    place(sources, shards, weights, 3 * weights.shape[1])
    for n, ref in enumerate((kept_ref, given_ref)):
        total = channel_terms(weights, mine_ref, y, core ^ n)
        total = total + channel_terms(weights, other_ref, y ^ 1, core ^ n)
        ref[...] = total.astype(ref.dtype)


def partial_kernel(weights, mine_ref, kept_ref, given_ref):
    core, y = lax.axis_index("tm") % 2, lax.axis_index("tm") // 2
    for n, ref in enumerate((kept_ref, given_ref)):
        ref[...] = channel_terms(weights, mine_ref, y, core ^ n)


def given_kernel(weights, partial_ref, other_ref, out_ref):
    core, y = lax.axis_index("tm") % 2, lax.axis_index("tm") // 2
    total = partial_ref[...] + channel_terms(weights, other_ref, y ^ 1, core ^ 1)
    out_ref[...] = total.astype(out_ref.dtype)


def kept_kernel(weights, partial_ref, other_ref, low_ref, received_ref, out_ref, held, sems):
    core, y = lax.axis_index("tm") % 2, lax.axis_index("tm") // 2
    low, high = low_ref.shape[1], held.shape[1]
    copies = [
        pltpu.make_async_copy(low_ref, out_ref.at[core, :, pl.ds(0, low)], sems.at[0]),
        pltpu.make_async_copy(received_ref, out_ref.at[1 - core, :, pl.ds(0, low)], sems.at[1]),
        pltpu.make_async_copy(held, out_ref.at[core, :, pl.ds(low, high)], sems.at[2]),
    ]
    copies[0].start()
    copies[1].start()
    total = partial_ref[...] + channel_terms(weights, other_ref, y ^ 1, core)
    held[...] = total.astype(held.dtype)
    copies[2].start()
    for copy in copies:
        copy.wait()


def fits(n_tm, n_agent, features):
    agents_here, rows_here, width = features.shape
    return (
        n_tm == 4
        and n_agent == 8
        and agents_here == 2
        and width == 4 * LANES
        and LANES % (width // HEADS) == 0
        and rows_here % LANES == 0
        and width % (16 * n_agent) == 0
        and n_tm * rows_here * width <= 2**20
    )


def split_heads(n_tm, n_agent, features, norm_gain, w_query, w_key, w_value, w_out, tracks):
    _, rows_here, width = features.shape
    head_dim = width // HEADS
    span = width // 2
    steps = n_tm * rows_here

    def across(value):
        return lax.ppermute(value, "tm", [(i, i ^ 2) for i in range(n_tm)])

    def swap(value):
        return lax.ppermute(value, "tm", [(i, i ^ 1) for i in range(n_tm)])

    def fetch(value, offsets):
        pairs = [
            (t * n_agent + (a ^ offsets[t % 2]), t * n_agent + a)
            for t in range(n_tm)
            for a in range(n_agent)
            if offsets[t % 2] is not None
        ]
        return lax.ppermute(value, ("tm", "agent"), pairs)

    vmem = pl.BlockSpec(memory_space=pltpu.VMEM)
    smem = pl.BlockSpec(memory_space=pltpu.SMEM)
    anywhere = pl.BlockSpec(memory_space=pl.ANY)

    def kernel(body, outs, args, scratch=(), specs=None, out_spec=vmem, aliases={}, **estimate):
        return pl.pallas_call(
            body,
            out_shape=[jax.ShapeDtypeStruct(shape, dtype) for shape, dtype in outs],
            in_specs=specs or [vmem] * len(args),
            out_specs=[out_spec] * len(outs),
            scratch_shapes=[pltpu.VMEM(*s) if isinstance(s, tuple) else s for s in scratch],
            input_output_aliases=aliases,
            compiler_params=params(),
            cost_estimate=cost(**estimate),
        )(*args)

    half, full = jnp.bfloat16, jnp.float32
    (packed,) = kernel(
        pack_kernel,
        [((width // n_agent, 4 * span), half)],
        tuple(
            pltpu.with_memory_space_constraint(w, pltpu.HBM)
            for w in (w_query, w_key, w_value, w_out)
        ),
        specs=[pl.BlockSpec(memory_space=pltpu.HBM)] * 4,
        scratch=[pltpu.SemaphoreType.DMA((4,))],
        flops=0,
    )
    projections, outward = packed[:, : 3 * span], packed[:, 3 * span :]
    sources = [(6, 4), (1, 3), (None, 2), (7, 5)]
    fetched = [fetch(packed if n else projections, pair) for n, pair in enumerate(sources[:3])]
    fetched.append(fetch(fetched[0], (1, 1)))
    out_far = fetch(outward, sources[0])
    out_shards = [out_far, *fetched[1:3], fetch(out_far, (1, 1))]
    other_rows = across(features)
    beside = swap(features)
    diagonal = swap(other_rows)
    swapped = [swap(value) for value in fetched]
    swapped_out = [swap(out_shards[0]), *swapped[1:3], swap(out_shards[3])]
    normed, bounds = kernel(
        norm_kernel,
        [((steps, width), half), ((2, 8, LANES), jnp.int32)],
        (tracks, norm_gain.reshape(1, width), features, beside, other_rows, diagonal),
        specs=[smem] + [vmem] * 5,
        flops=8 * steps * width,
    )
    shards = [packed] + [v for pair in zip(fetched, swapped) for v in pair]
    low = steps // 2
    high = steps - low
    exponentials = span // head_dim
    low_attended, weights, *low_held = kernel(
        functools.partial(low_kernel, sources, head_dim),
        [
            ((span, low), half),
            ((width, 3 * span), half),
            ((low, span), half),
            ((span, low), half),
        ],
        (bounds, normed, *shards),
        scratch=[((low, span), half)],
        flops=6 * low * width * span + 4 * low * low * span,
        transcendentals=low * low * exponentials,
    )
    low_other = across(low_attended)
    (high_attended,) = kernel(
        functools.partial(high_kernel, head_dim),
        [((span, high), half)],
        (bounds, normed, weights, *low_held),
        scratch=[((high, span), half), ((steps, span), half), ((span, steps), half)],
        flops=6 * high * width * span + 4 * high * steps * span,
        transcendentals=high * steps * exponentials,
    )
    high_other = across(high_attended)
    out_shards = [packed] + [v for pair in zip(out_shards, swapped_out) for v in pair]
    low_kept, low_given, out_weights = kernel(
        functools.partial(low_output_kernel, sources),
        [((span // 2, low), half)] * 2 + [((width, span), half)],
        (*out_shards, low_attended, low_other),
        flops=4 * low * span * span,
    )
    low_received = swap(low_given)
    kept, given = kernel(
        partial_kernel,
        [((span // 2, high), full)] * 2,
        (out_weights, high_attended),
        flops=2 * high * span * span,
    )
    (given,) = kernel(
        given_kernel,
        [((span // 2, high), half)],
        (out_weights, given, high_other),
        flops=high * span * span,
    )
    received = swap(given)
    (begun,) = kernel(
        kept_kernel,
        [((2, span // 2, steps), half)],
        (out_weights, kept, high_other, low_kept, low_received),
        scratch=[((span // 2, high), half), pltpu.SemaphoreType.DMA((3,))],
        out_spec=anywhere,
        flops=high * span * span,
    )
    out = lax.dynamic_update_slice(
        begun, received[None], (1 - lax.axis_index("tm") % 2, 0, low)
    )
    return out


def solution(mesh):
    in_specs = (
        P("agent", "tm", None),
        P(),
        P("agent", None),
        P("agent", None),
        P("agent", None),
        P("agent", None),
        P("agent", None),
    )
    out_specs = P("agent", "tm", None)
    n_tm, n_agent = mesh.shape["tm"], mesh.shape["agent"]

    def local(features, *rest):
        if fits(n_tm, n_agent, features):
            return split_heads(n_tm, n_agent, features, *rest)
        return body(features, *rest)

    return jax.shard_map(local, mesh=mesh, in_specs=in_specs, out_specs=out_specs, check_vma=False)
```

```python
import functools
import math

import jax
import jax.numpy as jnp
from jax import lax
from jax.experimental import pallas as pl
from jax.experimental.pallas import tpu as pltpu
from jax.sharding import PartitionSpec as P


HEADS = 8


EPSILON = 1e-05
NEGATIVE = -1e30
LANES = 128


def normalize(inputs, gain):
    values = inputs.astype(jnp.float32)
    meansq = jnp.mean(values * values, axis=-1, keepdims=True)
    return (values * lax.rsqrt(meansq + EPSILON) * gain).astype(jnp.bfloat16)


def project(normed, weight):
    return jnp.einsum("asd,de->ase", normed, weight, preferred_element_type=jnp.float32).astype(
        jnp.bfloat16
    )


def body(features, norm_gain, w_query, w_key, w_value, w_out, tracks):
    full_query, full_key, full_value, full_out = (
        lax.all_gather(w_query, "agent", axis=0, tiled=True),
        lax.all_gather(w_key, "agent", axis=0, tiled=True),
        lax.all_gather(w_value, "agent", axis=0, tiled=True),
        lax.all_gather(w_out, "agent", axis=0, tiled=True),
    )
    agents_here, rows_here, width = features.shape
    head_dim = width // HEADS
    scale = 1.0 / math.sqrt(head_dim)
    normed = normalize(features, norm_gain)
    starts = tracks[:, 0]
    ends = tracks[:, 1]
    queries = project(normed, full_query).reshape(agents_here, rows_here, HEADS, head_dim)
    first_row = lax.axis_index("tm") * rows_here
    query_pos = first_row + jnp.arange(rows_here, dtype=jnp.int32)
    row_live = (query_pos[None, :] >= starts[:, None]) & (query_pos[None, :] < ends[:, None])
    initial = (
        jnp.full((agents_here, HEADS, rows_here), NEGATIVE, jnp.float32),
        jnp.zeros((agents_here, HEADS, rows_here), jnp.float32),
        jnp.zeros((agents_here, HEADS, rows_here, head_dim), jnp.float32),
    )

    def attend(carry, key_block, value_block, key_start):
        highest, total, summed = carry
        count = key_block.shape[1]
        key_pos = key_start + jnp.arange(count, dtype=jnp.int32)
        scores = (
            jnp.einsum("athd,ashd->ahts", queries, key_block, preferred_element_type=jnp.float32)
            * scale
        )
        allowed = (
            (key_pos[None, None, :] >= starts[:, None, None])
            & (key_pos[None, None, :] <= query_pos[None, :, None])
            & row_live[:, :, None]
        )
        allowed = allowed[:, None]
        masked = jnp.where(allowed, scores, NEGATIVE)
        new_high = jnp.maximum(highest, jnp.max(masked, axis=-1))
        weights = jnp.where(allowed, jnp.exp(scores - new_high[..., None]), 0.0)
        factor = jnp.exp(highest - new_high)
        total = factor * total + jnp.sum(weights, axis=-1)
        summed = factor[..., None] * summed + jnp.einsum(
            "ahts,ashd->ahtd",
            weights.astype(jnp.bfloat16),
            value_block,
            preferred_element_type=jnp.float32,
        )
        return (new_high, total, summed)

    def sweep(carry, key_rows, value_rows, key_start):
        count = key_rows.shape[1]
        span = 512
        if span == count:
            return attend(carry, key_rows, value_rows, key_start)

        def advance(index, state):
            offset = (index * span).astype(jnp.int32)
            key_block = lax.dynamic_slice_in_dim(key_rows, offset, span, 1)
            value_block = lax.dynamic_slice_in_dim(value_rows, offset, span, 1)
            return attend(state, key_block, value_block, key_start + offset)

        return lax.fori_loop(0, count // span, advance, carry)

    piece = lax.all_gather(normed, "tm", axis=1, tiled=True)
    count = piece.shape[1]
    key_rows = project(piece, full_key).reshape(agents_here, count, HEADS, head_dim)
    value_rows = project(piece, full_value).reshape(agents_here, count, HEADS, head_dim)
    final = sweep(initial, key_rows, value_rows, jnp.int32(0))
    _, total, summed = final
    denom = jnp.where(row_live[:, None, :], total, 1.0)
    attended = summed / denom[..., None] * row_live[:, None, :, None].astype(jnp.float32)
    attended = (
        jnp.transpose(attended, (0, 2, 1, 3))
        .reshape(agents_here, rows_here, width)
        .astype(jnp.bfloat16)
    )
    projected = jnp.einsum(
        "asd,de->aes", attended, full_out, preferred_element_type=jnp.float32
    ).astype(jnp.bfloat16)
    return lax.all_to_all(projected, "tm", split_axis=1, concat_axis=2, tiled=True)


def params():
    return pltpu.CompilerParams(vmem_limit_bytes=24 * 2**20)


def cost(flops, transcendentals=0, bytes_accessed=2**20):
    return pl.CostEstimate(
        flops=flops, transcendentals=transcendentals, bytes_accessed=bytes_accessed
    )


def norm_kernel(tracks_ref, gain_ref, mine_ref, beside_ref, other_ref, diagonal_ref, *outs):
    normed_ref, bounds_ref = outs
    rows_here = mine_ref.shape[1]
    tm = lax.axis_index("tm")
    core = tm % 2
    gain = gain_ref[...]
    for k, ref in enumerate((mine_ref, beside_ref, other_ref, diagonal_ref)):
        rows = pl.ds(pl.multiple_of((tm ^ k) * rows_here, rows_here), rows_here)
        normed_ref[rows, :] = normalize(ref[core], gain)
    for n in range(2):
        bounds_ref[n] = jnp.full(bounds_ref.shape[1:], tracks_ref[core, n], jnp.int32)


def attend(bounds_ref, first, queries, keys, values, out_ref, head_dim):
    span, steps = out_ref.shape
    block = LANES
    heads = block // head_dim
    ratio = math.log2(math.e) / math.sqrt(head_dim)
    start, end = bounds_ref[0, :1, :block], bounds_ref[1, :1, :block]
    lane = lax.broadcasted_iota(jnp.int32, (block, block), 1)

    def score(t, group):
        query_block = queries[pl.ds(t, block), pl.ds(group, block)]
        one = [
            jnp.where((lane >= low) & (lane < low + head_dim), query_block, jnp.zeros_like(query_block))
            for low in range(0, block, head_dim)
        ]
        return lax.dot_general(
            keys[pl.ds(0, first + t + block), pl.ds(group, block)],
            jnp.concatenate(one, axis=0),
            (((1,), (1,)), ((), ())),
            preferred_element_type=jnp.float32,
        )

    def weigh(t, scores):
        reach = first + t + block
        key_pos = lax.broadcasted_iota(jnp.int32, (reach, block), 0)
        query_pos = first + t + lax.broadcasted_iota(jnp.int32, (reach, block), 1)
        allowed = (key_pos >= start) & (key_pos <= query_pos)
        scores = jnp.where(jnp.concatenate([allowed] * heads, axis=1), scores, NEGATIVE)
        highest = jnp.max(scores, axis=0, keepdims=True)
        weight = jnp.exp2((scores - highest) * ratio)
        return weight.astype(jnp.bfloat16), jnp.sum(weight, axis=0, keepdims=True)

    def finish(t, group, weight, total):
        summed = jnp.dot(
            values[pl.ds(group, block), pl.ds(0, first + t + block)],
            weight,
            preferred_element_type=jnp.float32,
        )
        column = first + t + lax.broadcasted_iota(jnp.int32, (1, block), 1)
        live = (column >= start) & (column < end)
        for h in range(heads):
            rows, lanes = slice(h * head_dim, (h + 1) * head_dim), slice(h * block, (h + 1) * block)
            result = jnp.where(live, summed[rows, lanes] / total[:, lanes], 0.0)
            out_ref[pl.ds(group + h * head_dim, head_dim), pl.ds(t, block)] = result.astype(
                jnp.bfloat16
            )

    tasks = [(t, group) for t in range(0, steps, block) for group in range(0, span, block)]
    scores, weights = {}, {}
    for n in range(len(tasks) + 2):
        if n < len(tasks):
            scores[n] = score(*tasks[n])
        if 0 <= n - 1 < len(tasks):
            weights[n - 1] = weigh(tasks[n - 1][0], scores.pop(n - 1))
        if n >= 2:
            finish(*tasks[n - 2], *weights.pop(n - 2))


def pack_kernel(*refs):
    sources, out_ref, sems = refs[:-2], refs[-2], refs[-1]
    span = out_ref.shape[1] // len(sources)
    first = pl.multiple_of(lax.axis_index("tm") // 2 * span, span)
    copies = [
        pltpu.make_async_copy(
            ref.at[:, pl.ds(first, span)], out_ref.at[:, pl.ds(n * span, span)], sems.at[n]
        )
        for n, ref in enumerate(sources)
    ]
    for copy in copies:
        copy.start()
    for copy in copies:
        copy.wait()


def place(sources, refs, target, begin):
    depth, columns = refs[0].shape[0], target.shape[1]
    agent = lax.axis_index("agent")
    core = lax.axis_index("tm") % 2

    def read(ref):
        low = min(begin, ref.shape[1] - columns)
        return ref[:, low : low + columns]

    def put(value, offset):
        rows = pl.ds(pl.multiple_of((agent ^ offset) * depth, depth), depth)
        target[rows, :] = value

    put(read(refs[0]), 0)
    for n, (first, second) in enumerate(sources):
        fetched, swapped = refs[1 + 2 * n : 3 + 2 * n]
        if first is None:
            put(jnp.where(core == 0, read(swapped), read(fetched)), second)
        else:
            put(read(fetched), jnp.where(core == 0, first, second))
            put(read(swapped), jnp.where(core == 0, second, first))


def project_rows(normed, weights, queries, keys, values):
    span = queries.shape[1]
    for n, target in enumerate((queries, keys, values)):
        full = jnp.dot(
            normed, weights[:, n * span : (n + 1) * span], preferred_element_type=jnp.float32
        )
        target[...] = (full.T if n == 2 else full).astype(jnp.bfloat16)


def low_kernel(sources, head_dim, bounds_ref, normed_ref, *refs):
    shards, refs = refs[: 1 + 2 * len(sources)], refs[1 + 2 * len(sources) :]
    out_ref, weights, keys, values, queries = refs
    place(sources, shards, weights, 0)
    steps = out_ref.shape[1]
    project_rows(normed_ref[:steps, :], weights, queries, keys, values)
    attend(bounds_ref, 0, queries, keys, values, out_ref, head_dim)


def high_kernel(head_dim, bounds_ref, normed_ref, weights, low_keys, low_values, *refs):
    out_ref, queries, keys, values = refs
    first = low_keys.shape[0]
    keys[:first, :] = low_keys[...]
    values[:, :first] = low_values[...]
    later = pl.ds(first, keys.shape[0] - first)
    project_rows(
        normed_ref[first:, :], weights, queries, keys.at[later, :], values.at[:, later]
    )
    attend(bounds_ref, first, queries, keys, values, out_ref, head_dim)


def channel_terms(weights, ref, chip, core):
    span = ref.shape[0]
    half = weights.shape[1] // 2
    rows = pl.ds(pl.multiple_of(chip * span, span), span)
    lanes = pl.ds(pl.multiple_of(core * half, half), half)
    return lax.dot_general(
        weights[rows, lanes], ref[...], (((0,), (0,)), ((), ())), preferred_element_type=jnp.float32
    )


def low_output_kernel(sources, *refs):
    shards, refs = refs[: 1 + 2 * len(sources)], refs[1 + 2 * len(sources) :]
    mine_ref, other_ref, kept_ref, given_ref, weights = refs
    core, y = lax.axis_index("tm") % 2, lax.axis_index("tm") // 2
    place(sources, shards, weights, 3 * weights.shape[1])
    for n, ref in enumerate((kept_ref, given_ref)):
        total = channel_terms(weights, mine_ref, y, core ^ n)
        total = total + channel_terms(weights, other_ref, y ^ 1, core ^ n)
        ref[...] = total.astype(ref.dtype)


def partial_kernel(weights, mine_ref, kept_ref, given_ref):
    core, y = lax.axis_index("tm") % 2, lax.axis_index("tm") // 2
    for n, ref in enumerate((kept_ref, given_ref)):
        ref[...] = channel_terms(weights, mine_ref, y, core ^ n)


def given_kernel(weights, partial_ref, other_ref, out_ref):
    core, y = lax.axis_index("tm") % 2, lax.axis_index("tm") // 2
    total = partial_ref[...] + channel_terms(weights, other_ref, y ^ 1, core ^ 1)
    out_ref[...] = total.astype(out_ref.dtype)


def kept_kernel(weights, partial_ref, other_ref, low_ref, received_ref, out_ref, held, sems):
    core, y = lax.axis_index("tm") % 2, lax.axis_index("tm") // 2
    low, high = low_ref.shape[1], held.shape[1]
    copies = [
        pltpu.make_async_copy(low_ref, out_ref.at[core, :, pl.ds(0, low)], sems.at[0]),
        pltpu.make_async_copy(received_ref, out_ref.at[1 - core, :, pl.ds(0, low)], sems.at[1]),
        pltpu.make_async_copy(held, out_ref.at[core, :, pl.ds(low, high)], sems.at[2]),
    ]
    copies[0].start()
    copies[1].start()
    total = partial_ref[...] + channel_terms(weights, other_ref, y ^ 1, core)
    held[...] = total.astype(held.dtype)
    copies[2].start()
    for copy in copies:
        copy.wait()


def fits(n_tm, n_agent, features):
    agents_here, rows_here, width = features.shape
    return (
        n_tm == 4
        and n_agent == 8
        and agents_here == 2
        and width == 4 * LANES
        and LANES % (width // HEADS) == 0
        and rows_here % LANES == 0
        and width % (16 * n_agent) == 0
        and n_tm * rows_here * width <= 2**20
    )


def split_heads(n_tm, n_agent, features, norm_gain, w_query, w_key, w_value, w_out, tracks):
    _, rows_here, width = features.shape
    head_dim = width // HEADS
    span = width // 2
    steps = n_tm * rows_here

    def across(value):
        return lax.ppermute(value, "tm", [(i, i ^ 2) for i in range(n_tm)])

    def swap(value):
        return lax.ppermute(value, "tm", [(i, i ^ 1) for i in range(n_tm)])

    def fetch(value, offsets):
        pairs = [
            (t * n_agent + (a ^ offsets[t % 2]), t * n_agent + a)
            for t in range(n_tm)
            for a in range(n_agent)
            if offsets[t % 2] is not None
        ]
        return lax.ppermute(value, ("tm", "agent"), pairs)

    vmem = pl.BlockSpec(memory_space=pltpu.VMEM)
    smem = pl.BlockSpec(memory_space=pltpu.SMEM)
    anywhere = pl.BlockSpec(memory_space=pl.ANY)

    def kernel(body, outs, args, scratch=(), specs=None, out_spec=vmem, aliases={}, **estimate):
        return pl.pallas_call(
            body,
            out_shape=[jax.ShapeDtypeStruct(shape, dtype) for shape, dtype in outs],
            in_specs=specs or [vmem] * len(args),
            out_specs=[out_spec] * len(outs),
            scratch_shapes=[pltpu.VMEM(*s) if isinstance(s, tuple) else s for s in scratch],
            input_output_aliases=aliases,
            compiler_params=params(),
            cost_estimate=cost(**estimate),
        )(*args)

    half, full = jnp.bfloat16, jnp.float32
    (packed,) = kernel(
        pack_kernel,
        [((width // n_agent, 4 * span), half)],
        tuple(
            pltpu.with_memory_space_constraint(w, pltpu.HBM)
            for w in (w_query, w_key, w_value, w_out)
        ),
        specs=[pl.BlockSpec(memory_space=pltpu.HBM)] * 4,
        scratch=[pltpu.SemaphoreType.DMA((4,))],
        flops=0,
    )
    projections, outward = packed[:, : 3 * span], packed[:, 3 * span :]
    sources = [(6, 4), (1, 3), (None, 2), (7, 5)]
    fetched = [fetch(packed if n else projections, pair) for n, pair in enumerate(sources[:3])]
    fetched.append(fetch(fetched[0], (1, 1)))
    out_far = fetch(outward, sources[0])
    out_shards = [out_far, *fetched[1:3], fetch(out_far, (1, 1))]
    other_rows = across(features)
    beside = swap(features)
    diagonal = swap(other_rows)
    swapped = [swap(value) for value in fetched]
    swapped_out = [swap(out_shards[0]), *swapped[1:3], swap(out_shards[3])]
    normed, bounds = kernel(
        norm_kernel,
        [((steps, width), half), ((2, 8, LANES), jnp.int32)],
        (tracks, norm_gain.reshape(1, width), features, beside, other_rows, diagonal),
        specs=[smem] + [vmem] * 5,
        flops=8 * steps * width,
    )
    shards = [packed] + [v for pair in zip(fetched, swapped) for v in pair]
    low = steps // 2
    high = steps - low
    exponentials = span // head_dim
    low_attended, weights, *low_held = kernel(
        functools.partial(low_kernel, sources, head_dim),
        [
            ((span, low), half),
            ((width, 3 * span), half),
            ((low, span), half),
            ((span, low), half),
        ],
        (bounds, normed, *shards),
        scratch=[((low, span), half)],
        flops=6 * low * width * span + 4 * low * low * span,
        transcendentals=low * low * exponentials,
    )
    low_other = across(low_attended)
    (high_attended,) = kernel(
        functools.partial(high_kernel, head_dim),
        [((span, high), half)],
        (bounds, normed, weights, *low_held),
        scratch=[((high, span), half), ((steps, span), half), ((span, steps), half)],
        flops=6 * high * width * span + 4 * high * steps * span,
        transcendentals=high * steps * exponentials,
    )
    high_other = across(high_attended)
    out_shards = [packed] + [v for pair in zip(out_shards, swapped_out) for v in pair]
    low_kept, low_given, out_weights = kernel(
        functools.partial(low_output_kernel, sources),
        [((span // 2, low), half)] * 2 + [((width, span), half)],
        (*out_shards, low_attended, low_other),
        flops=4 * low * span * span,
    )
    low_received = swap(low_given)
    kept, given = kernel(
        partial_kernel,
        [((span // 2, high), full)] * 2,
        (out_weights, high_attended),
        flops=2 * high * span * span,
    )
    (given,) = kernel(
        given_kernel,
        [((span // 2, high), half)],
        (out_weights, given, high_other),
        flops=high * span * span,
    )
    received = swap(given)
    (begun,) = kernel(
        kept_kernel,
        [((2, span // 2, steps), half)],
        (out_weights, kept, high_other, low_kept, low_received),
        scratch=[((span // 2, high), half), pltpu.SemaphoreType.DMA((3,))],
        out_spec=anywhere,
        flops=high * span * span,
    )
    out = lax.dynamic_update_slice(
        begun, received[None], (1 - lax.axis_index("tm") % 2, 0, low)
    )
    return out


def solution(mesh):
    in_specs = (
        P("agent", "tm", None),
        P(),
        P("agent", None),
        P("agent", None),
        P("agent", None),
        P("agent", None),
        P("agent", None),
    )
    out_specs = P("agent", "tm", None)
    n_tm, n_agent = mesh.shape["tm"], mesh.shape["agent"]

    def local(features, *rest):
        if fits(n_tm, n_agent, features):
            return split_heads(n_tm, n_agent, features, *rest)
        return body(features, *rest)

    return jax.shard_map(local, mesh=mesh, in_specs=in_specs, out_specs=out_specs, check_vma=False)
```

```python
import functools
import math

import jax
import jax.numpy as jnp
from jax import lax
from jax.experimental import pallas as pl
from jax.experimental.pallas import tpu as pltpu
from jax.sharding import PartitionSpec as P


HEADS = 8


EPSILON = 1e-05
NEGATIVE = -1e30
LANES = 128


def normalize(inputs, gain):
    values = inputs.astype(jnp.float32)
    meansq = jnp.mean(values * values, axis=-1, keepdims=True)
    return (values * lax.rsqrt(meansq + EPSILON) * gain).astype(jnp.bfloat16)


def project(normed, weight):
    return jnp.einsum("asd,de->ase", normed, weight, preferred_element_type=jnp.float32).astype(
        jnp.bfloat16
    )


def body(features, norm_gain, w_query, w_key, w_value, w_out, tracks):
    full_query, full_key, full_value, full_out = (
        lax.all_gather(w_query, "agent", axis=0, tiled=True),
        lax.all_gather(w_key, "agent", axis=0, tiled=True),
        lax.all_gather(w_value, "agent", axis=0, tiled=True),
        lax.all_gather(w_out, "agent", axis=0, tiled=True),
    )
    agents_here, rows_here, width = features.shape
    head_dim = width // HEADS
    scale = 1.0 / math.sqrt(head_dim)
    normed = normalize(features, norm_gain)
    starts = tracks[:, 0]
    ends = tracks[:, 1]
    queries = project(normed, full_query).reshape(agents_here, rows_here, HEADS, head_dim)
    first_row = lax.axis_index("tm") * rows_here
    query_pos = first_row + jnp.arange(rows_here, dtype=jnp.int32)
    row_live = (query_pos[None, :] >= starts[:, None]) & (query_pos[None, :] < ends[:, None])
    initial = (
        jnp.full((agents_here, HEADS, rows_here), NEGATIVE, jnp.float32),
        jnp.zeros((agents_here, HEADS, rows_here), jnp.float32),
        jnp.zeros((agents_here, HEADS, rows_here, head_dim), jnp.float32),
    )

    def attend(carry, key_block, value_block, key_start):
        highest, total, summed = carry
        count = key_block.shape[1]
        key_pos = key_start + jnp.arange(count, dtype=jnp.int32)
        scores = (
            jnp.einsum("athd,ashd->ahts", queries, key_block, preferred_element_type=jnp.float32)
            * scale
        )
        allowed = (
            (key_pos[None, None, :] >= starts[:, None, None])
            & (key_pos[None, None, :] <= query_pos[None, :, None])
            & row_live[:, :, None]
        )
        allowed = allowed[:, None]
        masked = jnp.where(allowed, scores, NEGATIVE)
        new_high = jnp.maximum(highest, jnp.max(masked, axis=-1))
        weights = jnp.where(allowed, jnp.exp(scores - new_high[..., None]), 0.0)
        factor = jnp.exp(highest - new_high)
        total = factor * total + jnp.sum(weights, axis=-1)
        summed = factor[..., None] * summed + jnp.einsum(
            "ahts,ashd->ahtd",
            weights.astype(jnp.bfloat16),
            value_block,
            preferred_element_type=jnp.float32,
        )
        return (new_high, total, summed)

    def sweep(carry, key_rows, value_rows, key_start):
        count = key_rows.shape[1]
        span = 512
        if span == count:
            return attend(carry, key_rows, value_rows, key_start)

        def advance(index, state):
            offset = (index * span).astype(jnp.int32)
            key_block = lax.dynamic_slice_in_dim(key_rows, offset, span, 1)
            value_block = lax.dynamic_slice_in_dim(value_rows, offset, span, 1)
            return attend(state, key_block, value_block, key_start + offset)

        return lax.fori_loop(0, count // span, advance, carry)

    piece = lax.all_gather(normed, "tm", axis=1, tiled=True)
    count = piece.shape[1]
    key_rows = project(piece, full_key).reshape(agents_here, count, HEADS, head_dim)
    value_rows = project(piece, full_value).reshape(agents_here, count, HEADS, head_dim)
    final = sweep(initial, key_rows, value_rows, jnp.int32(0))
    _, total, summed = final
    denom = jnp.where(row_live[:, None, :], total, 1.0)
    attended = summed / denom[..., None] * row_live[:, None, :, None].astype(jnp.float32)
    attended = (
        jnp.transpose(attended, (0, 2, 1, 3))
        .reshape(agents_here, rows_here, width)
        .astype(jnp.bfloat16)
    )
    projected = jnp.einsum(
        "asd,de->aes", attended, full_out, preferred_element_type=jnp.float32
    ).astype(jnp.bfloat16)
    return lax.all_to_all(projected, "tm", split_axis=1, concat_axis=2, tiled=True)


def params():
    return pltpu.CompilerParams(vmem_limit_bytes=24 * 2**20)


def cost(flops, transcendentals=0, bytes_accessed=2**20):
    return pl.CostEstimate(
        flops=flops, transcendentals=transcendentals, bytes_accessed=bytes_accessed
    )


def norm_kernel(tracks_ref, gain_ref, mine_ref, beside_ref, other_ref, diagonal_ref, *outs):
    normed_ref, bounds_ref = outs
    rows_here = mine_ref.shape[1]
    tm = lax.axis_index("tm")
    core = tm % 2
    gain = gain_ref[...]
    for k, ref in enumerate((mine_ref, beside_ref, other_ref, diagonal_ref)):
        rows = pl.ds(pl.multiple_of((tm ^ k) * rows_here, rows_here), rows_here)
        normed_ref[rows, :] = normalize(ref[core], gain)
    for n in range(2):
        bounds_ref[n] = jnp.full(bounds_ref.shape[1:], tracks_ref[core, n], jnp.int32)


def attend(bounds_ref, first, queries, keys, values, out_ref, head_dim):
    span, steps = out_ref.shape
    block = LANES
    heads = block // head_dim
    ratio = math.log2(math.e) / math.sqrt(head_dim)
    start, end = bounds_ref[0, :1, :block], bounds_ref[1, :1, :block]
    lane = lax.broadcasted_iota(jnp.int32, (block, block), 1)

    def score(t, group):
        query_block = queries[pl.ds(t, block), pl.ds(group, block)]
        one = [
            jnp.where((lane >= low) & (lane < low + head_dim), query_block, jnp.zeros_like(query_block))
            for low in range(0, block, head_dim)
        ]
        return lax.dot_general(
            keys[pl.ds(0, first + t + block), pl.ds(group, block)],
            jnp.concatenate(one, axis=0),
            (((1,), (1,)), ((), ())),
            preferred_element_type=jnp.float32,
        )

    def weigh(t, scores):
        reach = first + t + block
        key_pos = lax.broadcasted_iota(jnp.int32, (reach, block), 0)
        query_pos = first + t + lax.broadcasted_iota(jnp.int32, (reach, block), 1)
        allowed = (key_pos >= start) & (key_pos <= query_pos)
        scores = jnp.where(jnp.concatenate([allowed] * heads, axis=1), scores, NEGATIVE)
        highest = jnp.max(scores, axis=0, keepdims=True)
        weight = jnp.exp2((scores - highest) * ratio)
        return weight.astype(jnp.bfloat16), jnp.sum(weight, axis=0, keepdims=True)

    def finish(t, group, weight, total):
        summed = jnp.dot(
            values[pl.ds(group, block), pl.ds(0, first + t + block)],
            weight,
            preferred_element_type=jnp.float32,
        )
        column = first + t + lax.broadcasted_iota(jnp.int32, (1, block), 1)
        live = (column >= start) & (column < end)
        for h in range(heads):
            rows, lanes = slice(h * head_dim, (h + 1) * head_dim), slice(h * block, (h + 1) * block)
            result = jnp.where(live, summed[rows, lanes] / total[:, lanes], 0.0)
            out_ref[pl.ds(group + h * head_dim, head_dim), pl.ds(t, block)] = result.astype(
                jnp.bfloat16
            )

    tasks = [(t, group) for t in range(0, steps, block) for group in range(0, span, block)]
    scores, weights = {}, {}
    for n in range(len(tasks) + 2):
        if n < len(tasks):
            scores[n] = score(*tasks[n])
        if 0 <= n - 1 < len(tasks):
            weights[n - 1] = weigh(tasks[n - 1][0], scores.pop(n - 1))
        if n >= 2:
            finish(*tasks[n - 2], *weights.pop(n - 2))


def pack_kernel(*refs):
    sources, out_ref, sems = refs[:-2], refs[-2], refs[-1]
    span = out_ref.shape[1] // len(sources)
    first = pl.multiple_of(lax.axis_index("tm") // 2 * span, span)
    copies = [
        pltpu.make_async_copy(
            ref.at[:, pl.ds(first, span)], out_ref.at[:, pl.ds(n * span, span)], sems.at[n]
        )
        for n, ref in enumerate(sources)
    ]
    for copy in copies:
        copy.start()
    for copy in copies:
        copy.wait()


def place(sources, refs, target, begin):
    depth, columns = refs[0].shape[0], target.shape[1]
    agent = lax.axis_index("agent")
    core = lax.axis_index("tm") % 2

    def read(ref):
        low = min(begin, ref.shape[1] - columns)
        return ref[:, low : low + columns]

    def put(value, offset):
        rows = pl.ds(pl.multiple_of((agent ^ offset) * depth, depth), depth)
        target[rows, :] = value

    put(read(refs[0]), 0)
    for n, (first, second) in enumerate(sources):
        fetched, swapped = refs[1 + 2 * n : 3 + 2 * n]
        if first is None:
            put(jnp.where(core == 0, read(swapped), read(fetched)), second)
        else:
            put(read(fetched), jnp.where(core == 0, first, second))
            put(read(swapped), jnp.where(core == 0, second, first))


def project_rows(normed, weights, queries, keys, values):
    span = queries.shape[1]
    for n, target in enumerate((queries, keys, values)):
        full = jnp.dot(
            normed, weights[:, n * span : (n + 1) * span], preferred_element_type=jnp.float32
        )
        target[...] = (full.T if n == 2 else full).astype(jnp.bfloat16)


def low_kernel(sources, head_dim, bounds_ref, normed_ref, *refs):
    shards, refs = refs[: 1 + 2 * len(sources)], refs[1 + 2 * len(sources) :]
    out_ref, weights, keys, values, queries = refs
    place(sources, shards, weights, 0)
    steps = out_ref.shape[1]
    project_rows(normed_ref[:steps, :], weights, queries, keys, values)
    attend(bounds_ref, 0, queries, keys, values, out_ref, head_dim)


def high_kernel(head_dim, bounds_ref, normed_ref, weights, low_keys, low_values, *refs):
    out_ref, queries, keys, values = refs
    first = low_keys.shape[0]
    keys[:first, :] = low_keys[...]
    values[:, :first] = low_values[...]
    later = pl.ds(first, keys.shape[0] - first)
    project_rows(
        normed_ref[first:, :], weights, queries, keys.at[later, :], values.at[:, later]
    )
    attend(bounds_ref, first, queries, keys, values, out_ref, head_dim)


def channel_terms(weights, ref, chip, core):
    span = ref.shape[0]
    half = weights.shape[0] // 2
    rows = pl.ds(pl.multiple_of(core * half, half), half)
    lanes = pl.ds(pl.multiple_of(chip * span, span), span)
    return jnp.dot(weights[rows, lanes], ref[...], preferred_element_type=jnp.float32)


def low_output_kernel(sources, *refs):
    shards, refs = refs[: 1 + 2 * len(sources)], refs[1 + 2 * len(sources) :]
    mine_ref, other_ref, kept_ref, given_ref, weights, placed = refs
    core, y = lax.axis_index("tm") % 2, lax.axis_index("tm") // 2
    place(sources, shards, placed, 3 * placed.shape[1])
    weights[...] = placed[...].astype(jnp.float32).T.astype(weights.dtype)
    for n, ref in enumerate((kept_ref, given_ref)):
        total = channel_terms(weights, mine_ref, y, core ^ n)
        total = total + channel_terms(weights, other_ref, y ^ 1, core ^ n)
        ref[...] = total.astype(ref.dtype)


def partial_kernel(weights, mine_ref, kept_ref, given_ref):
    core, y = lax.axis_index("tm") % 2, lax.axis_index("tm") // 2
    for n, ref in enumerate((kept_ref, given_ref)):
        ref[...] = channel_terms(weights, mine_ref, y, core ^ n)


def given_kernel(weights, partial_ref, other_ref, out_ref):
    core, y = lax.axis_index("tm") % 2, lax.axis_index("tm") // 2
    total = partial_ref[...] + channel_terms(weights, other_ref, y ^ 1, core ^ 1)
    out_ref[...] = total.astype(out_ref.dtype)


def kept_kernel(weights, partial_ref, other_ref, low_ref, received_ref, out_ref, held, sems):
    core, y = lax.axis_index("tm") % 2, lax.axis_index("tm") // 2
    low, high = low_ref.shape[1], held.shape[1]
    copies = [
        pltpu.make_async_copy(low_ref, out_ref.at[core, :, pl.ds(0, low)], sems.at[0]),
        pltpu.make_async_copy(received_ref, out_ref.at[1 - core, :, pl.ds(0, low)], sems.at[1]),
        pltpu.make_async_copy(held, out_ref.at[core, :, pl.ds(low, high)], sems.at[2]),
    ]
    copies[0].start()
    copies[1].start()
    total = partial_ref[...] + channel_terms(weights, other_ref, y ^ 1, core)
    held[...] = total.astype(held.dtype)
    copies[2].start()
    for copy in copies:
        copy.wait()


def fits(n_tm, n_agent, features):
    agents_here, rows_here, width = features.shape
    return (
        n_tm == 4
        and n_agent == 8
        and agents_here == 2
        and width == 4 * LANES
        and LANES % (width // HEADS) == 0
        and rows_here % LANES == 0
        and width % (16 * n_agent) == 0
        and n_tm * rows_here * width <= 2**20
    )


def split_heads(n_tm, n_agent, features, norm_gain, w_query, w_key, w_value, w_out, tracks):
    _, rows_here, width = features.shape
    head_dim = width // HEADS
    span = width // 2
    steps = n_tm * rows_here

    def across(value):
        return lax.ppermute(value, "tm", [(i, i ^ 2) for i in range(n_tm)])

    def swap(value):
        return lax.ppermute(value, "tm", [(i, i ^ 1) for i in range(n_tm)])

    def fetch(value, offsets):
        pairs = [
            (t * n_agent + (a ^ offsets[t % 2]), t * n_agent + a)
            for t in range(n_tm)
            for a in range(n_agent)
            if offsets[t % 2] is not None
        ]
        return lax.ppermute(value, ("tm", "agent"), pairs)

    vmem = pl.BlockSpec(memory_space=pltpu.VMEM)
    smem = pl.BlockSpec(memory_space=pltpu.SMEM)
    anywhere = pl.BlockSpec(memory_space=pl.ANY)

    def kernel(body, outs, args, scratch=(), specs=None, out_spec=vmem, aliases={}, **estimate):
        return pl.pallas_call(
            body,
            out_shape=[jax.ShapeDtypeStruct(shape, dtype) for shape, dtype in outs],
            in_specs=specs or [vmem] * len(args),
            out_specs=[out_spec] * len(outs),
            scratch_shapes=[pltpu.VMEM(*s) if isinstance(s, tuple) else s for s in scratch],
            input_output_aliases=aliases,
            compiler_params=params(),
            cost_estimate=cost(**estimate),
        )(*args)

    half, full = jnp.bfloat16, jnp.float32
    (packed,) = kernel(
        pack_kernel,
        [((width // n_agent, 4 * span), half)],
        tuple(
            pltpu.with_memory_space_constraint(w, pltpu.HBM)
            for w in (w_query, w_key, w_value, w_out)
        ),
        specs=[pl.BlockSpec(memory_space=pltpu.HBM)] * 4,
        scratch=[pltpu.SemaphoreType.DMA((4,))],
        flops=0,
    )
    projections, outward = packed[:, : 3 * span], packed[:, 3 * span :]
    sources = [(6, 4), (1, 3), (None, 2), (7, 5)]
    fetched = [fetch(packed if n else projections, pair) for n, pair in enumerate(sources[:3])]
    fetched.append(fetch(fetched[0], (1, 1)))
    out_far = fetch(outward, sources[0])
    out_shards = [out_far, *fetched[1:3], fetch(out_far, (1, 1))]
    other_rows = across(features)
    beside = swap(features)
    diagonal = swap(other_rows)
    swapped = [swap(value) for value in fetched]
    swapped_out = [swap(out_shards[0]), *swapped[1:3], swap(out_shards[3])]
    normed, bounds = kernel(
        norm_kernel,
        [((steps, width), half), ((2, 8, LANES), jnp.int32)],
        (tracks, norm_gain.reshape(1, width), features, beside, other_rows, diagonal),
        specs=[smem] + [vmem] * 5,
        flops=8 * steps * width,
    )
    shards = [packed] + [v for pair in zip(fetched, swapped) for v in pair]
    low = steps // 2
    high = steps - low
    exponentials = span // head_dim
    low_attended, weights, *low_held = kernel(
        functools.partial(low_kernel, sources, head_dim),
        [
            ((span, low), half),
            ((width, 3 * span), half),
            ((low, span), half),
            ((span, low), half),
        ],
        (bounds, normed, *shards),
        scratch=[((low, span), half)],
        flops=6 * low * width * span + 4 * low * low * span,
        transcendentals=low * low * exponentials,
    )
    low_other = across(low_attended)
    (high_attended,) = kernel(
        functools.partial(high_kernel, head_dim),
        [((span, high), half)],
        (bounds, normed, weights, *low_held),
        scratch=[((high, span), half), ((steps, span), half), ((span, steps), half)],
        flops=6 * high * width * span + 4 * high * steps * span,
        transcendentals=high * steps * exponentials,
    )
    high_other = across(high_attended)
    out_shards = [packed] + [v for pair in zip(out_shards, swapped_out) for v in pair]
    low_kept, low_given, out_weights = kernel(
        functools.partial(low_output_kernel, sources),
        [((span // 2, low), half)] * 2 + [((span, width), half)],
        (*out_shards, low_attended, low_other),
        scratch=[((width, span), half)],
        flops=4 * low * span * span,
    )
    low_received = swap(low_given)
    kept, given = kernel(
        partial_kernel,
        [((span // 2, high), full)] * 2,
        (out_weights, high_attended),
        flops=2 * high * span * span,
    )
    (given,) = kernel(
        given_kernel,
        [((span // 2, high), half)],
        (out_weights, given, high_other),
        flops=high * span * span,
    )
    received = swap(given)
    (begun,) = kernel(
        kept_kernel,
        [((2, span // 2, steps), half)],
        (out_weights, kept, high_other, low_kept, low_received),
        scratch=[((span // 2, high), half), pltpu.SemaphoreType.DMA((3,))],
        out_spec=anywhere,
        flops=high * span * span,
    )
    out = lax.dynamic_update_slice(
        begun, received[None], (1 - lax.axis_index("tm") % 2, 0, low)
    )
    return out


def solution(mesh):
    in_specs = (
        P("agent", "tm", None),
        P(),
        P("agent", None),
        P("agent", None),
        P("agent", None),
        P("agent", None),
        P("agent", None),
    )
    out_specs = P("agent", "tm", None)
    n_tm, n_agent = mesh.shape["tm"], mesh.shape["agent"]

    def local(features, *rest):
        if fits(n_tm, n_agent, features):
            return split_heads(n_tm, n_agent, features, *rest)
        return body(features, *rest)

    return jax.shard_map(local, mesh=mesh, in_specs=in_specs, out_specs=out_specs, check_vma=False)
```

```python
import functools
import math

import jax
import jax.numpy as jnp
from jax import lax
from jax.experimental import pallas as pl
from jax.experimental.pallas import tpu as pltpu
from jax.sharding import PartitionSpec as P


HEADS = 8


EPSILON = 1e-05
NEGATIVE = -1e30
LANES = 128


def normalize(inputs, gain):
    values = inputs.astype(jnp.float32)
    meansq = jnp.mean(values * values, axis=-1, keepdims=True)
    return (values * lax.rsqrt(meansq + EPSILON) * gain).astype(jnp.bfloat16)


def project(normed, weight):
    return jnp.einsum("asd,de->ase", normed, weight, preferred_element_type=jnp.float32).astype(
        jnp.bfloat16
    )


def body(features, norm_gain, w_query, w_key, w_value, w_out, tracks):
    full_query, full_key, full_value, full_out = (
        lax.all_gather(w_query, "agent", axis=0, tiled=True),
        lax.all_gather(w_key, "agent", axis=0, tiled=True),
        lax.all_gather(w_value, "agent", axis=0, tiled=True),
        lax.all_gather(w_out, "agent", axis=0, tiled=True),
    )
    agents_here, rows_here, width = features.shape
    head_dim = width // HEADS
    scale = 1.0 / math.sqrt(head_dim)
    normed = normalize(features, norm_gain)
    starts = tracks[:, 0]
    ends = tracks[:, 1]
    queries = project(normed, full_query).reshape(agents_here, rows_here, HEADS, head_dim)
    first_row = lax.axis_index("tm") * rows_here
    query_pos = first_row + jnp.arange(rows_here, dtype=jnp.int32)
    row_live = (query_pos[None, :] >= starts[:, None]) & (query_pos[None, :] < ends[:, None])
    initial = (
        jnp.full((agents_here, HEADS, rows_here), NEGATIVE, jnp.float32),
        jnp.zeros((agents_here, HEADS, rows_here), jnp.float32),
        jnp.zeros((agents_here, HEADS, rows_here, head_dim), jnp.float32),
    )

    def attend(carry, key_block, value_block, key_start):
        highest, total, summed = carry
        count = key_block.shape[1]
        key_pos = key_start + jnp.arange(count, dtype=jnp.int32)
        scores = (
            jnp.einsum("athd,ashd->ahts", queries, key_block, preferred_element_type=jnp.float32)
            * scale
        )
        allowed = (
            (key_pos[None, None, :] >= starts[:, None, None])
            & (key_pos[None, None, :] <= query_pos[None, :, None])
            & row_live[:, :, None]
        )
        allowed = allowed[:, None]
        masked = jnp.where(allowed, scores, NEGATIVE)
        new_high = jnp.maximum(highest, jnp.max(masked, axis=-1))
        weights = jnp.where(allowed, jnp.exp(scores - new_high[..., None]), 0.0)
        factor = jnp.exp(highest - new_high)
        total = factor * total + jnp.sum(weights, axis=-1)
        summed = factor[..., None] * summed + jnp.einsum(
            "ahts,ashd->ahtd",
            weights.astype(jnp.bfloat16),
            value_block,
            preferred_element_type=jnp.float32,
        )
        return (new_high, total, summed)

    def sweep(carry, key_rows, value_rows, key_start):
        count = key_rows.shape[1]
        span = 512
        if span == count:
            return attend(carry, key_rows, value_rows, key_start)

        def advance(index, state):
            offset = (index * span).astype(jnp.int32)
            key_block = lax.dynamic_slice_in_dim(key_rows, offset, span, 1)
            value_block = lax.dynamic_slice_in_dim(value_rows, offset, span, 1)
            return attend(state, key_block, value_block, key_start + offset)

        return lax.fori_loop(0, count // span, advance, carry)

    piece = lax.all_gather(normed, "tm", axis=1, tiled=True)
    count = piece.shape[1]
    key_rows = project(piece, full_key).reshape(agents_here, count, HEADS, head_dim)
    value_rows = project(piece, full_value).reshape(agents_here, count, HEADS, head_dim)
    final = sweep(initial, key_rows, value_rows, jnp.int32(0))
    _, total, summed = final
    denom = jnp.where(row_live[:, None, :], total, 1.0)
    attended = summed / denom[..., None] * row_live[:, None, :, None].astype(jnp.float32)
    attended = (
        jnp.transpose(attended, (0, 2, 1, 3))
        .reshape(agents_here, rows_here, width)
        .astype(jnp.bfloat16)
    )
    projected = jnp.einsum(
        "asd,de->aes", attended, full_out, preferred_element_type=jnp.float32
    ).astype(jnp.bfloat16)
    return lax.all_to_all(projected, "tm", split_axis=1, concat_axis=2, tiled=True)


def params():
    return pltpu.CompilerParams(vmem_limit_bytes=24 * 2**20)


def cost(flops, transcendentals=0, bytes_accessed=2**20):
    return pl.CostEstimate(
        flops=flops, transcendentals=transcendentals, bytes_accessed=bytes_accessed
    )


def norm_kernel(tracks_ref, gain_ref, mine_ref, beside_ref, other_ref, diagonal_ref, *outs):
    normed_ref, bounds_ref = outs
    rows_here = mine_ref.shape[1]
    tm = lax.axis_index("tm")
    core = tm % 2
    gain = gain_ref[...]
    for k, ref in enumerate((mine_ref, beside_ref, other_ref, diagonal_ref)):
        rows = pl.ds(pl.multiple_of((tm ^ k) * rows_here, rows_here), rows_here)
        normed_ref[rows, :] = normalize(ref[core], gain)
    for n in range(2):
        bounds_ref[n] = jnp.full(bounds_ref.shape[1:], tracks_ref[core, n], jnp.int32)


def attend(bounds_ref, first, queries, keys, values, out_ref, head_dim):
    span, steps = out_ref.shape
    block = LANES
    heads = block // head_dim
    ratio = math.log2(math.e) / math.sqrt(head_dim)
    start, end = bounds_ref[0, :1, :block], bounds_ref[1, :1, :block]
    lane = lax.broadcasted_iota(jnp.int32, (block, block), 1)

    def score(t, group):
        query_block = queries[pl.ds(t, block), pl.ds(group, block)]
        one = [
            jnp.where((lane >= low) & (lane < low + head_dim), query_block, jnp.zeros_like(query_block))
            for low in range(0, block, head_dim)
        ]
        return lax.dot_general(
            keys[pl.ds(0, first + t + block), pl.ds(group, block)],
            jnp.concatenate(one, axis=0),
            (((1,), (1,)), ((), ())),
            preferred_element_type=jnp.float32,
        )

    def weigh(t, scores):
        reach = first + t + block
        key_pos = lax.broadcasted_iota(jnp.int32, (reach, block), 0)
        query_pos = first + t + lax.broadcasted_iota(jnp.int32, (reach, block), 1)
        allowed = (key_pos >= start) & (key_pos <= query_pos)
        scores = jnp.where(jnp.concatenate([allowed] * heads, axis=1), scores, NEGATIVE)
        highest = jnp.max(scores, axis=0, keepdims=True)
        weight = jnp.exp2((scores - highest) * ratio)
        return weight.astype(jnp.bfloat16), jnp.sum(weight, axis=0, keepdims=True)

    def finish(t, group, weight, total):
        summed = jnp.dot(
            values[pl.ds(group, block), pl.ds(0, first + t + block)],
            weight,
            preferred_element_type=jnp.float32,
        )
        column = first + t + lax.broadcasted_iota(jnp.int32, (1, block), 1)
        live = (column >= start) & (column < end)
        for h in range(heads):
            rows, lanes = slice(h * head_dim, (h + 1) * head_dim), slice(h * block, (h + 1) * block)
            result = jnp.where(live, summed[rows, lanes] / total[:, lanes], 0.0)
            out_ref[pl.ds(group + h * head_dim, head_dim), pl.ds(t, block)] = result.astype(
                jnp.bfloat16
            )

    tasks = [(t, group) for t in range(0, steps, block) for group in range(0, span, block)]
    scores, weights = {}, {}
    for n in range(len(tasks) + 2):
        if n < len(tasks):
            scores[n] = score(*tasks[n])
        if 0 <= n - 1 < len(tasks):
            weights[n - 1] = weigh(tasks[n - 1][0], scores.pop(n - 1))
        if n >= 2:
            finish(*tasks[n - 2], *weights.pop(n - 2))


def pack_kernel(*refs):
    sources, out_ref, sems = refs[:-2], refs[-2], refs[-1]
    span = out_ref.shape[1] // len(sources)
    first = pl.multiple_of(lax.axis_index("tm") // 2 * span, span)
    copies = [
        pltpu.make_async_copy(
            ref.at[:, pl.ds(first, span)], out_ref.at[:, pl.ds(n * span, span)], sems.at[n]
        )
        for n, ref in enumerate(sources)
    ]
    for copy in copies:
        copy.start()
    for copy in copies:
        copy.wait()


def place(sources, refs, target, begin):
    depth, columns = refs[0].shape[0], target.shape[1]
    agent = lax.axis_index("agent")
    core = lax.axis_index("tm") % 2

    def read(ref):
        low = min(begin, ref.shape[1] - columns)
        return ref[:, low : low + columns]

    def put(value, offset):
        rows = pl.ds(pl.multiple_of((agent ^ offset) * depth, depth), depth)
        target[rows, :] = value

    put(read(refs[0]), 0)
    for n, (first, second) in enumerate(sources):
        fetched, swapped = refs[1 + 2 * n : 3 + 2 * n]
        if first is None:
            put(jnp.where(core == 0, read(swapped), read(fetched)), second)
        else:
            put(read(fetched), jnp.where(core == 0, first, second))
            put(read(swapped), jnp.where(core == 0, second, first))


def project_rows(normed, weights, queries, keys, values):
    span = queries.shape[1]
    for n, target in enumerate((queries, keys, values)):
        full = jnp.dot(
            normed, weights[:, n * span : (n + 1) * span], preferred_element_type=jnp.float32
        )
        rounded = full.astype(jnp.bfloat16)
        target[...] = rounded.T if n == 2 else rounded


def low_kernel(sources, head_dim, bounds_ref, normed_ref, *refs):
    shards, refs = refs[: 1 + 2 * len(sources)], refs[1 + 2 * len(sources) :]
    out_ref, weights, keys, values, queries = refs
    place(sources, shards, weights, 0)
    steps = out_ref.shape[1]
    project_rows(normed_ref[:steps, :], weights, queries, keys, values)
    attend(bounds_ref, 0, queries, keys, values, out_ref, head_dim)


def high_kernel(head_dim, bounds_ref, normed_ref, weights, low_keys, low_values, *refs):
    out_ref, queries, keys, values = refs
    first = low_keys.shape[0]
    keys[:first, :] = low_keys[...]
    values[:, :first] = low_values[...]
    later = pl.ds(first, keys.shape[0] - first)
    project_rows(
        normed_ref[first:, :], weights, queries, keys.at[later, :], values.at[:, later]
    )
    attend(bounds_ref, first, queries, keys, values, out_ref, head_dim)


def channel_terms(weights, ref, chip, core):
    span = ref.shape[0]
    half = weights.shape[0] // 2
    rows = pl.ds(pl.multiple_of(core * half, half), half)
    lanes = pl.ds(pl.multiple_of(chip * span, span), span)
    return jnp.dot(weights[rows, lanes], ref[...], preferred_element_type=jnp.float32)


def low_output_kernel(sources, *refs):
    shards, refs = refs[: 1 + 2 * len(sources)], refs[1 + 2 * len(sources) :]
    mine_ref, other_ref, kept_ref, given_ref, weights, placed = refs
    core, y = lax.axis_index("tm") % 2, lax.axis_index("tm") // 2
    place(sources, shards, placed, 3 * placed.shape[1])
    weights[...] = placed[...].T
    for n, ref in enumerate((kept_ref, given_ref)):
        total = channel_terms(weights, mine_ref, y, core ^ n)
        total = total + channel_terms(weights, other_ref, y ^ 1, core ^ n)
        ref[...] = total.astype(ref.dtype)


def partial_kernel(weights, mine_ref, kept_ref, given_ref):
    core, y = lax.axis_index("tm") % 2, lax.axis_index("tm") // 2
    for n, ref in enumerate((kept_ref, given_ref)):
        ref[...] = channel_terms(weights, mine_ref, y, core ^ n)


def given_kernel(weights, partial_ref, other_ref, out_ref):
    core, y = lax.axis_index("tm") % 2, lax.axis_index("tm") // 2
    total = partial_ref[...] + channel_terms(weights, other_ref, y ^ 1, core ^ 1)
    out_ref[...] = total.astype(out_ref.dtype)


def kept_kernel(weights, partial_ref, other_ref, low_ref, received_ref, out_ref, held, sems):
    core, y = lax.axis_index("tm") % 2, lax.axis_index("tm") // 2
    low, high = low_ref.shape[1], held.shape[1]
    copies = [
        pltpu.make_async_copy(low_ref, out_ref.at[core, :, pl.ds(0, low)], sems.at[0]),
        pltpu.make_async_copy(received_ref, out_ref.at[1 - core, :, pl.ds(0, low)], sems.at[1]),
        pltpu.make_async_copy(held, out_ref.at[core, :, pl.ds(low, high)], sems.at[2]),
    ]
    copies[0].start()
    copies[1].start()
    total = partial_ref[...] + channel_terms(weights, other_ref, y ^ 1, core)
    held[...] = total.astype(held.dtype)
    copies[2].start()
    for copy in copies:
        copy.wait()


def fits(n_tm, n_agent, features):
    agents_here, rows_here, width = features.shape
    return (
        n_tm == 4
        and n_agent == 8
        and agents_here == 2
        and width == 4 * LANES
        and LANES % (width // HEADS) == 0
        and rows_here % LANES == 0
        and width % (16 * n_agent) == 0
        and n_tm * rows_here * width <= 2**20
    )


def split_heads(n_tm, n_agent, features, norm_gain, w_query, w_key, w_value, w_out, tracks):
    _, rows_here, width = features.shape
    head_dim = width // HEADS
    span = width // 2
    steps = n_tm * rows_here

    def across(value):
        return lax.ppermute(value, "tm", [(i, i ^ 2) for i in range(n_tm)])

    def swap(value):
        return lax.ppermute(value, "tm", [(i, i ^ 1) for i in range(n_tm)])

    def fetch(value, offsets):
        pairs = [
            (t * n_agent + (a ^ offsets[t % 2]), t * n_agent + a)
            for t in range(n_tm)
            for a in range(n_agent)
            if offsets[t % 2] is not None
        ]
        return lax.ppermute(value, ("tm", "agent"), pairs)

    vmem = pl.BlockSpec(memory_space=pltpu.VMEM)
    smem = pl.BlockSpec(memory_space=pltpu.SMEM)
    anywhere = pl.BlockSpec(memory_space=pl.ANY)

    def kernel(body, outs, args, scratch=(), specs=None, out_spec=vmem, aliases={}, **estimate):
        return pl.pallas_call(
            body,
            out_shape=[jax.ShapeDtypeStruct(shape, dtype) for shape, dtype in outs],
            in_specs=specs or [vmem] * len(args),
            out_specs=[out_spec] * len(outs),
            scratch_shapes=[pltpu.VMEM(*s) if isinstance(s, tuple) else s for s in scratch],
            input_output_aliases=aliases,
            compiler_params=params(),
            cost_estimate=cost(**estimate),
        )(*args)

    half, full = jnp.bfloat16, jnp.float32
    (packed,) = kernel(
        pack_kernel,
        [((width // n_agent, 4 * span), half)],
        tuple(
            pltpu.with_memory_space_constraint(w, pltpu.HBM)
            for w in (w_query, w_key, w_value, w_out)
        ),
        specs=[pl.BlockSpec(memory_space=pltpu.HBM)] * 4,
        scratch=[pltpu.SemaphoreType.DMA((4,))],
        flops=0,
    )
    projections, outward = packed[:, : 3 * span], packed[:, 3 * span :]
    sources = [(6, 4), (1, 3), (None, 2), (7, 5)]
    fetched = [fetch(packed if n else projections, pair) for n, pair in enumerate(sources[:3])]
    fetched.append(fetch(fetched[0], (1, 1)))
    out_far = fetch(outward, sources[0])
    out_shards = [out_far, *fetched[1:3], fetch(out_far, (1, 1))]
    other_rows = across(features)
    beside = swap(features)
    diagonal = swap(other_rows)
    swapped = [swap(value) for value in fetched]
    swapped_out = [swap(out_shards[0]), *swapped[1:3], swap(out_shards[3])]
    normed, bounds = kernel(
        norm_kernel,
        [((steps, width), half), ((2, 8, LANES), jnp.int32)],
        (tracks, norm_gain.reshape(1, width), features, beside, other_rows, diagonal),
        specs=[smem] + [vmem] * 5,
        flops=8 * steps * width,
    )
    shards = [packed] + [v for pair in zip(fetched, swapped) for v in pair]
    low = steps // 2
    high = steps - low
    exponentials = span // head_dim
    low_attended, weights, *low_held = kernel(
        functools.partial(low_kernel, sources, head_dim),
        [
            ((span, low), half),
            ((width, 3 * span), half),
            ((low, span), half),
            ((span, low), half),
        ],
        (bounds, normed, *shards),
        scratch=[((low, span), half)],
        flops=6 * low * width * span + 4 * low * low * span,
        transcendentals=low * low * exponentials,
    )
    low_other = across(low_attended)
    (high_attended,) = kernel(
        functools.partial(high_kernel, head_dim),
        [((span, high), half)],
        (bounds, normed, weights, *low_held),
        scratch=[((high, span), half), ((steps, span), half), ((span, steps), half)],
        flops=6 * high * width * span + 4 * high * steps * span,
        transcendentals=high * steps * exponentials,
    )
    high_other = across(high_attended)
    out_shards = [packed] + [v for pair in zip(out_shards, swapped_out) for v in pair]
    low_kept, low_given, out_weights = kernel(
        functools.partial(low_output_kernel, sources),
        [((span // 2, low), half)] * 2 + [((span, width), half)],
        (*out_shards, low_attended, low_other),
        scratch=[((width, span), half)],
        flops=4 * low * span * span,
    )
    low_received = swap(low_given)
    kept, given = kernel(
        partial_kernel,
        [((span // 2, high), full)] * 2,
        (out_weights, high_attended),
        flops=2 * high * span * span,
    )
    (given,) = kernel(
        given_kernel,
        [((span // 2, high), half)],
        (out_weights, given, high_other),
        flops=high * span * span,
    )
    received = swap(given)
    (begun,) = kernel(
        kept_kernel,
        [((2, span // 2, steps), half)],
        (out_weights, kept, high_other, low_kept, low_received),
        scratch=[((span // 2, high), half), pltpu.SemaphoreType.DMA((3,))],
        out_spec=anywhere,
        flops=high * span * span,
    )
    out = lax.dynamic_update_slice(
        begun, received[None], (1 - lax.axis_index("tm") % 2, 0, low)
    )
    return out


def solution(mesh):
    in_specs = (
        P("agent", "tm", None),
        P(),
        P("agent", None),
        P("agent", None),
        P("agent", None),
        P("agent", None),
        P("agent", None),
    )
    out_specs = P("agent", "tm", None)
    n_tm, n_agent = mesh.shape["tm"], mesh.shape["agent"]

    def local(features, *rest):
        if fits(n_tm, n_agent, features):
            return split_heads(n_tm, n_agent, features, *rest)
        return body(features, *rest)

    return jax.shard_map(local, mesh=mesh, in_specs=in_specs, out_specs=out_specs, check_vma=False)
```
